32 devices in a mesh: lat: 8 (over z, y), lay: 4 (over x, core).
Axes of the slice: x: 2, y: 2, z: 4, core: 2. Of those that a mesh axis runs over, the one named last changes fastest.
Arguments:
- wave_field: float32 [2, 32, 512, 512], P(None, 'lay', 'lat'), may hold values from -6 to 6
- contrast: float32 [32, 512, 512], P('lay', 'lat'), may hold values from 0.1 to 1.5
- layer_of_plane: int32 [32], replicated, may hold values from 0 to 7, never falling along the last dimension, each value on 1 to 8 neighbouring positions
- toeplitz_table: float32 [2, 8, 63], replicated, may hold values from -1 to 1
- hankel_table: float32 [2, 8, 63], replicated, may hold values from -1 to 1
- layer_rates: float32 [8], replicated, may hold values from 0.5 to 1.5
Outputs:
- scattered_field: float32 [2, 32, 512, 512], P(None, 'lay', 'lat')
The draws below stay inside these ranges and needn't reach their ends.
Inputs may be any that keep to these rules, and one draw needn't show every extreme that they name: `layer_of_plane`: layer numbers never fall from one plane to the next; every layer holds 1 to 8 planes.
All inputs are finite; a program needn't handle non-finite values.
Results may differ from the reference program's by a relative error of at most 0.00007.
Values sent between devices are 32-bit elements; how exact they have to be, the bound alone decides.
A program may use at most 128 MiB of HBM per device.

```python
import math
import jax
import jax.numpy as jnp
import numpy as np
from jax import lax

NX = 512
NY = 512
LAYERS = 8
NZ = 32


def steps_of(key, shape, cuts, least, largest):
    factor_of, own = 1.0, jax.random.fold_in(key, 6)
    for position, parts in cuts:
        steps = jnp.exp(jax.random.uniform(jax.random.fold_in(own, position), (parts,), jnp.float32, least / len(cuts), largest / len(cuts)))
        factor_of = factor_of * jnp.repeat(steps, shape[position] // parts).reshape([-1 if axis == position else 1 for axis in range(len(shape))])
    return factor_of


def profile(count, total, reach, skew):
    portions = [(1 << 20) // math.isqrt(rank ** skew) + 1 for rank in range(2, count + 1)]
    surplus, given = total - reach - (count - 1), [1] * (count - 1)
    while surplus > 0:
        movable = [i for i in range(count - 1) if given[i] < reach]
        mass, left = sum([portions[i] for i in movable]), surplus
        for i in movable:
            extra = min(reach - given[i], max(1, left * portions[i] // mass), surplus)
            given[i] = given[i] + extra
            surplus = surplus - extra
    return np.array([reach] + given)


def uneven_parts(own_key, number_of, total, most, slope):
    if number_of == 2:
        one = jax.random.randint(own_key, (), max(1, total - most), min(most, total - 1) + 1)
        return jnp.stack([one, total - one])
    lengths = jnp.asarray(profile(number_of, total, most, slope), jnp.int32)
    twos = (number_of - 1) // 2
    giver, taker = lengths[1:1 + 2 * twos:2], lengths[2:2 + 2 * twos:2]
    margin = jnp.minimum(giver - 1, most - taker)
    shifted = jax.random.randint(jax.random.fold_in(own_key, 1), (twos,), 0, 1 << 20) % (margin + 1)
    lengths = lengths.at[1:1 + 2 * twos:2].set(giver - shifted).at[2:2 + 2 * twos:2].set(taker + shifted)
    return lengths[jax.random.permutation(jax.random.fold_in(own_key, 2), number_of)]


def noise(key, shape, scale, reach, pieces=(), dtype=jnp.bfloat16):
    factor_of = steps_of(key, shape, pieces, -0.22, 0.18) if pieces else 1.0
    array = jax.random.normal(key, shape, jnp.float32) * scale * factor_of
    return jnp.minimum(jnp.maximum(array, -reach), reach).astype(dtype)


def setup_inputs(seed: int = 0) -> dict:
    key_list = jax.random.split(jax.random.key(seed), 7)
    wave_field = noise(key_list[0], (2, NZ, NX, NY), 1.0, 6.0, ((1, 4), (2, 8)), jnp.float32)
    contrast = jnp.clip(0.1 + 1.4 * jax.random.uniform(key_list[1], (NZ, NX, NY), jnp.float32) ** steps_of(key_list[1], (NZ, NX, NY), ((0, 4), (1, 8)), -0.2, 0.2), 0.1, 1.5)
    layer_of_plane = jnp.searchsorted(jnp.cumsum(uneven_parts(key_list[2], LAYERS, NZ, 2 * NZ // LAYERS, 2)), jnp.arange(NZ), side="right").astype(jnp.int32)
    toeplitz_table = noise(key_list[3], (2, LAYERS, 2 * NZ - 1), NZ ** -0.5, 1.0, (), jnp.float32)
    hankel_table = noise(key_list[4], (2, LAYERS, 2 * NZ - 1), NZ ** -0.5, 1.0, (), jnp.float32)
    layer_rates = jnp.clip(jnp.exp(jax.random.uniform(key_list[5], (LAYERS,), jnp.float32, math.log(0.5), math.log(1.5))), 0.5, 1.5)
    return {"wave_field": wave_field, "contrast": contrast, "layer_of_plane": layer_of_plane, "toeplitz_table": toeplitz_table, "hankel_table": hankel_table, "layer_rates": layer_rates}


def signed_freq(amount):
    index = jnp.arange(amount).astype(jnp.int32)
    return jnp.where(index >= amount // 2, index - amount, index).astype(jnp.float32) / (amount / 2)

def reference(wave_field, contrast, layer_of_plane, toeplitz_table, hankel_table, layer_rates):
    complex_field = wave_field[0] + 1j * wave_field[1]
    spectrum = jnp.fft.fft2(complex_field, axes=(1, 2))
    freq_x = signed_freq(NX)
    freq_y = signed_freq(NY)
    steepness = jnp.sqrt(1.0 + freq_x[:, None] ** 2 + freq_y[None, :] ** 2)
    planes = jnp.arange(NZ).astype(jnp.int32)
    toeplitz_c = toeplitz_table[0] + 1j * toeplitz_table[1]
    hankel_c = hankel_table[0] + 1j * hankel_table[1]

    def one_plane(plane):
        layer_here = layer_of_plane[plane]
        rate_here = layer_rates[layer_here]
        offset = plane - planes
        amp_toeplitz = toeplitz_c[layer_here, offset + NZ - 1]
        amp_hankel = hankel_c[layer_here, plane + planes]
        decay_toeplitz = jnp.exp(-rate_here * steepness[None] * jnp.abs(offset).astype(jnp.float32)[:, None, None] / NZ)
        decay_hankel = jnp.exp(-rate_here * steepness[None] * (plane + planes).astype(jnp.float32)[:, None, None] / (2 * NZ))
        kernel = amp_toeplitz[:, None, None] * decay_toeplitz + amp_hankel[:, None, None] * decay_hankel
        return lax.optimization_barrier(jnp.sum(kernel * spectrum, axis=0))
    mixed = lax.map(one_plane, planes)
    space = jnp.fft.ifft2(mixed, axes=(1, 2))
    return jnp.stack([jnp.real(space) * contrast, jnp.imag(space) * contrast]).astype(jnp.float32)
```

```python
import math

import functools

import jax
import jax.numpy as jnp
import numpy as np
from jax import lax
from jax.experimental import pallas as pl
from jax.experimental.pallas import tpu as pltpu
from jax.sharding import PartitionSpec as P

HIGHEST = lax.Precision.HIGHEST


def signed_of(index, amount):
    return jnp.where(index >= amount // 2, index - amount, index).astype(jnp.float32) / (amount / 2)


def phase_tables(rows, cols, amount, sign):
    index_row = lax.broadcasted_iota(jnp.int32, (rows, cols), 0)
    index_col = lax.broadcasted_iota(jnp.int32, (rows, cols), 1)
    angle = 2.0 * math.pi / amount * (index_row * index_col % amount).astype(jnp.float32)
    return (jnp.cos(angle), sign * jnp.sin(angle))


def complex_apply(real_part, imag_part, cos_table, sin_table, form):
    out_real = jnp.einsum(form, real_part, cos_table, precision=HIGHEST) - jnp.einsum(
        form, imag_part, sin_table, precision=HIGHEST
    )
    out_imag = jnp.einsum(form, real_part, sin_table, precision=HIGHEST) + jnp.einsum(
        form, imag_part, cos_table, precision=HIGHEST
    )
    return (out_real, out_imag)


def fourier_last(real_part, imag_part, sign, factor):
    amount = real_part.shape[-1]
    leading = real_part.shape[:-1]
    first = 1
    for divisor in range(1, math.isqrt(amount) + 1):
        if amount % divisor == 0:
            first = divisor
    second = amount // first
    flat_real = real_part.reshape(-1, second, first)
    flat_imag = imag_part.reshape(-1, second, first)
    cos_second, sin_second = phase_tables(second, second, second, sign)
    section_real, section_imag = complex_apply(
        flat_real, flat_imag, cos_second, sin_second, "pmn,mk->pkn"
    )
    twist_cos, twist_sin = phase_tables(second, first, amount, sign)
    turned_real = section_real * twist_cos - section_imag * twist_sin
    turned_imag = section_real * twist_sin + section_imag * twist_cos
    cos_first, sin_first = phase_tables(first, first, first, sign)
    final_real, final_imag = complex_apply(
        turned_real, turned_imag, cos_first, sin_first, "pkn,nj->pjk"
    )
    final_real = final_real.reshape(leading + (amount,)) * factor
    final_imag = final_imag.reshape(leading + (amount,)) * factor
    return (final_real, final_imag)


def pick_amplitudes(rows, index, width):
    positions = jnp.arange(width, dtype=jnp.int32)
    onehot = (index[:, :, None] == positions[None, None, :]).astype(jnp.float32)
    return jnp.einsum("pan,ain->pai", rows, onehot, precision=HIGHEST)


def general_body(wave_field, contrast, layer_of_plane, toeplitz_table, hankel_table, layer_rates):
    row_count = wave_field.shape[2]
    width_y = wave_field.shape[3]
    lat_count = lax.axis_size("lat")
    lay_count = lax.axis_size("lay")
    width_x = row_count * lat_count
    ky_band = width_y // lat_count
    table_width = toeplitz_table.shape[-1]
    plane_total = (table_width + 1) // 2
    layer_count = layer_rates.shape[0]
    spec_real, spec_imag = fourier_last(wave_field[0], wave_field[1], -1.0, 1.0)
    along_y = jnp.stack([spec_real, spec_imag], 2)
    freq_x = signed_of(jnp.arange(width_x, dtype=jnp.int32), width_x)
    ky_first = lax.axis_index("lat") * ky_band
    layer_ids = jnp.arange(layer_count, dtype=jnp.int32)

    def couple(z_out, z_in, source, ky_rows):
        onehot = (layer_of_plane[z_out][:, None] == layer_ids[None, :]).astype(jnp.float32)
        rate_out = jnp.dot(onehot, layer_rates, precision=HIGHEST)
        rows_toeplitz = jnp.einsum("al,pln->pan", onehot, toeplitz_table, precision=HIGHEST)
        rows_hankel = jnp.einsum("al,pln->pan", onehot, hankel_table, precision=HIGHEST)
        offset = z_out[:, None] - z_in[None, :]
        plane_sum = z_out[:, None] + z_in[None, :]
        amp_toeplitz = pick_amplitudes(rows_toeplitz, offset + plane_total - 1, table_width)
        amp_hankel = pick_amplitudes(rows_hankel, plane_sum, table_width)
        freq_y = signed_of(ky_rows, width_y)
        steepness = jnp.sqrt(1.0 + freq_y[:, None] ** 2 + freq_x[None, :] ** 2)
        scaled = rate_out[:, None, None, None] * steepness[None, None] / plane_total
        decay_toeplitz = jnp.exp(-scaled * jnp.abs(offset).astype(jnp.float32)[:, :, None, None])
        decay_hankel = jnp.exp(-scaled * (0.5 * plane_sum.astype(jnp.float32))[:, :, None, None])
        kern_real = (
            amp_toeplitz[0][:, :, None, None] * decay_toeplitz
            + amp_hankel[0][:, :, None, None] * decay_hankel
        )
        kern_imag = (
            amp_toeplitz[1][:, :, None, None] * decay_toeplitz
            + amp_hankel[1][:, :, None, None] * decay_hankel
        )
        real_src = source[None, :, 0]
        imag_src = source[None, :, 1]
        out_real = jnp.sum(kern_real * real_src - kern_imag * imag_src, axis=1)
        out_imag = jnp.sum(kern_real * imag_src + kern_imag * real_src, axis=1)
        return jnp.stack([out_real, out_imag], 1)

    narrow = ky_band // lay_count
    narrow_rows = ky_first + lax.axis_index("lay") * narrow + jnp.arange(narrow, dtype=jnp.int32)
    lines_in = lax.all_to_all(along_y, "lat", split_axis=3, concat_axis=1, tiled=True)
    line_real = jnp.transpose(lines_in[:, :, 0], (0, 2, 1))
    line_imag = jnp.transpose(lines_in[:, :, 1], (0, 2, 1))
    out_real, out_imag = fourier_last(line_real, line_imag, -1.0, 1.0)
    spectrum = jnp.stack([out_real, out_imag], 1)
    gathered = lax.all_to_all(spectrum, "lay", split_axis=2, concat_axis=0, tiled=True)
    all_planes = gathered.shape[0]
    every_plane = jnp.arange(all_planes, dtype=jnp.int32)
    block_size = math.gcd(all_planes, 8)

    def one_block(which):
        z_out = which * block_size + jnp.arange(block_size, dtype=jnp.int32)
        return couple(z_out, every_plane, gathered, narrow_rows)

    stacked = lax.map(one_block, jnp.arange(all_planes // block_size, dtype=jnp.int32))
    coupled = stacked.reshape(all_planes, 2, narrow_rows.shape[0], width_x)
    mixed = lax.all_to_all(coupled, "lay", split_axis=0, concat_axis=2, tiled=True)
    out_real, out_imag = fourier_last(mixed[:, 0], mixed[:, 1], 1.0, 1.0 / width_x)
    spatial_x = jnp.transpose(jnp.stack([out_real, out_imag], 1), (0, 3, 1, 2))
    lines = lax.all_to_all(spatial_x, "lat", split_axis=1, concat_axis=3, tiled=True)
    space_real, space_imag = fourier_last(lines[:, :, 0], lines[:, :, 1], 1.0, 1.0 / width_y)
    return jnp.stack([space_real, space_imag], 0) * contrast[None]


LANES = 128
SUBLANES = 8
MESH = pl.DeviceIdType.MESH


def split_pair(table):
    table = table.astype(np.float32)
    high = table.astype(jnp.bfloat16)
    return high, (table - high.astype(np.float32)).astype(jnp.bfloat16)


def split_tables(amount):
    half = amount // 2
    index = np.arange(half)
    angle = 2.0 * np.pi / half * (index[:, None] * index[None, :] % half)
    cos_part, sin_part = np.cos(angle), np.sin(angle)
    right = np.block([[cos_part, -sin_part], [sin_part, cos_part]])
    high, low = split_pair(right)
    turn = 2.0 * np.pi / amount * index
    twiddle = np.stack([np.cos(turn), np.sin(turn)]).astype(np.float32)
    return high, low, np.ascontiguousarray(high.T), np.ascontiguousarray(low.T), twiddle


def class_tables(amount, classes):
    length = amount // classes
    index = np.arange(length)
    every = []
    for which in range(classes):
        turns = (which + classes * index[:, None]) * index[None, :] % amount
        angle = 2.0 * np.pi / amount * turns
        cos_part, sin_part = np.cos(angle), np.sin(angle)
        forward = np.block([[cos_part, sin_part], [-sin_part, cos_part]])
        every.append(np.stack([*split_pair(forward), *split_pair(forward.T)]))
    return np.stack(every).reshape(2, classes // 2, 4, 2 * length, 2 * length)


def split(value):
    high = value.astype(jnp.bfloat16)
    return high, (value - high.astype(jnp.float32)).astype(jnp.bfloat16)


def product(left, right, contract):
    dot = functools.partial(
        lax.dot_general,
        dimension_numbers=(contract, ((), ())),
        preferred_element_type=jnp.float32,
    )
    return dot(left[0], right[0]) + (dot(left[1], right[0]) + dot(left[0], right[1]))


def swap_halves(first, second):
    low = lax.broadcasted_iota(jnp.int32, first.shape, first.ndim - 1) < LANES // 2
    one = jnp.where(low, first, pltpu.roll(second, LANES // 2, first.ndim - 1))
    two = jnp.where(low, pltpu.roll(first, LANES // 2, first.ndim - 1), second)
    return one, two


def butterfly_in(real_part, imag_part, twiddle):
    half = real_part.shape[-1] // 2
    cos_row, sin_row = twiddle[0:1, :], twiddle[1:2, :]
    even = (real_part[:, :half] + real_part[:, half:], imag_part[:, :half] + imag_part[:, half:])
    real_gap = real_part[:, :half] - real_part[:, half:]
    imag_gap = imag_part[:, :half] - imag_part[:, half:]
    odd = (
        real_gap * cos_row + imag_gap * sin_row,
        imag_gap * cos_row - real_gap * sin_row,
    )
    return even, odd


def butterfly_out(even, odd, twiddle):
    cos_row, sin_row = twiddle[0:1, :], twiddle[1:2, :]
    real_turn = odd[0] * cos_row - odd[1] * sin_row
    imag_turn = odd[0] * sin_row + odd[1] * cos_row
    real_part = jnp.concatenate([even[0] + real_turn, even[0] - real_turn], 1)
    imag_part = jnp.concatenate([even[1] + imag_turn, even[1] - imag_turn], 1)
    return real_part, imag_part


ROOT_HALF = math.sqrt(0.5)


def turn_eighths(pair, which, sign):
    if which == 0:
        return pair
    low = lax.broadcasted_iota(jnp.int32, pair.shape, pair.ndim - 1) < LANES // 2
    other = pltpu.roll(pair, LANES // 2, pair.ndim - 1)
    crossed = jnp.where(low, other, -other) if sign < 0 else jnp.where(low, -other, other)
    if which == 2:
        return crossed
    return ROOT_HALF * (crossed + pair) if which == 1 else ROOT_HALF * (crossed - pair)


def fold_classes(real_parts, imag_parts):
    def plus(first, second):
        return tuple(parts[first] + parts[second] for parts in (real_parts, imag_parts))

    def minus(first, second):
        return tuple(parts[first] - parts[second] for parts in (real_parts, imag_parts))

    sum_even, sum_odd, gap_even, gap_odd = plus(0, 2), plus(1, 3), minus(0, 2), minus(1, 3)
    fours = [
        (sum_even[0] + sum_odd[0], sum_even[1] + sum_odd[1]),
        (gap_even[0] + gap_odd[1], gap_even[1] - gap_odd[0]),
        (sum_even[0] - sum_odd[0], sum_even[1] - sum_odd[1]),
        (gap_even[0] - gap_odd[1], gap_even[1] + gap_odd[0]),
    ]
    sides = []
    for which, (real_part, imag_part) in enumerate(fours):
        near, far = swap_halves(real_part, imag_part)
        far = turn_eighths(far, which, -1)
        sides.append((near + far, near - far))
    return sides


def unfold_classes(sides):
    fours = []
    for which, (first, second) in enumerate(sides):
        near, far = first + second, turn_eighths(first - second, which, 1)
        fours.append(swap_halves(near, far))
    sum_even = [fours[0][i] + fours[2][i] for i in range(2)]
    gap_even = [fours[0][i] - fours[2][i] for i in range(2)]
    sum_odd = [fours[1][i] + fours[3][i] for i in range(2)]
    gap_odd = [fours[1][i] - fours[3][i] for i in range(2)]
    return [
        (sum_even[0] + sum_odd[0], sum_even[1] + sum_odd[1]),
        (gap_even[0] - gap_odd[1], gap_even[1] + gap_odd[0]),
        (sum_even[0] - sum_odd[0], sum_even[1] - sum_odd[1]),
        (gap_even[0] + gap_odd[1], gap_even[1] - gap_odd[0]),
    ]


ORDER = (3, 2, 1)


def couple_kernel(
    lat_count, lay_count, planes, rows,
    layer_ref, rate_ref, toeplitz_ref, hankel_ref,
    field_any, fh_any, fl_any, ih_any, il_any, tables_any, twiddle_ref,
    out_ref,
    send_fold, recv_fold, send_in, recv_in, send_out, recv_mid, send_fin, recv_fin,
    field_x, spectrum, mixed, powers,
    field_ref, fh_ref, fl_ref, ih_ref, il_ref, tables_ref,
    fold_send, fold_recv, in_send, in_recv, out_send, out_recv, fin_send, fin_recv, load_sem,
):
    inner = 2
    outer = lat_count // inner
    peers = inner * lay_count
    my_lat, my_lay = lax.axis_index("lat"), lax.axis_index("lay")
    my_outer = my_lat // inner
    my_peer = my_lat % inner * lay_count + my_lay
    lines, width_y = field_ref.shape[1:]
    width_x = rows * lat_count
    half_x = width_x // 2
    classes = 2 * outer
    length = width_y // classes
    depth = length // peers
    plane_total = planes * lay_count
    layer_count = rate_ref.shape[0]
    pairs = planes // 2

    def column(way):
        low = (my_outer % 2 + way % 2) % 2
        high = (my_outer // 2 + way // 2) % 2
        return 2 * high + low

    def column_id(way):
        return column(way) * inner + my_lat % inner, my_lay

    def peer(step):
        return (my_peer + step) % peers

    def peer_id(step):
        to = peer(step)
        return my_outer * inner + to // lay_count, to % lay_count

    def over_peers(act):
        def one(step, carry):
            act(step)
            return carry

        lax.fori_loop(1, peers, one, 0)

    chunk = LANES
    chunks = lines // chunk
    loads = [
        pltpu.make_async_copy(
            field_any.at[:, pl.ds(i * chunk, chunk)],
            field_ref.at[:, pl.ds(i * chunk, chunk)],
            load_sem.at[i],
        )
        for i in range(chunks)
    ] + [
        pltpu.make_async_copy(source, target, load_sem.at[chunks + i])
        for i, (source, target) in enumerate(
            [
                (tables_any.at[0, my_outer], tables_ref.at[0]),
                (tables_any.at[1, my_outer], tables_ref.at[1]),
                (fh_any, fh_ref), (fl_any, fl_ref), (ih_any, ih_ref), (il_any, il_ref),
            ]
        )
    ]
    for load in loads:
        load.start()

    barrier = pltpu.get_barrier_semaphore()
    for way in range(1, outer):
        pl.semaphore_signal(barrier, inc=1, device_id=column_id(way), device_id_type=MESH)
    over_peers(
        lambda step: pl.semaphore_signal(
            barrier, inc=1, device_id=peer_id(step), device_id_type=MESH
        )
    )

    def remote(source, target, sems, index, device):
        return pltpu.make_async_remote_copy(
            src_ref=source,
            dst_ref=target,
            send_sem=sems[0].at[index],
            recv_sem=sems[1].at[index],
            device_id=device,
            device_id_type=MESH,
        )

    def fold_copy(side, way):
        return remote(
            send_fold.at[column(way), side], recv_fold.at[my_outer, side],
            (fold_send, fold_recv), (side, way), column_id(way),
        )

    def in_copy(origin, side, step):
        return remote(
            send_in.at[peer(step), origin, side], recv_in.at[origin, my_peer, side],
            (in_send, in_recv), (origin, side, step), peer_id(step),
        )

    def out_copy(side, pair, step):
        return remote(
            send_out.at[peer(step), side, pair], recv_mid.at[my_peer, side, pair],
            (out_send, out_recv), (side, pair, step), peer_id(step),
        )

    def fin_copy(side, pair, way):
        return remote(
            send_fin.at[column(way), side, pair], recv_fin.at[my_outer, side, pair],
            (fin_send, fin_recv), (side, pair, way), column_id(way),
        )

    for i in range(chunks):
        where = slice(i * chunk, (i + 1) * chunk)
        loads[i].wait()
        parts = [
            [field_ref[comp, where, t * LANES:(t + 1) * LANES] for t in range(outer)]
            for comp in range(2)
        ]
        for which, both in enumerate(fold_classes(*parts)):
            for side in range(2):
                send_fold[which, side, where] = both[side]

    pl.semaphore_wait(barrier, outer - 1 + peers - 1)
    for side in range(2):
        for way in ORDER:
            fold_copy(side, way).start()

    loads[chunks].wait()
    loads[chunks + 1].wait()

    def transform_y(source, origin, side):
        for start in range(0, lines, 2 * LANES):
            where = slice(start, start + 2 * LANES)
            right = split(source[origin, side, where])
            result = product((tables_ref[side, 0], tables_ref[side, 1]), right, ((1,), (1,)))
            for comp in range(2):
                piece = result[comp * length:(comp + 1) * length]
                send_in[:, origin, side, comp, :, where] = piece.reshape(peers, depth, 2 * LANES)
        over_peers(lambda step: in_copy(origin, side, step).start())
        recv_in[origin, my_peer, side] = send_in[my_peer, origin, side]

    for side in range(2):
        transform_y(send_fold, my_outer, side)

    def signed(index, amount):
        index = jnp.where(index >= amount // 2, index - amount, index)
        return index.astype(jnp.float32) / (amount / 2)

    tile = (depth, width_x)
    place_x = lax.broadcasted_iota(jnp.int32, tile, 1)
    freq_x = signed(2 * (place_x % half_x) + place_x // half_x, width_x)
    for side in range(2):
        place_y = my_peer * depth + lax.broadcasted_iota(jnp.int32, tile, 0)
        freq_y = signed(classes * place_y + my_outer + outer * side, width_y)
        steepness = jnp.sqrt(1.0 + freq_x * freq_x + freq_y * freq_y)

        def one_layer(layer, carry):
            base = jnp.exp(steepness * (-rate_ref[layer] / (2 * plane_total)))

            def one_power(m, value):
                powers[side, layer, m] = value
                return value * base

            lax.fori_loop(0, 2 * plane_total - 1, one_power, jnp.ones(tile, jnp.float32))
            return carry

        lax.fori_loop(0, layer_count, one_layer, 0)

    for i in range(chunks + 2, chunks + 6):
        loads[i].wait()

    def gather(side, way):
        fold_copy(side, way).wait_recv()
        transform_y(recv_fold, column(way), side)

    for way in ORDER:
        gather(0, way)

    def load_lines(side):
        def one_lay(lay, carry):
            for pair in range(pairs):
                lanes = slice(pair * LANES, (pair + 1) * LANES)
                for block in range(outer):
                    first = recv_in[block, lay, side, :, :, lanes]
                    second = recv_in[block, lay_count + lay, side, :, :, lanes]
                    even, odd = swap_halves(first, second)
                    place = slice(block * LANES, (block + 1) * LANES)
                    field_x[:, lay * planes + 2 * pair, :, place] = even
                    field_x[:, lay * planes + 2 * pair + 1, :, place] = odd
            return carry

        lax.fori_loop(0, lay_count, one_lay, 0)

    group = min(plane_total, LANES // SUBLANES)

    def transform_x(step, carry):
        some = pl.ds(step * group, group)
        flat = (group * depth, width_x)
        halves = butterfly_in(
            field_x[0, some].reshape(flat), field_x[1, some].reshape(flat), twiddle_ref
        )
        for half, pair in enumerate(halves):
            left = split(jnp.concatenate(pair, 1))
            result = product(left, (fh_ref[...], fl_ref[...]), ((1,), (0,)))
            for comp in range(2):
                piece = result[:, comp * half_x:(comp + 1) * half_x]
                spectrum[comp, some, :, half * half_x:(half + 1) * half_x] = piece.reshape(
                    group, depth, half_x
                )
        return carry

    some_planes = 2 * lay_count

    def invert_x():
        halves = []
        for half in range(2):
            place = slice(half * half_x, (half + 1) * half_x)
            flat = (some_planes * depth, half_x)
            left = split(
                jnp.concatenate(
                    [mixed[comp, :, :, place].reshape(flat) for comp in range(2)], 1
                )
            )
            result = product(left, (ih_ref[...], il_ref[...]), ((1,), (0,)))
            halves.append((result[:, :half_x], result[:, half_x:]))
        real_part, imag_part = butterfly_out(halves[0], halves[1], twiddle_ref)
        full = (some_planes, depth, width_x)
        factor = 1.0 / (width_x * width_y)
        mixed[0] = (real_part * factor).reshape(full)
        mixed[1] = (imag_part * factor).reshape(full)

    def store_lines(side, pair):
        for lay in range(lay_count):
            for block in range(outer):
                place = slice(block * LANES, (block + 1) * LANES)
                even, odd = mixed[:, 2 * lay, :, place], mixed[:, 2 * lay + 1, :, place]
                first, second = swap_halves(even, odd)
                send_out[lay, side, pair, :, :, place] = first
                send_out[lay_count + lay, side, pair, :, :, place] = second

    def couple(side, pair):
        def one_plane(place, carry):
            plane = place // 2 * planes + 2 * pair + place % 2
            layer = layer_ref[plane]
            real_sum = jnp.zeros(tile, jnp.float32)
            imag_sum = jnp.zeros(tile, jnp.float32)
            for source in range(plane_total):
                offset = plane - source
                direct = powers[side, layer, 2 * jnp.abs(offset)]
                mirror = powers[side, layer, plane + source]
                at = offset + plane_total - 1
                kern_real = (
                    toeplitz_ref[0, layer, at] * direct
                    + hankel_ref[0, layer, plane + source] * mirror
                )
                kern_imag = (
                    toeplitz_ref[1, layer, at] * direct
                    + hankel_ref[1, layer, plane + source] * mirror
                )
                real_src, imag_src = spectrum[0, source], spectrum[1, source]
                real_sum += kern_real * real_src - kern_imag * imag_src
                imag_sum += kern_real * imag_src + kern_imag * real_src
            mixed[0, place] = real_sum
            mixed[1, place] = imag_sum
            return carry

        lax.fori_loop(0, some_planes, one_plane, 0)

    def invert_y(side, pair):
        over_peers(lambda step: out_copy(side, pair, step).wait_recv())
        stack = jnp.concatenate(
            [recv_mid[:, side, pair, comp].reshape(length, outer * LANES) for comp in range(2)], 0
        )
        result = product((tables_ref[side, 2], tables_ref[side, 3]), split(stack), ((1,), (0,)))
        for block in range(outer):
            send_fin[block, side, pair] = result[:, block * LANES:(block + 1) * LANES].T
        for way in ORDER:
            fin_copy(side, pair, way).start()
        recv_fin[my_outer, side, pair] = send_fin[my_outer, side, pair]

    for side in range(2):
        for origin in range(outer):
            over_peers(lambda step: in_copy(origin, side, step).wait_recv())
        load_lines(side)
        lax.fori_loop(0, plane_total // group, transform_x, 0)

        def one_pair(pair, carry):
            couple(side, pair)
            invert_x()
            store_lines(side, pair)
            over_peers(lambda step: out_copy(side, pair, step).start())
            recv_mid[my_peer, side, pair] = send_out[my_peer, side, pair]

            @pl.when(pair >= 1)
            def _():
                invert_y(side, pair - 1)

            if side == 0:

                @pl.when(pair == pairs - 2)
                def _():
                    gather(1, ORDER[0])

                @pl.when(pair == pairs - 1)
                def _():
                    gather(1, ORDER[1])

            return carry

        lax.fori_loop(0, pairs, one_pair, 0)
        invert_y(side, pairs - 1)
        if side == 0:
            gather(1, ORDER[2])

    for side in range(2):
        for way in ORDER:
            fold_copy(side, way).wait_send()
        for origin in range(outer):
            over_peers(lambda step: in_copy(origin, side, step).wait_send())

        def sent(pair, carry):
            over_peers(lambda step: out_copy(side, pair, step).wait_send())
            return carry

        lax.fori_loop(0, pairs, sent, 0)

    def finish(pair, carry):
        for side in range(2):
            for way in ORDER:
                fin_copy(side, pair, way).wait_recv()
        where = pl.ds(pair * LANES, LANES)
        sides = [(recv_fin[which, 0, pair], recv_fin[which, 1, pair]) for which in range(outer)]
        for t, (real_part, imag_part) in enumerate(unfold_classes(sides)):
            out_ref[0, where, t * LANES:(t + 1) * LANES] = real_part
            out_ref[1, where, t * LANES:(t + 1) * LANES] = imag_part
        return carry

    lax.fori_loop(0, pairs, finish, 0)

    def drain(pair, carry):
        for side in range(2):
            for way in ORDER:
                fin_copy(side, pair, way).wait_send()
        return carry

    lax.fori_loop(0, pairs, drain, 0)


def fast_body(wave_field, contrast, layer_of_plane, toeplitz_table, hankel_table, layer_rates):
    _, planes, rows, width_y = wave_field.shape
    lat_count, lay_count = lax.axis_size("lat"), lax.axis_size("lay")
    outer, peers = lat_count // 2, 2 * lay_count
    width_x = rows * lat_count
    depth = width_y // (2 * outer * peers)
    plane_total = planes * lay_count
    layer_count = layer_rates.shape[0]
    lines = planes * rows
    pairs = planes // 2
    fh, fl, ih, il, twiddle = (jnp.asarray(t) for t in split_tables(width_x))
    tables = jnp.asarray(class_tables(width_y, 2 * outer))
    smem = pl.BlockSpec(memory_space=pltpu.SMEM)
    vmem = pl.BlockSpec(memory_space=pltpu.VMEM)
    far = pl.BlockSpec(memory_space=pltpu.HBM)
    folded = (outer, 2, lines, LANES)
    final = (outer, 2, pairs, LANES, LANES)
    tile_all = (2, plane_total, depth, width_x)
    dma = pltpu.SemaphoreType.DMA
    space = pl.pallas_call(
        functools.partial(couple_kernel, lat_count, lay_count, planes, rows),
        out_shape=jax.ShapeDtypeStruct((2, lines, width_y), jnp.float32),
        in_specs=[smem] * 4 + [far] * 6 + [vmem],
        out_specs=vmem,
        scratch_shapes=[
            pltpu.VMEM(folded, jnp.float32),
            pltpu.VMEM(folded, jnp.float32),
            pltpu.VMEM((peers, outer, 2, 2, depth, lines), jnp.float32),
            pltpu.VMEM((outer, peers, 2, 2, depth, lines), jnp.float32),
            pltpu.VMEM((peers, 2, pairs, 2, depth, outer * LANES), jnp.float32),
            pltpu.VMEM((peers, 2, pairs, 2, depth, outer * LANES), jnp.float32),
            pltpu.VMEM(final, jnp.float32),
            pltpu.VMEM(final, jnp.float32),
            pltpu.VMEM(tile_all, jnp.float32),
            pltpu.VMEM(tile_all, jnp.float32),
            pltpu.VMEM((2, 2 * lay_count, depth, width_x), jnp.float32),
            pltpu.VMEM((2, layer_count, 2 * plane_total - 1, depth, width_x), jnp.float32),
            pltpu.VMEM((2, lines, width_y), jnp.float32),
            pltpu.VMEM(fh.shape, fh.dtype),
            pltpu.VMEM(fl.shape, fl.dtype),
            pltpu.VMEM(ih.shape, ih.dtype),
            pltpu.VMEM(il.shape, il.dtype),
            pltpu.VMEM((2,) + tables.shape[2:], tables.dtype),
            dma((2, outer)), dma((2, outer)),
            dma((outer, 2, peers)), dma((outer, 2, peers)),
            dma((2, pairs, peers)), dma((2, pairs, peers)),
            dma((2, pairs, outer)), dma((2, pairs, outer)),
            dma((lines // LANES + 6,)),
        ],
        compiler_params=pltpu.CompilerParams(
            collective_id=0, has_side_effects=True, vmem_limit_bytes=48 * 1024 * 1024
        ),
        name="couple",
    )(
        layer_of_plane, layer_rates, toeplitz_table, hankel_table,
        wave_field.reshape(2, lines, width_y), fh, fl, ih, il, tables, twiddle,
    )
    return space.reshape(wave_field.shape) * contrast[None]


def body(wave_field, *others):
    _, planes, rows, width_y = wave_field.shape
    lat_count, lay_count = lax.axis_size("lat"), lax.axis_size("lay")
    outer, peers = lat_count // 2, 2 * lay_count
    width_x = rows * lat_count
    fits = (
        lat_count % 2 == 0
        and outer == 4
        and 2 * rows == LANES
        and planes % 2 == 0
        and planes >= 4
        and width_x == width_y
        and width_y == outer * LANES
        and width_y == 2 * outer * peers * SUBLANES
        and (planes * lay_count) % (LANES // SUBLANES) == 0
        and (planes * rows) % (2 * LANES) == 0
    )
    return (fast_body if fits else general_body)(wave_field, *others)


def solution(mesh):
    return jax.shard_map(
        body,
        mesh=mesh,
        in_specs=(P(None, "lay", "lat", None), P("lay", "lat", None), P(), P(), P(), P()),
        out_specs=P(None, "lay", "lat", None),
        check_vma=False,
    )
```

```python
import math

import functools

import jax
import jax.numpy as jnp
import numpy as np
from jax import lax
from jax.experimental import pallas as pl
from jax.experimental.pallas import tpu as pltpu
from jax.sharding import PartitionSpec as P

HIGHEST = lax.Precision.HIGHEST


def signed_of(index, amount):
    return jnp.where(index >= amount // 2, index - amount, index).astype(jnp.float32) / (amount / 2)


def phase_tables(rows, cols, amount, sign):
    index_row = lax.broadcasted_iota(jnp.int32, (rows, cols), 0)
    index_col = lax.broadcasted_iota(jnp.int32, (rows, cols), 1)
    angle = 2.0 * math.pi / amount * (index_row * index_col % amount).astype(jnp.float32)
    return (jnp.cos(angle), sign * jnp.sin(angle))


def complex_apply(real_part, imag_part, cos_table, sin_table, form):
    out_real = jnp.einsum(form, real_part, cos_table, precision=HIGHEST) - jnp.einsum(
        form, imag_part, sin_table, precision=HIGHEST
    )
    out_imag = jnp.einsum(form, real_part, sin_table, precision=HIGHEST) + jnp.einsum(
        form, imag_part, cos_table, precision=HIGHEST
    )
    return (out_real, out_imag)


def fourier_last(real_part, imag_part, sign, factor):
    amount = real_part.shape[-1]
    leading = real_part.shape[:-1]
    first = 1
    for divisor in range(1, math.isqrt(amount) + 1):
        if amount % divisor == 0:
            first = divisor
    second = amount // first
    flat_real = real_part.reshape(-1, second, first)
    flat_imag = imag_part.reshape(-1, second, first)
    cos_second, sin_second = phase_tables(second, second, second, sign)
    section_real, section_imag = complex_apply(
        flat_real, flat_imag, cos_second, sin_second, "pmn,mk->pkn"
    )
    twist_cos, twist_sin = phase_tables(second, first, amount, sign)
    turned_real = section_real * twist_cos - section_imag * twist_sin
    turned_imag = section_real * twist_sin + section_imag * twist_cos
    cos_first, sin_first = phase_tables(first, first, first, sign)
    final_real, final_imag = complex_apply(
        turned_real, turned_imag, cos_first, sin_first, "pkn,nj->pjk"
    )
    final_real = final_real.reshape(leading + (amount,)) * factor
    final_imag = final_imag.reshape(leading + (amount,)) * factor
    return (final_real, final_imag)


def pick_amplitudes(rows, index, width):
    positions = jnp.arange(width, dtype=jnp.int32)
    onehot = (index[:, :, None] == positions[None, None, :]).astype(jnp.float32)
    return jnp.einsum("pan,ain->pai", rows, onehot, precision=HIGHEST)


def general_body(wave_field, contrast, layer_of_plane, toeplitz_table, hankel_table, layer_rates):
    row_count = wave_field.shape[2]
    width_y = wave_field.shape[3]
    lat_count = lax.axis_size("lat")
    lay_count = lax.axis_size("lay")
    width_x = row_count * lat_count
    ky_band = width_y // lat_count
    table_width = toeplitz_table.shape[-1]
    plane_total = (table_width + 1) // 2
    layer_count = layer_rates.shape[0]
    spec_real, spec_imag = fourier_last(wave_field[0], wave_field[1], -1.0, 1.0)
    along_y = jnp.stack([spec_real, spec_imag], 2)
    freq_x = signed_of(jnp.arange(width_x, dtype=jnp.int32), width_x)
    ky_first = lax.axis_index("lat") * ky_band
    layer_ids = jnp.arange(layer_count, dtype=jnp.int32)

    def couple(z_out, z_in, source, ky_rows):
        onehot = (layer_of_plane[z_out][:, None] == layer_ids[None, :]).astype(jnp.float32)
        rate_out = jnp.dot(onehot, layer_rates, precision=HIGHEST)
        rows_toeplitz = jnp.einsum("al,pln->pan", onehot, toeplitz_table, precision=HIGHEST)
        rows_hankel = jnp.einsum("al,pln->pan", onehot, hankel_table, precision=HIGHEST)
        offset = z_out[:, None] - z_in[None, :]
        plane_sum = z_out[:, None] + z_in[None, :]
        amp_toeplitz = pick_amplitudes(rows_toeplitz, offset + plane_total - 1, table_width)
        amp_hankel = pick_amplitudes(rows_hankel, plane_sum, table_width)
        freq_y = signed_of(ky_rows, width_y)
        steepness = jnp.sqrt(1.0 + freq_y[:, None] ** 2 + freq_x[None, :] ** 2)
        scaled = rate_out[:, None, None, None] * steepness[None, None] / plane_total
        decay_toeplitz = jnp.exp(-scaled * jnp.abs(offset).astype(jnp.float32)[:, :, None, None])
        decay_hankel = jnp.exp(-scaled * (0.5 * plane_sum.astype(jnp.float32))[:, :, None, None])
        kern_real = (
            amp_toeplitz[0][:, :, None, None] * decay_toeplitz
            + amp_hankel[0][:, :, None, None] * decay_hankel
        )
        kern_imag = (
            amp_toeplitz[1][:, :, None, None] * decay_toeplitz
            + amp_hankel[1][:, :, None, None] * decay_hankel
        )
        real_src = source[None, :, 0]
        imag_src = source[None, :, 1]
        out_real = jnp.sum(kern_real * real_src - kern_imag * imag_src, axis=1)
        out_imag = jnp.sum(kern_real * imag_src + kern_imag * real_src, axis=1)
        return jnp.stack([out_real, out_imag], 1)

    narrow = ky_band // lay_count
    narrow_rows = ky_first + lax.axis_index("lay") * narrow + jnp.arange(narrow, dtype=jnp.int32)
    lines_in = lax.all_to_all(along_y, "lat", split_axis=3, concat_axis=1, tiled=True)
    line_real = jnp.transpose(lines_in[:, :, 0], (0, 2, 1))
    line_imag = jnp.transpose(lines_in[:, :, 1], (0, 2, 1))
    out_real, out_imag = fourier_last(line_real, line_imag, -1.0, 1.0)
    spectrum = jnp.stack([out_real, out_imag], 1)
    gathered = lax.all_to_all(spectrum, "lay", split_axis=2, concat_axis=0, tiled=True)
    all_planes = gathered.shape[0]
    every_plane = jnp.arange(all_planes, dtype=jnp.int32)
    block_size = math.gcd(all_planes, 8)

    def one_block(which):
        z_out = which * block_size + jnp.arange(block_size, dtype=jnp.int32)
        return couple(z_out, every_plane, gathered, narrow_rows)

    stacked = lax.map(one_block, jnp.arange(all_planes // block_size, dtype=jnp.int32))
    coupled = stacked.reshape(all_planes, 2, narrow_rows.shape[0], width_x)
    mixed = lax.all_to_all(coupled, "lay", split_axis=0, concat_axis=2, tiled=True)
    out_real, out_imag = fourier_last(mixed[:, 0], mixed[:, 1], 1.0, 1.0 / width_x)
    spatial_x = jnp.transpose(jnp.stack([out_real, out_imag], 1), (0, 3, 1, 2))
    lines = lax.all_to_all(spatial_x, "lat", split_axis=1, concat_axis=3, tiled=True)
    space_real, space_imag = fourier_last(lines[:, :, 0], lines[:, :, 1], 1.0, 1.0 / width_y)
    return jnp.stack([space_real, space_imag], 0) * contrast[None]


LANES = 128
SUBLANES = 8
MESH = pl.DeviceIdType.MESH


def split_pair(table):
    table = table.astype(np.float32)
    high = table.astype(jnp.bfloat16)
    return high, (table - high.astype(np.float32)).astype(jnp.bfloat16)


def split_tables(amount):
    half = amount // 2
    index = np.arange(half)
    angle = 2.0 * np.pi / half * (index[:, None] * index[None, :] % half)
    cos_part, sin_part = np.cos(angle), np.sin(angle)
    right = np.block([[cos_part, -sin_part], [sin_part, cos_part]])
    high, low = split_pair(right)
    turn = 2.0 * np.pi / amount * index
    twiddle = np.stack([np.cos(turn), np.sin(turn)]).astype(np.float32)
    return high, low, np.ascontiguousarray(high.T), np.ascontiguousarray(low.T), twiddle


def class_tables(amount, classes):
    length = amount // classes
    index = np.arange(length)
    every = []
    for which in range(classes):
        turns = (which + classes * index[:, None]) * index[None, :] % amount
        angle = 2.0 * np.pi / amount * turns
        cos_part, sin_part = np.cos(angle), np.sin(angle)
        forward = np.block([[cos_part, sin_part], [-sin_part, cos_part]])
        every.append(np.stack([*split_pair(forward), *split_pair(forward.T)]))
    return np.stack(every).reshape(2, classes // 2, 4, 2 * length, 2 * length)


def split(value):
    high = value.astype(jnp.bfloat16)
    return high, (value - high.astype(jnp.float32)).astype(jnp.bfloat16)


def product(left, right, contract):
    dot = functools.partial(
        lax.dot_general,
        dimension_numbers=(contract, ((), ())),
        preferred_element_type=jnp.float32,
    )
    return dot(left[0], right[0]) + (dot(left[1], right[0]) + dot(left[0], right[1]))


def swap_halves(first, second):
    low = lax.broadcasted_iota(jnp.int32, first.shape, first.ndim - 1) < LANES // 2
    one = jnp.where(low, first, pltpu.roll(second, LANES // 2, first.ndim - 1))
    two = jnp.where(low, pltpu.roll(first, LANES // 2, first.ndim - 1), second)
    return one, two


def butterfly_in(real_part, imag_part, twiddle):
    half = real_part.shape[-1] // 2
    cos_row, sin_row = twiddle[0:1, :], twiddle[1:2, :]
    even = (real_part[:, :half] + real_part[:, half:], imag_part[:, :half] + imag_part[:, half:])
    real_gap = real_part[:, :half] - real_part[:, half:]
    imag_gap = imag_part[:, :half] - imag_part[:, half:]
    odd = (
        real_gap * cos_row + imag_gap * sin_row,
        imag_gap * cos_row - real_gap * sin_row,
    )
    return even, odd


def butterfly_out(even, odd, twiddle):
    cos_row, sin_row = twiddle[0:1, :], twiddle[1:2, :]
    real_turn = odd[0] * cos_row - odd[1] * sin_row
    imag_turn = odd[0] * sin_row + odd[1] * cos_row
    real_part = jnp.concatenate([even[0] + real_turn, even[0] - real_turn], 1)
    imag_part = jnp.concatenate([even[1] + imag_turn, even[1] - imag_turn], 1)
    return real_part, imag_part


ROOT_HALF = math.sqrt(0.5)


def turn_eighths(pair, which, sign):
    if which == 0:
        return pair
    low = lax.broadcasted_iota(jnp.int32, pair.shape, pair.ndim - 1) < LANES // 2
    other = pltpu.roll(pair, LANES // 2, pair.ndim - 1)
    crossed = jnp.where(low, other, -other) if sign < 0 else jnp.where(low, -other, other)
    if which == 2:
        return crossed
    return ROOT_HALF * (crossed + pair) if which == 1 else ROOT_HALF * (crossed - pair)


def fold_classes(real_parts, imag_parts):
    def plus(first, second):
        return tuple(parts[first] + parts[second] for parts in (real_parts, imag_parts))

    def minus(first, second):
        return tuple(parts[first] - parts[second] for parts in (real_parts, imag_parts))

    sum_even, sum_odd, gap_even, gap_odd = plus(0, 2), plus(1, 3), minus(0, 2), minus(1, 3)
    fours = [
        (sum_even[0] + sum_odd[0], sum_even[1] + sum_odd[1]),
        (gap_even[0] + gap_odd[1], gap_even[1] - gap_odd[0]),
        (sum_even[0] - sum_odd[0], sum_even[1] - sum_odd[1]),
        (gap_even[0] - gap_odd[1], gap_even[1] + gap_odd[0]),
    ]
    sides = []
    for which, (real_part, imag_part) in enumerate(fours):
        near, far = swap_halves(real_part, imag_part)
        far = turn_eighths(far, which, -1)
        sides.append((near + far, near - far))
    return sides


def unfold_classes(sides):
    fours = []
    for which, (first, second) in enumerate(sides):
        near, far = first + second, turn_eighths(first - second, which, 1)
        fours.append(swap_halves(near, far))
    sum_even = [fours[0][i] + fours[2][i] for i in range(2)]
    gap_even = [fours[0][i] - fours[2][i] for i in range(2)]
    sum_odd = [fours[1][i] + fours[3][i] for i in range(2)]
    gap_odd = [fours[1][i] - fours[3][i] for i in range(2)]
    return [
        (sum_even[0] + sum_odd[0], sum_even[1] + sum_odd[1]),
        (gap_even[0] - gap_odd[1], gap_even[1] + gap_odd[0]),
        (sum_even[0] - sum_odd[0], sum_even[1] - sum_odd[1]),
        (gap_even[0] + gap_odd[1], gap_even[1] - gap_odd[0]),
    ]


ORDER = (3, 2, 1)
PARTS = 2


def couple_kernel(
    lat_count, lay_count, planes, rows,
    layer_any, rate_any, toeplitz_any, hankel_any,
    field_any, fh_any, fl_any, ih_any, il_any, tables_any, twiddle_any,
    out_any,
    send_fold, recv_fold, send_in, recv_in, send_out, recv_mid, send_fin, recv_fin,
    field_x, spectrum, mixed, powers,
    field_ref, fh_ref, fl_ref, ih_ref, il_ref, tables_ref, twiddle_ref,
    layer_ref, rate_ref, toeplitz_ref, hankel_ref, out_ref,
    fold_send, fold_recv, in_send, in_recv, out_send, out_recv, fin_send, fin_recv, load_sem, store_sem,
):
    inner = 2
    outer = lat_count // inner
    peers = inner * lay_count
    my_lat, my_lay = lax.axis_index("lat"), lax.axis_index("lay")
    my_outer = my_lat // inner
    my_peer = my_lat % inner * lay_count + my_lay
    lines, width_y = field_ref.shape[1:]
    width_x = rows * lat_count
    half_x = width_x // 2
    classes = 2 * outer
    length = width_y // classes
    depth = length // peers
    plane_total = planes * lay_count
    layer_count = rate_ref.shape[0]
    pairs = planes // 2

    def column(way):
        low = (my_outer % 2 + way % 2) % 2
        high = (my_outer // 2 + way // 2) % 2
        return 2 * high + low

    def column_id(way):
        return column(way) * inner + my_lat % inner, my_lay

    def peer(step):
        return (my_peer + step) % peers

    def peer_id(step):
        to = peer(step)
        return my_outer * inner + to // lay_count, to % lay_count

    def over_peers(act):
        def one(step, carry):
            act(step)
            return carry

        lax.fori_loop(1, peers, one, 0)

    chunk = LANES
    chunks = lines // chunk
    loads = [
        pltpu.make_async_copy(
            field_any.at[:, pl.ds(i * chunk, chunk)],
            field_ref.at[:, pl.ds(i * chunk, chunk)],
            load_sem.at[i],
        )
        for i in range(chunks)
    ] + [
        pltpu.make_async_copy(source, target, load_sem.at[chunks + i])
        for i, (source, target) in enumerate(
            [
                (tables_any.at[0, my_outer], tables_ref.at[0]),
                (tables_any.at[1, my_outer], tables_ref.at[1]),
                (rate_any, rate_ref), (layer_any, layer_ref),
                (toeplitz_any, toeplitz_ref), (hankel_any, hankel_ref),
                (fh_any, fh_ref), (fl_any, fl_ref), (ih_any, ih_ref), (il_any, il_ref),
                (twiddle_any, twiddle_ref),
            ]
        )
    ]
    for load in loads[:chunks]:
        load.start()

    barrier = pltpu.get_barrier_semaphore()
    for way in range(1, outer):
        pl.semaphore_signal(barrier, inc=1, device_id=column_id(way), device_id_type=MESH)
    over_peers(
        lambda step: pl.semaphore_signal(
            barrier, inc=1, device_id=peer_id(step), device_id_type=MESH
        )
    )

    def remote(source, target, sems, device):
        return pltpu.make_async_remote_copy(
            src_ref=source,
            dst_ref=target,
            send_sem=sems[0],
            recv_sem=sems[1],
            device_id=device,
            device_id_type=MESH,
        )

    def wait_bytes(view, sem):
        pltpu.make_async_copy(view, view, sem).wait()

    others, ways = pl.ds(0, peers - 1), pl.ds(0, outer - 1)

    def fold_copy(side, way, part):
        where = pl.ds(part * (lines // PARTS), lines // PARTS)
        return remote(
            send_fold.at[column(way), side, where], recv_fold.at[my_outer, side, where],
            (fold_send, fold_recv.at[side, way]), column_id(way),
        )

    def in_copy(origin, side, step):
        return remote(
            send_in.at[peer(step), origin, side], recv_in.at[origin, my_peer, side],
            (in_send, in_recv.at[origin, side]), peer_id(step),
        )

    def out_copy(side, pair, step):
        return remote(
            send_out.at[peer(step), side, pair], recv_mid.at[my_peer, side, pair],
            (out_send, out_recv.at[side, pair]), peer_id(step),
        )

    def fin_copy(side, pair, way):
        return remote(
            send_fin.at[column(way), side, pair], recv_fin.at[my_outer, side, pair],
            (fin_send, fin_recv.at[pair]), column_id(way),
        )

    middle = (my_outer + 1) // 2 % 2

    def fold(part):
        for i in range(part * chunks // PARTS, (part + 1) * chunks // PARTS):
            where = slice(i * chunk, (i + 1) * chunk)
            loads[i].wait()
            parts = [
                [field_ref[comp, where, t * LANES:(t + 1) * LANES] for t in range(outer)]
                for comp in range(2)
            ]
            for which, both in enumerate(fold_classes(*parts)):
                for side in range(2):
                    send_fold[which, side, where] = both[side]

    def send_folded(side, part):
        for way in ORDER:
            fold_copy(side, way, part).start()

    for part in range(PARTS):
        fold(part)
        if part == 0:
            for load in loads[chunks:]:
                load.start()
            pl.semaphore_wait(barrier, outer - 1 + peers - 1)
        send_folded(0, part)

    @pl.when(middle == 1)
    def _():
        for part in range(PARTS):
            send_folded(1, part)

    loads[chunks].wait()
    loads[chunks + 1].wait()

    def transform_y(source, origin, side):
        for start in range(0, lines, 2 * LANES):
            where = slice(start, start + 2 * LANES)
            right = split(source[origin, side, where])
            result = product((tables_ref[side, 0], tables_ref[side, 1]), right, ((1,), (1,)))
            for comp in range(2):
                piece = result[comp * length:(comp + 1) * length]
                send_in[:, origin, side, comp, :, where] = piece.reshape(peers, depth, 2 * LANES)
        over_peers(lambda step: in_copy(origin, side, step).start())
        recv_in[origin, my_peer, side] = send_in[my_peer, origin, side]

    for side in range(2):
        transform_y(send_fold, my_outer, side)
    loads[chunks + 2].wait()

    def signed(index, amount):
        index = jnp.where(index >= amount // 2, index - amount, index)
        return index.astype(jnp.float32) / (amount / 2)

    tile = (depth, width_x)
    place_x = lax.broadcasted_iota(jnp.int32, tile, 1)
    freq_x = signed(2 * (place_x % half_x) + place_x // half_x, width_x)
    for side in range(2):
        place_y = my_peer * depth + lax.broadcasted_iota(jnp.int32, tile, 0)
        freq_y = signed(classes * place_y + my_outer + outer * side, width_y)
        steepness = jnp.sqrt(1.0 + freq_x * freq_x + freq_y * freq_y)

        def one_layer(layer, carry):
            base = jnp.exp(steepness * (-rate_ref[layer] / (2 * plane_total)))

            def one_power(m, value):
                powers[side, layer, m] = value
                return value * base

            lax.fori_loop(0, 2 * plane_total - 1, one_power, jnp.ones(tile, jnp.float32))
            return carry

        lax.fori_loop(0, layer_count, one_layer, 0)

    for load in loads[chunks + 3:]:
        load.wait()

    def gather(side, way):
        wait_bytes(recv_fold.at[column(way), side], fold_recv.at[side, way])
        transform_y(recv_fold, column(way), side)

    early, late = 3 - middle, 2 + middle
    gather(0, early)
    gather(0, 1)
    gather(0, late)

    @pl.when(middle == 0)
    def _():
        for part in range(PARTS):
            send_folded(1, part)

    def load_lines(side):
        def one_lay(lay, carry):
            for pair in range(pairs):
                lanes = slice(pair * LANES, (pair + 1) * LANES)
                for block in range(outer):
                    first = recv_in[block, lay, side, :, :, lanes]
                    second = recv_in[block, lay_count + lay, side, :, :, lanes]
                    even, odd = swap_halves(first, second)
                    place = slice(block * LANES, (block + 1) * LANES)
                    field_x[:, lay * planes + 2 * pair, :, place] = even
                    field_x[:, lay * planes + 2 * pair + 1, :, place] = odd
            return carry

        lax.fori_loop(0, lay_count, one_lay, 0)

    group = min(plane_total, LANES // SUBLANES)

    def transform_x(step, carry):
        some = pl.ds(step * group, group)
        flat = (group * depth, width_x)
        halves = butterfly_in(
            field_x[0, some].reshape(flat), field_x[1, some].reshape(flat), twiddle_ref
        )
        for half, pair in enumerate(halves):
            left = split(jnp.concatenate(pair, 1))
            result = product(left, (fh_ref[...], fl_ref[...]), ((1,), (0,)))
            for comp in range(2):
                piece = result[:, comp * half_x:(comp + 1) * half_x]
                spectrum[comp, some, :, half * half_x:(half + 1) * half_x] = piece.reshape(
                    group, depth, half_x
                )
        return carry

    some_planes = 2 * lay_count

    def invert_x():
        halves = []
        for half in range(2):
            place = slice(half * half_x, (half + 1) * half_x)
            flat = (some_planes * depth, half_x)
            left = split(
                jnp.concatenate(
                    [mixed[comp, :, :, place].reshape(flat) for comp in range(2)], 1
                )
            )
            result = product(left, (ih_ref[...], il_ref[...]), ((1,), (0,)))
            halves.append((result[:, :half_x], result[:, half_x:]))
        real_part, imag_part = butterfly_out(halves[0], halves[1], twiddle_ref)
        full = (some_planes, depth, width_x)
        factor = 1.0 / (width_x * width_y)
        mixed[0] = (real_part * factor).reshape(full)
        mixed[1] = (imag_part * factor).reshape(full)

    def store_lines(side, pair):
        for lay in range(lay_count):
            for block in range(outer):
                place = slice(block * LANES, (block + 1) * LANES)
                even, odd = mixed[:, 2 * lay, :, place], mixed[:, 2 * lay + 1, :, place]
                first, second = swap_halves(even, odd)
                send_out[lay, side, pair, :, :, place] = first
                send_out[lay_count + lay, side, pair, :, :, place] = second

    def couple(side, pair):
        def one_plane(place, carry):
            plane = place // 2 * planes + 2 * pair + place % 2
            layer = layer_ref[plane]
            real_sum = jnp.zeros(tile, jnp.float32)
            imag_sum = jnp.zeros(tile, jnp.float32)
            for source in range(plane_total):
                offset = plane - source
                direct = powers[side, layer, 2 * jnp.abs(offset)]
                mirror = powers[side, layer, plane + source]
                at = offset + plane_total - 1
                kern_real = (
                    toeplitz_ref[0, layer, at] * direct
                    + hankel_ref[0, layer, plane + source] * mirror
                )
                kern_imag = (
                    toeplitz_ref[1, layer, at] * direct
                    + hankel_ref[1, layer, plane + source] * mirror
                )
                real_src, imag_src = spectrum[0, source], spectrum[1, source]
                real_sum += kern_real * real_src - kern_imag * imag_src
                imag_sum += kern_real * imag_src + kern_imag * real_src
            mixed[0, place] = real_sum
            mixed[1, place] = imag_sum
            return carry

        lax.fori_loop(0, some_planes, one_plane, 0)

    def invert_y(side, pair):
        wait_bytes(recv_mid.at[others, side, pair], out_recv.at[side, pair])
        stack = jnp.concatenate(
            [recv_mid[:, side, pair, comp].reshape(length, outer * LANES) for comp in range(2)], 0
        )
        result = product((tables_ref[side, 2], tables_ref[side, 3]), split(stack), ((1,), (0,)))
        for block in range(outer):
            send_fin[block, side, pair] = result[:, block * LANES:(block + 1) * LANES].T
        recv_fin[my_outer, side, pair] = send_fin[my_outer, side, pair]

    def send_final(side, pair):
        for way in ORDER:
            fin_copy(side, pair, way).start()

    for side in range(2):
        for origin in range(outer):
            wait_bytes(recv_in.at[origin, others, side], in_recv.at[origin, side])
        load_lines(side)
        lax.fori_loop(0, plane_total // group, transform_x, 0)

        def one_pair(pair, carry):
            couple(side, pair)
            invert_x()
            store_lines(side, pair)
            over_peers(lambda step: out_copy(side, pair, step).start())
            recv_mid[my_peer, side, pair] = send_out[my_peer, side, pair]

            if side == 0:

                @pl.when(pair == pairs - 2)
                def _():
                    gather(1, early)

                @pl.when(pair == pairs - 1)
                def _():
                    gather(1, 1)

            @pl.when(pair >= 1)
            def _():
                invert_y(side, pair - 1)
                if side == 0:

                    @pl.when(middle == 1)
                    def _():
                        send_final(side, pair - 1)

                else:
                    send_final(side, pair - 1)

            return carry

        lax.fori_loop(0, pairs, one_pair, 0)
        if side == 0:
            gather(1, late)

            @pl.when(middle == 0)
            def _():
                for pair in range(pairs - 1):
                    send_final(side, pair)

        invert_y(side, pairs - 1)
        send_final(side, pairs - 1)

    wait_bytes(send_fold.at[ways], fold_send)
    wait_bytes(send_in.at[others], in_send)
    wait_bytes(send_out.at[others], out_send)

    def store(pair):
        where = pl.ds(pair * LANES, LANES)
        return pltpu.make_async_copy(
            out_ref.at[:, where], out_any.at[:, where], store_sem.at[pair]
        )

    def finish(pair, carry):
        wait_bytes(recv_fin.at[ways, :, pair], fin_recv.at[pair])
        where = pl.ds(pair * LANES, LANES)
        sides = [(recv_fin[which, 0, pair], recv_fin[which, 1, pair]) for which in range(outer)]
        for t, (real_part, imag_part) in enumerate(unfold_classes(sides)):
            out_ref[0, where, t * LANES:(t + 1) * LANES] = real_part
            out_ref[1, where, t * LANES:(t + 1) * LANES] = imag_part
        store(pair).start()
        return carry

    lax.fori_loop(0, pairs, finish, 0)

    wait_bytes(send_fin.at[ways], fin_send)
    for pair in range(pairs):
        store(pair).wait()


def fast_body(wave_field, contrast, layer_of_plane, toeplitz_table, hankel_table, layer_rates):
    _, planes, rows, width_y = wave_field.shape
    lat_count, lay_count = lax.axis_size("lat"), lax.axis_size("lay")
    outer, peers = lat_count // 2, 2 * lay_count
    width_x = rows * lat_count
    depth = width_y // (2 * outer * peers)
    plane_total = planes * lay_count
    layer_count = layer_rates.shape[0]
    lines = planes * rows
    pairs = planes // 2
    fh, fl, ih, il, twiddle = (jnp.asarray(t) for t in split_tables(width_x))
    tables = jnp.asarray(class_tables(width_y, 2 * outer))
    operands = [
        layer_of_plane, layer_rates, toeplitz_table, hankel_table,
        wave_field.reshape(2, lines, width_y), fh, fl, ih, il, tables, twiddle,
    ]
    folded = (outer, 2, lines, LANES)
    final = (outer, 2, pairs, LANES, LANES)
    tile_all = (2, plane_total, depth, width_x)
    dma = pltpu.SemaphoreType.DMA
    space = pl.pallas_call(
        functools.partial(couple_kernel, lat_count, lay_count, planes, rows),
        out_shape=jax.ShapeDtypeStruct((2, lines, width_y), jnp.float32),
        in_specs=[pl.BlockSpec(memory_space=pltpu.HBM)] * len(operands),
        out_specs=pl.BlockSpec(memory_space=pl.ANY),
        scratch_shapes=[
            pltpu.VMEM(folded, jnp.float32),
            pltpu.VMEM(folded, jnp.float32),
            pltpu.VMEM((peers, outer, 2, 2, depth, lines), jnp.float32),
            pltpu.VMEM((outer, peers, 2, 2, depth, lines), jnp.float32),
            pltpu.VMEM((peers, 2, pairs, 2, depth, outer * LANES), jnp.float32),
            pltpu.VMEM((peers, 2, pairs, 2, depth, outer * LANES), jnp.float32),
            pltpu.VMEM(final, jnp.float32),
            pltpu.VMEM(final, jnp.float32),
            pltpu.VMEM(tile_all, jnp.float32),
            pltpu.VMEM(tile_all, jnp.float32),
            pltpu.VMEM((2, 2 * lay_count, depth, width_x), jnp.float32),
            pltpu.VMEM((2, layer_count, 2 * plane_total - 1, depth, width_x), jnp.float32),
            pltpu.VMEM((2, lines, width_y), jnp.float32),
            pltpu.VMEM(fh.shape, fh.dtype),
            pltpu.VMEM(fl.shape, fl.dtype),
            pltpu.VMEM(ih.shape, ih.dtype),
            pltpu.VMEM(il.shape, il.dtype),
            pltpu.VMEM((2,) + tables.shape[2:], tables.dtype),
            pltpu.VMEM(twiddle.shape, twiddle.dtype),
            pltpu.SMEM(layer_of_plane.shape, layer_of_plane.dtype),
            pltpu.SMEM(layer_rates.shape, layer_rates.dtype),
            pltpu.SMEM(toeplitz_table.shape, toeplitz_table.dtype),
            pltpu.SMEM(hankel_table.shape, hankel_table.dtype),
            pltpu.VMEM((2, lines, width_y), jnp.float32),
            dma(()), dma((2, outer)),
            dma(()), dma((outer, 2)),
            dma(()), dma((2, pairs)),
            dma(()), dma((pairs,)),
            dma((lines // LANES + 11,)),
            dma((pairs,)),
        ],
        compiler_params=pltpu.CompilerParams(
            collective_id=0, has_side_effects=True, vmem_limit_bytes=48 * 1024 * 1024
        ),
        name="couple",
    )(*(pltpu.with_memory_space_constraint(value, pltpu.HBM) for value in operands))
    return space.reshape(wave_field.shape) * contrast[None]


def body(wave_field, *others):
    _, planes, rows, width_y = wave_field.shape
    lat_count, lay_count = lax.axis_size("lat"), lax.axis_size("lay")
    outer, peers = lat_count // 2, 2 * lay_count
    width_x = rows * lat_count
    fits = (
        lat_count % 2 == 0
        and outer == 4
        and 2 * rows == LANES
        and planes % 2 == 0
        and planes >= 4
        and width_x == width_y
        and width_y == outer * LANES
        and width_y == 2 * outer * peers * SUBLANES
        and (planes * lay_count) % (LANES // SUBLANES) == 0
        and (planes * rows) % (2 * PARTS * LANES) == 0
    )
    return (fast_body if fits else general_body)(wave_field, *others)


def solution(mesh):
    return jax.shard_map(
        body,
        mesh=mesh,
        in_specs=(P(None, "lay", "lat", None), P("lay", "lat", None), P(), P(), P(), P()),
        out_specs=P(None, "lay", "lat", None),
        check_vma=False,
    )
```

```python
import math

import functools

import jax
import jax.numpy as jnp
import numpy as np
from jax import lax
from jax.experimental import pallas as pl
from jax.experimental.pallas import tpu as pltpu
from jax.sharding import PartitionSpec as P

HIGHEST = lax.Precision.HIGHEST


def signed_of(index, amount):
    return jnp.where(index >= amount // 2, index - amount, index).astype(jnp.float32) / (amount / 2)


def phase_tables(rows, cols, amount, sign):
    index_row = lax.broadcasted_iota(jnp.int32, (rows, cols), 0)
    index_col = lax.broadcasted_iota(jnp.int32, (rows, cols), 1)
    angle = 2.0 * math.pi / amount * (index_row * index_col % amount).astype(jnp.float32)
    return (jnp.cos(angle), sign * jnp.sin(angle))


def complex_apply(real_part, imag_part, cos_table, sin_table, form):
    out_real = jnp.einsum(form, real_part, cos_table, precision=HIGHEST) - jnp.einsum(
        form, imag_part, sin_table, precision=HIGHEST
    )
    out_imag = jnp.einsum(form, real_part, sin_table, precision=HIGHEST) + jnp.einsum(
        form, imag_part, cos_table, precision=HIGHEST
    )
    return (out_real, out_imag)


def fourier_last(real_part, imag_part, sign, factor):
    amount = real_part.shape[-1]
    leading = real_part.shape[:-1]
    first = 1
    for divisor in range(1, math.isqrt(amount) + 1):
        if amount % divisor == 0:
            first = divisor
    second = amount // first
    flat_real = real_part.reshape(-1, second, first)
    flat_imag = imag_part.reshape(-1, second, first)
    cos_second, sin_second = phase_tables(second, second, second, sign)
    section_real, section_imag = complex_apply(
        flat_real, flat_imag, cos_second, sin_second, "pmn,mk->pkn"
    )
    twist_cos, twist_sin = phase_tables(second, first, amount, sign)
    turned_real = section_real * twist_cos - section_imag * twist_sin
    turned_imag = section_real * twist_sin + section_imag * twist_cos
    cos_first, sin_first = phase_tables(first, first, first, sign)
    final_real, final_imag = complex_apply(
        turned_real, turned_imag, cos_first, sin_first, "pkn,nj->pjk"
    )
    final_real = final_real.reshape(leading + (amount,)) * factor
    final_imag = final_imag.reshape(leading + (amount,)) * factor
    return (final_real, final_imag)


def pick_amplitudes(rows, index, width):
    positions = jnp.arange(width, dtype=jnp.int32)
    onehot = (index[:, :, None] == positions[None, None, :]).astype(jnp.float32)
    return jnp.einsum("pan,ain->pai", rows, onehot, precision=HIGHEST)


def general_body(wave_field, contrast, layer_of_plane, toeplitz_table, hankel_table, layer_rates):
    row_count = wave_field.shape[2]
    width_y = wave_field.shape[3]
    lat_count = lax.axis_size("lat")
    lay_count = lax.axis_size("lay")
    width_x = row_count * lat_count
    ky_band = width_y // lat_count
    table_width = toeplitz_table.shape[-1]
    plane_total = (table_width + 1) // 2
    layer_count = layer_rates.shape[0]
    spec_real, spec_imag = fourier_last(wave_field[0], wave_field[1], -1.0, 1.0)
    along_y = jnp.stack([spec_real, spec_imag], 2)
    freq_x = signed_of(jnp.arange(width_x, dtype=jnp.int32), width_x)
    ky_first = lax.axis_index("lat") * ky_band
    layer_ids = jnp.arange(layer_count, dtype=jnp.int32)

    def couple(z_out, z_in, source, ky_rows):
        onehot = (layer_of_plane[z_out][:, None] == layer_ids[None, :]).astype(jnp.float32)
        rate_out = jnp.dot(onehot, layer_rates, precision=HIGHEST)
        rows_toeplitz = jnp.einsum("al,pln->pan", onehot, toeplitz_table, precision=HIGHEST)
        rows_hankel = jnp.einsum("al,pln->pan", onehot, hankel_table, precision=HIGHEST)
        offset = z_out[:, None] - z_in[None, :]
        plane_sum = z_out[:, None] + z_in[None, :]
        amp_toeplitz = pick_amplitudes(rows_toeplitz, offset + plane_total - 1, table_width)
        amp_hankel = pick_amplitudes(rows_hankel, plane_sum, table_width)
        freq_y = signed_of(ky_rows, width_y)
        steepness = jnp.sqrt(1.0 + freq_y[:, None] ** 2 + freq_x[None, :] ** 2)
        scaled = rate_out[:, None, None, None] * steepness[None, None] / plane_total
        decay_toeplitz = jnp.exp(-scaled * jnp.abs(offset).astype(jnp.float32)[:, :, None, None])
        decay_hankel = jnp.exp(-scaled * (0.5 * plane_sum.astype(jnp.float32))[:, :, None, None])
        kern_real = (
            amp_toeplitz[0][:, :, None, None] * decay_toeplitz
            + amp_hankel[0][:, :, None, None] * decay_hankel
        )
        kern_imag = (
            amp_toeplitz[1][:, :, None, None] * decay_toeplitz
            + amp_hankel[1][:, :, None, None] * decay_hankel
        )
        real_src = source[None, :, 0]
        imag_src = source[None, :, 1]
        out_real = jnp.sum(kern_real * real_src - kern_imag * imag_src, axis=1)
        out_imag = jnp.sum(kern_real * imag_src + kern_imag * real_src, axis=1)
        return jnp.stack([out_real, out_imag], 1)

    narrow = ky_band // lay_count
    narrow_rows = ky_first + lax.axis_index("lay") * narrow + jnp.arange(narrow, dtype=jnp.int32)
    lines_in = lax.all_to_all(along_y, "lat", split_axis=3, concat_axis=1, tiled=True)
    line_real = jnp.transpose(lines_in[:, :, 0], (0, 2, 1))
    line_imag = jnp.transpose(lines_in[:, :, 1], (0, 2, 1))
    out_real, out_imag = fourier_last(line_real, line_imag, -1.0, 1.0)
    spectrum = jnp.stack([out_real, out_imag], 1)
    gathered = lax.all_to_all(spectrum, "lay", split_axis=2, concat_axis=0, tiled=True)
    all_planes = gathered.shape[0]
    every_plane = jnp.arange(all_planes, dtype=jnp.int32)
    block_size = math.gcd(all_planes, 8)

    def one_block(which):
        z_out = which * block_size + jnp.arange(block_size, dtype=jnp.int32)
        return couple(z_out, every_plane, gathered, narrow_rows)

    stacked = lax.map(one_block, jnp.arange(all_planes // block_size, dtype=jnp.int32))
    coupled = stacked.reshape(all_planes, 2, narrow_rows.shape[0], width_x)
    mixed = lax.all_to_all(coupled, "lay", split_axis=0, concat_axis=2, tiled=True)
    out_real, out_imag = fourier_last(mixed[:, 0], mixed[:, 1], 1.0, 1.0 / width_x)
    spatial_x = jnp.transpose(jnp.stack([out_real, out_imag], 1), (0, 3, 1, 2))
    lines = lax.all_to_all(spatial_x, "lat", split_axis=1, concat_axis=3, tiled=True)
    space_real, space_imag = fourier_last(lines[:, :, 0], lines[:, :, 1], 1.0, 1.0 / width_y)
    return jnp.stack([space_real, space_imag], 0) * contrast[None]


LANES = 128
SUBLANES = 8
MESH = pl.DeviceIdType.MESH


def split_pair(table):
    table = table.astype(np.float32)
    high = table.astype(jnp.bfloat16)
    return high, (table - high.astype(np.float32)).astype(jnp.bfloat16)


def split_tables(amount):
    half = amount // 2
    index = np.arange(half)
    angle = 2.0 * np.pi / half * (index[:, None] * index[None, :] % half)
    cos_part, sin_part = np.cos(angle), np.sin(angle)
    right = np.block([[cos_part, -sin_part], [sin_part, cos_part]])
    high, low = split_pair(right)
    turn = 2.0 * np.pi / amount * index
    twiddle = np.stack([np.cos(turn), np.sin(turn)]).astype(np.float32)
    return high, low, np.ascontiguousarray(high.T), np.ascontiguousarray(low.T), twiddle


def class_tables(amount, classes):
    length = amount // classes
    index = np.arange(length)
    every = []
    for which in range(classes):
        turns = (which + classes * index[:, None]) * index[None, :] % amount
        angle = 2.0 * np.pi / amount * turns
        cos_part, sin_part = np.cos(angle), np.sin(angle)
        forward = np.block([[cos_part, sin_part], [-sin_part, cos_part]])
        every.append(np.stack([*split_pair(forward), *split_pair(forward.T)]))
    return np.stack(every).reshape(2, classes // 2, 4, 2 * length, 2 * length)


def split(value):
    high = value.astype(jnp.bfloat16)
    return high, (value - high.astype(jnp.float32)).astype(jnp.bfloat16)


def product(left, right, contract):
    dot = functools.partial(
        lax.dot_general,
        dimension_numbers=(contract, ((), ())),
        preferred_element_type=jnp.float32,
    )
    return dot(left[0], right[0]) + (dot(left[1], right[0]) + dot(left[0], right[1]))


def swap_halves(first, second):
    low = lax.broadcasted_iota(jnp.int32, first.shape, first.ndim - 1) < LANES // 2
    one = jnp.where(low, first, pltpu.roll(second, LANES // 2, first.ndim - 1))
    two = jnp.where(low, pltpu.roll(first, LANES // 2, first.ndim - 1), second)
    return one, two


def butterfly_in(real_part, imag_part, twiddle):
    half = real_part.shape[-1] // 2
    cos_row, sin_row = twiddle[0:1, :], twiddle[1:2, :]
    even = (real_part[:, :half] + real_part[:, half:], imag_part[:, :half] + imag_part[:, half:])
    real_gap = real_part[:, :half] - real_part[:, half:]
    imag_gap = imag_part[:, :half] - imag_part[:, half:]
    odd = (
        real_gap * cos_row + imag_gap * sin_row,
        imag_gap * cos_row - real_gap * sin_row,
    )
    return even, odd


def butterfly_out(even, odd, twiddle):
    cos_row, sin_row = twiddle[0:1, :], twiddle[1:2, :]
    real_turn = odd[0] * cos_row - odd[1] * sin_row
    imag_turn = odd[0] * sin_row + odd[1] * cos_row
    real_part = jnp.concatenate([even[0] + real_turn, even[0] - real_turn], 1)
    imag_part = jnp.concatenate([even[1] + imag_turn, even[1] - imag_turn], 1)
    return real_part, imag_part


ROOT_HALF = math.sqrt(0.5)


def turn_eighths(pair, which, sign):
    if which == 0:
        return pair
    low = lax.broadcasted_iota(jnp.int32, pair.shape, pair.ndim - 1) < LANES // 2
    other = pltpu.roll(pair, LANES // 2, pair.ndim - 1)
    crossed = jnp.where(low, other, -other) if sign < 0 else jnp.where(low, -other, other)
    if which == 2:
        return crossed
    return ROOT_HALF * (crossed + pair) if which == 1 else ROOT_HALF * (crossed - pair)


def fold_classes(real_parts, imag_parts):
    def plus(first, second):
        return tuple(parts[first] + parts[second] for parts in (real_parts, imag_parts))

    def minus(first, second):
        return tuple(parts[first] - parts[second] for parts in (real_parts, imag_parts))

    sum_even, sum_odd, gap_even, gap_odd = plus(0, 2), plus(1, 3), minus(0, 2), minus(1, 3)
    fours = [
        (sum_even[0] + sum_odd[0], sum_even[1] + sum_odd[1]),
        (gap_even[0] + gap_odd[1], gap_even[1] - gap_odd[0]),
        (sum_even[0] - sum_odd[0], sum_even[1] - sum_odd[1]),
        (gap_even[0] - gap_odd[1], gap_even[1] + gap_odd[0]),
    ]
    sides = []
    for which, (real_part, imag_part) in enumerate(fours):
        near, far = swap_halves(real_part, imag_part)
        far = turn_eighths(far, which, -1)
        sides.append((near + far, near - far))
    return sides


def unfold_classes(sides):
    fours = []
    for which, (first, second) in enumerate(sides):
        near, far = first + second, turn_eighths(first - second, which, 1)
        fours.append(swap_halves(near, far))
    sum_even = [fours[0][i] + fours[2][i] for i in range(2)]
    gap_even = [fours[0][i] - fours[2][i] for i in range(2)]
    sum_odd = [fours[1][i] + fours[3][i] for i in range(2)]
    gap_odd = [fours[1][i] - fours[3][i] for i in range(2)]
    return [
        (sum_even[0] + sum_odd[0], sum_even[1] + sum_odd[1]),
        (gap_even[0] - gap_odd[1], gap_even[1] + gap_odd[0]),
        (sum_even[0] - sum_odd[0], sum_even[1] - sum_odd[1]),
        (gap_even[0] + gap_odd[1], gap_even[1] - gap_odd[0]),
    ]


ORDER = (3, 2, 1)
PARTS = 2


def couple_kernel(
    lat_count, lay_count, planes, rows,
    layer_any, rate_any, toeplitz_any, hankel_any,
    field_any, contrast_any, fh_any, fl_any, ih_any, il_any, tables_any, twiddle_any,
    out_any,
    send_fold, recv_fold, send_in, recv_in, send_out, recv_mid, send_fin, recv_fin,
    field_x, spectrum, mixed, powers,
    field_ref, fh_ref, fl_ref, ih_ref, il_ref, tables_ref, twiddle_ref,
    layer_ref, rate_ref, toeplitz_ref, hankel_ref, out_ref, contrast_ref,
    fold_send, fold_recv, in_send, in_recv, out_send, out_recv, fin_send, fin_recv, load_sem, store_sem,
):
    inner = 2
    outer = lat_count // inner
    peers = inner * lay_count
    my_lat, my_lay = lax.axis_index("lat"), lax.axis_index("lay")
    my_outer = my_lat // inner
    my_peer = my_lat % inner * lay_count + my_lay
    lines, width_y = field_ref.shape[1:]
    width_x = rows * lat_count
    half_x = width_x // 2
    classes = 2 * outer
    length = width_y // classes
    depth = length // peers
    plane_total = planes * lay_count
    layer_count = rate_ref.shape[0]
    pairs = planes // 2

    def column(way):
        low = (my_outer % 2 + way % 2) % 2
        high = (my_outer // 2 + way // 2) % 2
        return 2 * high + low

    def column_id(way):
        return column(way) * inner + my_lat % inner, my_lay

    def peer(step):
        return (my_peer + step) % peers

    def peer_id(step):
        to = peer(step)
        return my_outer * inner + to // lay_count, to % lay_count

    def over_peers(act):
        def one(step, carry):
            act(step)
            return carry

        lax.fori_loop(1, peers, one, 0)

    chunk = LANES
    chunks = lines // chunk
    loads = [
        pltpu.make_async_copy(
            field_any.at[:, pl.ds(i * chunk, chunk)],
            field_ref.at[:, pl.ds(i * chunk, chunk)],
            load_sem.at[i],
        )
        for i in range(chunks)
    ] + [
        pltpu.make_async_copy(source, target, load_sem.at[chunks + i])
        for i, (source, target) in enumerate(
            [
                (tables_any.at[0, my_outer], tables_ref.at[0]),
                (tables_any.at[1, my_outer], tables_ref.at[1]),
                (rate_any, rate_ref), (layer_any, layer_ref),
                (toeplitz_any, toeplitz_ref), (hankel_any, hankel_ref),
                (fh_any, fh_ref), (fl_any, fl_ref), (ih_any, ih_ref), (il_any, il_ref),
                (twiddle_any, twiddle_ref), (contrast_any, contrast_ref),
            ]
        )
    ]
    for load in loads[:chunks]:
        load.start()

    barrier = pltpu.get_barrier_semaphore()
    for way in range(1, outer):
        pl.semaphore_signal(barrier, inc=1, device_id=column_id(way), device_id_type=MESH)
    over_peers(
        lambda step: pl.semaphore_signal(
            barrier, inc=1, device_id=peer_id(step), device_id_type=MESH
        )
    )

    def remote(source, target, sems, device):
        return pltpu.make_async_remote_copy(
            src_ref=source,
            dst_ref=target,
            send_sem=sems[0],
            recv_sem=sems[1],
            device_id=device,
            device_id_type=MESH,
        )

    def wait_bytes(view, sem):
        pltpu.make_async_copy(view, view, sem).wait()

    others, ways = pl.ds(0, peers - 1), pl.ds(0, outer - 1)

    def fold_copy(side, way, part):
        where = pl.ds(part * (lines // PARTS), lines // PARTS)
        return remote(
            send_fold.at[column(way), side, where], recv_fold.at[my_outer, side, where],
            (fold_send, fold_recv.at[side, way]), column_id(way),
        )

    def in_copy(origin, side, step):
        return remote(
            send_in.at[peer(step), origin, side], recv_in.at[origin, my_peer, side],
            (in_send, in_recv.at[origin, side]), peer_id(step),
        )

    def out_copy(side, pair, step):
        return remote(
            send_out.at[peer(step), side, pair], recv_mid.at[my_peer, side, pair],
            (out_send, out_recv.at[side, pair]), peer_id(step),
        )

    def fin_copy(side, pair, way):
        return remote(
            send_fin.at[column(way), side, pair], recv_fin.at[my_outer, side, pair],
            (fin_send, fin_recv.at[pair]), column_id(way),
        )

    middle = (my_outer + 1) // 2 % 2

    def fold(part):
        for i in range(part * chunks // PARTS, (part + 1) * chunks // PARTS):
            where = slice(i * chunk, (i + 1) * chunk)
            loads[i].wait()
            parts = [
                [field_ref[comp, where, t * LANES:(t + 1) * LANES] for t in range(outer)]
                for comp in range(2)
            ]
            for which, both in enumerate(fold_classes(*parts)):
                for side in range(2):
                    send_fold[which, side, where] = both[side]

    def send_folded(side, ways, parts):
        for part in parts:
            for way in ways:
                fold_copy(side, way, part).start()

    for part in range(PARTS):
        fold(part)
        if part == 0:
            for load in loads[chunks:]:
                load.start()
            pl.semaphore_wait(barrier, outer - 1 + peers - 1)
        send_folded(0, ORDER, [part])

    @pl.when(middle == 1)
    def _():
        for way in (3, 1, 2):
            send_folded(1, [way], range(PARTS))

    loads[chunks].wait()
    loads[chunks + 1].wait()

    def transform_y(source, origin, side):
        for start in range(0, lines, 2 * LANES):
            where = slice(start, start + 2 * LANES)
            right = split(source[origin, side, where])
            result = product((tables_ref[side, 0], tables_ref[side, 1]), right, ((1,), (1,)))
            for comp in range(2):
                piece = result[comp * length:(comp + 1) * length]
                send_in[:, origin, side, comp, :, where] = piece.reshape(peers, depth, 2 * LANES)
        over_peers(lambda step: in_copy(origin, side, step).start())
        recv_in[origin, my_peer, side] = send_in[my_peer, origin, side]

    for side in range(2):
        transform_y(send_fold, my_outer, side)
    loads[chunks + 2].wait()

    def signed(index, amount):
        index = jnp.where(index >= amount // 2, index - amount, index)
        return index.astype(jnp.float32) / (amount / 2)

    tile = (depth, width_x)
    place_x = lax.broadcasted_iota(jnp.int32, tile, 1)
    freq_x = signed(2 * (place_x % half_x) + place_x // half_x, width_x)
    for side in range(2):
        place_y = my_peer * depth + lax.broadcasted_iota(jnp.int32, tile, 0)
        freq_y = signed(classes * place_y + my_outer + outer * side, width_y)
        steepness = jnp.sqrt(1.0 + freq_x * freq_x + freq_y * freq_y)

        def one_layer(layer, carry):
            base = jnp.exp(steepness * (-rate_ref[layer] / (2 * plane_total)))

            def one_power(m, value):
                powers[side, layer, m] = value
                return value * base

            lax.fori_loop(0, 2 * plane_total - 1, one_power, jnp.ones(tile, jnp.float32))
            return carry

        lax.fori_loop(0, layer_count, one_layer, 0)

    for load in loads[chunks + 3:]:
        load.wait()

    def gather(side, way):
        wait_bytes(recv_fold.at[column(way), side], fold_recv.at[side, way])
        transform_y(recv_fold, column(way), side)

    early, late = 3 - middle, 2 + middle
    gather(0, early)
    gather(0, 1)
    gather(0, late)

    @pl.when(middle == 0)
    def _():
        for way in (1, 3, 2):
            send_folded(1, [way], range(PARTS))

    def load_lines(side):
        def one_lay(lay, carry):
            for pair in range(pairs):
                lanes = slice(pair * LANES, (pair + 1) * LANES)
                for block in range(outer):
                    first = recv_in[block, lay, side, :, :, lanes]
                    second = recv_in[block, lay_count + lay, side, :, :, lanes]
                    even, odd = swap_halves(first, second)
                    place = slice(block * LANES, (block + 1) * LANES)
                    field_x[:, lay * planes + 2 * pair, :, place] = even
                    field_x[:, lay * planes + 2 * pair + 1, :, place] = odd
            return carry

        lax.fori_loop(0, lay_count, one_lay, 0)

    group = min(plane_total, LANES // SUBLANES)

    def transform_x(step, carry):
        some = pl.ds(step * group, group)
        flat = (group * depth, width_x)
        halves = butterfly_in(
            field_x[0, some].reshape(flat), field_x[1, some].reshape(flat), twiddle_ref
        )
        for half, pair in enumerate(halves):
            left = split(jnp.concatenate(pair, 1))
            result = product(left, (fh_ref[...], fl_ref[...]), ((1,), (0,)))
            for comp in range(2):
                piece = result[:, comp * half_x:(comp + 1) * half_x]
                spectrum[comp, some, :, half * half_x:(half + 1) * half_x] = piece.reshape(
                    group, depth, half_x
                )
        return carry

    some_planes = 2 * lay_count

    def invert_x():
        halves = []
        for half in range(2):
            place = slice(half * half_x, (half + 1) * half_x)
            flat = (some_planes * depth, half_x)
            left = split(
                jnp.concatenate(
                    [mixed[comp, :, :, place].reshape(flat) for comp in range(2)], 1
                )
            )
            result = product(left, (ih_ref[...], il_ref[...]), ((1,), (0,)))
            halves.append((result[:, :half_x], result[:, half_x:]))
        real_part, imag_part = butterfly_out(halves[0], halves[1], twiddle_ref)
        full = (some_planes, depth, width_x)
        factor = 1.0 / (width_x * width_y)
        mixed[0] = (real_part * factor).reshape(full)
        mixed[1] = (imag_part * factor).reshape(full)

    def store_lines(side, pair):
        for lay in range(lay_count):
            for block in range(outer):
                place = slice(block * LANES, (block + 1) * LANES)
                even, odd = mixed[:, 2 * lay, :, place], mixed[:, 2 * lay + 1, :, place]
                first, second = swap_halves(even, odd)
                send_out[lay, side, pair, :, :, place] = first
                send_out[lay_count + lay, side, pair, :, :, place] = second

    def couple(side, pair):
        def one_plane(place, carry):
            plane = place // 2 * planes + 2 * pair + place % 2
            layer = layer_ref[plane]
            real_sum = jnp.zeros(tile, jnp.float32)
            imag_sum = jnp.zeros(tile, jnp.float32)
            for source in range(plane_total):
                offset = plane - source
                direct = powers[side, layer, 2 * jnp.abs(offset)]
                mirror = powers[side, layer, plane + source]
                at = offset + plane_total - 1
                kern_real = (
                    toeplitz_ref[0, layer, at] * direct
                    + hankel_ref[0, layer, plane + source] * mirror
                )
                kern_imag = (
                    toeplitz_ref[1, layer, at] * direct
                    + hankel_ref[1, layer, plane + source] * mirror
                )
                real_src, imag_src = spectrum[0, source], spectrum[1, source]
                real_sum += kern_real * real_src - kern_imag * imag_src
                imag_sum += kern_real * imag_src + kern_imag * real_src
            mixed[0, place] = real_sum
            mixed[1, place] = imag_sum
            return carry

        lax.fori_loop(0, some_planes, one_plane, 0)

    def invert_y(side, pair):
        wait_bytes(recv_mid.at[others, side, pair], out_recv.at[side, pair])
        stack = jnp.concatenate(
            [recv_mid[:, side, pair, comp].reshape(length, outer * LANES) for comp in range(2)], 0
        )
        result = product((tables_ref[side, 2], tables_ref[side, 3]), split(stack), ((1,), (0,)))
        for block in range(outer):
            send_fin[block, side, pair] = result[:, block * LANES:(block + 1) * LANES].T
        recv_fin[my_outer, side, pair] = send_fin[my_outer, side, pair]

    def send_final(side, pair):
        for way in (early, late, 1):
            fin_copy(side, pair, way).start()

    for side in range(2):
        for origin in range(outer):
            wait_bytes(recv_in.at[origin, others, side], in_recv.at[origin, side])
        load_lines(side)
        lax.fori_loop(0, plane_total // group, transform_x, 0)

        def one_pair(pair, carry):
            couple(side, pair)
            invert_x()
            store_lines(side, pair)
            if side == 0:

                @pl.when(pair == pairs - 1)
                def _():
                    gather(1, 2)

            over_peers(lambda step: out_copy(side, pair, step).start())
            recv_mid[my_peer, side, pair] = send_out[my_peer, side, pair]

            if side == 0:

                @pl.when(pair == 1)
                def _():
                    gather(1, 1)

                @pl.when(pair == 2 - middle)
                def _():
                    gather(1, 3)

                @pl.when(pair >= 2)
                def _():
                    invert_y(0, pair - 2)

                    @pl.when(middle == 1)
                    def _():
                        send_final(0, pair - 2)

            else:

                @pl.when(pair == 0)
                def _():
                    invert_y(0, pairs - 1)
                    send_final(0, pairs - 1)

                @pl.when(pair >= 1)
                def _():
                    invert_y(1, pair - 1)
                    send_final(1, pair - 1)

            return carry

        lax.fori_loop(0, pairs, one_pair, 0)
        if side == 0:
            invert_y(0, pairs - 2)

            @pl.when(middle == 0)
            def _():
                for pair in range(pairs - 2):
                    send_final(0, pair)

            send_final(0, pairs - 2)
        else:
            invert_y(1, pairs - 1)
            send_final(1, pairs - 1)

    wait_bytes(send_fold.at[ways], fold_send)
    wait_bytes(send_in.at[others], in_send)
    wait_bytes(send_out.at[others], out_send)

    def store(pair):
        where = pl.ds(pair * LANES, LANES)
        return pltpu.make_async_copy(
            out_ref.at[:, where], out_any.at[:, where], store_sem.at[pair]
        )

    def finish(pair, carry):
        wait_bytes(recv_fin.at[ways, :, pair], fin_recv.at[pair])
        where = pl.ds(pair * LANES, LANES)
        sides = [(recv_fin[which, 0, pair], recv_fin[which, 1, pair]) for which in range(outer)]
        for t, (real_part, imag_part) in enumerate(unfold_classes(sides)):
            place = slice(t * LANES, (t + 1) * LANES)
            scale = contrast_ref[where, place]
            out_ref[0, where, place] = real_part * scale
            out_ref[1, where, place] = imag_part * scale
        store(pair).start()
        return carry

    lax.fori_loop(0, pairs, finish, 0)

    wait_bytes(send_fin.at[ways], fin_send)
    for pair in range(pairs):
        store(pair).wait()


def fast_body(wave_field, contrast, layer_of_plane, toeplitz_table, hankel_table, layer_rates):
    _, planes, rows, width_y = wave_field.shape
    lat_count, lay_count = lax.axis_size("lat"), lax.axis_size("lay")
    outer, peers = lat_count // 2, 2 * lay_count
    width_x = rows * lat_count
    depth = width_y // (2 * outer * peers)
    plane_total = planes * lay_count
    layer_count = layer_rates.shape[0]
    lines = planes * rows
    pairs = planes // 2
    fh, fl, ih, il, twiddle = (jnp.asarray(t) for t in split_tables(width_x))
    tables = jnp.asarray(class_tables(width_y, 2 * outer))
    operands = [
        layer_of_plane, layer_rates, toeplitz_table, hankel_table,
        wave_field.reshape(2, lines, width_y), contrast.reshape(lines, width_y), fh, fl, ih, il, tables, twiddle,
    ]
    folded = (outer, 2, lines, LANES)
    final = (outer, 2, pairs, LANES, LANES)
    tile_all = (2, plane_total, depth, width_x)
    dma = pltpu.SemaphoreType.DMA
    space = pl.pallas_call(
        functools.partial(couple_kernel, lat_count, lay_count, planes, rows),
        out_shape=jax.ShapeDtypeStruct((2, lines, width_y), jnp.float32),
        in_specs=[pl.BlockSpec(memory_space=pltpu.HBM)] * len(operands),
        out_specs=pl.BlockSpec(memory_space=pl.ANY),
        scratch_shapes=[
            pltpu.VMEM(folded, jnp.float32),
            pltpu.VMEM(folded, jnp.float32),
            pltpu.VMEM((peers, outer, 2, 2, depth, lines), jnp.float32),
            pltpu.VMEM((outer, peers, 2, 2, depth, lines), jnp.float32),
            pltpu.VMEM((peers, 2, pairs, 2, depth, outer * LANES), jnp.float32),
            pltpu.VMEM((peers, 2, pairs, 2, depth, outer * LANES), jnp.float32),
            pltpu.VMEM(final, jnp.float32),
            pltpu.VMEM(final, jnp.float32),
            pltpu.VMEM(tile_all, jnp.float32),
            pltpu.VMEM(tile_all, jnp.float32),
            pltpu.VMEM((2, 2 * lay_count, depth, width_x), jnp.float32),
            pltpu.VMEM((2, layer_count, 2 * plane_total - 1, depth, width_x), jnp.float32),
            pltpu.VMEM((2, lines, width_y), jnp.float32),
            pltpu.VMEM(fh.shape, fh.dtype),
            pltpu.VMEM(fl.shape, fl.dtype),
            pltpu.VMEM(ih.shape, ih.dtype),
            pltpu.VMEM(il.shape, il.dtype),
            pltpu.VMEM((2,) + tables.shape[2:], tables.dtype),
            pltpu.VMEM(twiddle.shape, twiddle.dtype),
            pltpu.SMEM(layer_of_plane.shape, layer_of_plane.dtype),
            pltpu.SMEM(layer_rates.shape, layer_rates.dtype),
            pltpu.SMEM(toeplitz_table.shape, toeplitz_table.dtype),
            pltpu.SMEM(hankel_table.shape, hankel_table.dtype),
            pltpu.VMEM((2, lines, width_y), jnp.float32),
            pltpu.VMEM((lines, width_y), jnp.float32),
            dma(()), dma((2, outer)),
            dma(()), dma((outer, 2)),
            dma(()), dma((2, pairs)),
            dma(()), dma((pairs,)),
            dma((lines // LANES + 12,)),
            dma((pairs,)),
        ],
        compiler_params=pltpu.CompilerParams(
            collective_id=0, has_side_effects=True, vmem_limit_bytes=48 * 1024 * 1024
        ),
        name="couple",
    )(*(pltpu.with_memory_space_constraint(value, pltpu.HBM) for value in operands))
    return space.reshape(wave_field.shape)


def body(wave_field, *others):
    _, planes, rows, width_y = wave_field.shape
    lat_count, lay_count = lax.axis_size("lat"), lax.axis_size("lay")
    outer, peers = lat_count // 2, 2 * lay_count
    width_x = rows * lat_count
    fits = (
        lat_count % 2 == 0
        and outer == 4
        and 2 * rows == LANES
        and planes % 2 == 0
        and planes >= 4
        and width_x == width_y
        and width_y == outer * LANES
        and width_y == 2 * outer * peers * SUBLANES
        and (planes * lay_count) % (LANES // SUBLANES) == 0
        and (planes * rows) % (PARTS * LANES) == 0
    )
    return (fast_body if fits else general_body)(wave_field, *others)


def solution(mesh):
    return jax.shard_map(
        body,
        mesh=mesh,
        in_specs=(P(None, "lay", "lat", None), P("lay", "lat", None), P(), P(), P(), P()),
        out_specs=P(None, "lay", "lat", None),
        check_vma=False,
    )
```

```python
import math

import functools

import jax
import jax.numpy as jnp
import numpy as np
from jax import lax
from jax.experimental import pallas as pl
from jax.experimental.pallas import tpu as pltpu
from jax.sharding import PartitionSpec as P

HIGHEST = lax.Precision.HIGHEST


def signed_of(index, amount):
    return jnp.where(index >= amount // 2, index - amount, index).astype(jnp.float32) / (amount / 2)


def phase_tables(rows, cols, amount, sign):
    index_row = lax.broadcasted_iota(jnp.int32, (rows, cols), 0)
    index_col = lax.broadcasted_iota(jnp.int32, (rows, cols), 1)
    angle = 2.0 * math.pi / amount * (index_row * index_col % amount).astype(jnp.float32)
    return (jnp.cos(angle), sign * jnp.sin(angle))


def complex_apply(real_part, imag_part, cos_table, sin_table, form):
    out_real = jnp.einsum(form, real_part, cos_table, precision=HIGHEST) - jnp.einsum(
        form, imag_part, sin_table, precision=HIGHEST
    )
    out_imag = jnp.einsum(form, real_part, sin_table, precision=HIGHEST) + jnp.einsum(
        form, imag_part, cos_table, precision=HIGHEST
    )
    return (out_real, out_imag)


def fourier_last(real_part, imag_part, sign, factor):
    amount = real_part.shape[-1]
    leading = real_part.shape[:-1]
    first = 1
    for divisor in range(1, math.isqrt(amount) + 1):
        if amount % divisor == 0:
            first = divisor
    second = amount // first
    flat_real = real_part.reshape(-1, second, first)
    flat_imag = imag_part.reshape(-1, second, first)
    cos_second, sin_second = phase_tables(second, second, second, sign)
    section_real, section_imag = complex_apply(
        flat_real, flat_imag, cos_second, sin_second, "pmn,mk->pkn"
    )
    twist_cos, twist_sin = phase_tables(second, first, amount, sign)
    turned_real = section_real * twist_cos - section_imag * twist_sin
    turned_imag = section_real * twist_sin + section_imag * twist_cos
    cos_first, sin_first = phase_tables(first, first, first, sign)
    final_real, final_imag = complex_apply(
        turned_real, turned_imag, cos_first, sin_first, "pkn,nj->pjk"
    )
    final_real = final_real.reshape(leading + (amount,)) * factor
    final_imag = final_imag.reshape(leading + (amount,)) * factor
    return (final_real, final_imag)


def pick_amplitudes(rows, index, width):
    positions = jnp.arange(width, dtype=jnp.int32)
    onehot = (index[:, :, None] == positions[None, None, :]).astype(jnp.float32)
    return jnp.einsum("pan,ain->pai", rows, onehot, precision=HIGHEST)


def general_body(wave_field, contrast, layer_of_plane, toeplitz_table, hankel_table, layer_rates):
    row_count = wave_field.shape[2]
    width_y = wave_field.shape[3]
    lat_count = lax.axis_size("lat")
    lay_count = lax.axis_size("lay")
    width_x = row_count * lat_count
    ky_band = width_y // lat_count
    table_width = toeplitz_table.shape[-1]
    plane_total = (table_width + 1) // 2
    layer_count = layer_rates.shape[0]
    spec_real, spec_imag = fourier_last(wave_field[0], wave_field[1], -1.0, 1.0)
    along_y = jnp.stack([spec_real, spec_imag], 2)
    freq_x = signed_of(jnp.arange(width_x, dtype=jnp.int32), width_x)
    ky_first = lax.axis_index("lat") * ky_band
    layer_ids = jnp.arange(layer_count, dtype=jnp.int32)

    def couple(z_out, z_in, source, ky_rows):
        onehot = (layer_of_plane[z_out][:, None] == layer_ids[None, :]).astype(jnp.float32)
        rate_out = jnp.dot(onehot, layer_rates, precision=HIGHEST)
        rows_toeplitz = jnp.einsum("al,pln->pan", onehot, toeplitz_table, precision=HIGHEST)
        rows_hankel = jnp.einsum("al,pln->pan", onehot, hankel_table, precision=HIGHEST)
        offset = z_out[:, None] - z_in[None, :]
        plane_sum = z_out[:, None] + z_in[None, :]
        amp_toeplitz = pick_amplitudes(rows_toeplitz, offset + plane_total - 1, table_width)
        amp_hankel = pick_amplitudes(rows_hankel, plane_sum, table_width)
        freq_y = signed_of(ky_rows, width_y)
        steepness = jnp.sqrt(1.0 + freq_y[:, None] ** 2 + freq_x[None, :] ** 2)
        scaled = rate_out[:, None, None, None] * steepness[None, None] / plane_total
        decay_toeplitz = jnp.exp(-scaled * jnp.abs(offset).astype(jnp.float32)[:, :, None, None])
        decay_hankel = jnp.exp(-scaled * (0.5 * plane_sum.astype(jnp.float32))[:, :, None, None])
        kern_real = (
            amp_toeplitz[0][:, :, None, None] * decay_toeplitz
            + amp_hankel[0][:, :, None, None] * decay_hankel
        )
        kern_imag = (
            amp_toeplitz[1][:, :, None, None] * decay_toeplitz
            + amp_hankel[1][:, :, None, None] * decay_hankel
        )
        real_src = source[None, :, 0]
        imag_src = source[None, :, 1]
        out_real = jnp.sum(kern_real * real_src - kern_imag * imag_src, axis=1)
        out_imag = jnp.sum(kern_real * imag_src + kern_imag * real_src, axis=1)
        return jnp.stack([out_real, out_imag], 1)

    narrow = ky_band // lay_count
    narrow_rows = ky_first + lax.axis_index("lay") * narrow + jnp.arange(narrow, dtype=jnp.int32)
    lines_in = lax.all_to_all(along_y, "lat", split_axis=3, concat_axis=1, tiled=True)
    line_real = jnp.transpose(lines_in[:, :, 0], (0, 2, 1))
    line_imag = jnp.transpose(lines_in[:, :, 1], (0, 2, 1))
    out_real, out_imag = fourier_last(line_real, line_imag, -1.0, 1.0)
    spectrum = jnp.stack([out_real, out_imag], 1)
    gathered = lax.all_to_all(spectrum, "lay", split_axis=2, concat_axis=0, tiled=True)
    all_planes = gathered.shape[0]
    every_plane = jnp.arange(all_planes, dtype=jnp.int32)
    block_size = math.gcd(all_planes, 8)

    def one_block(which):
        z_out = which * block_size + jnp.arange(block_size, dtype=jnp.int32)
        return couple(z_out, every_plane, gathered, narrow_rows)

    stacked = lax.map(one_block, jnp.arange(all_planes // block_size, dtype=jnp.int32))
    coupled = stacked.reshape(all_planes, 2, narrow_rows.shape[0], width_x)
    mixed = lax.all_to_all(coupled, "lay", split_axis=0, concat_axis=2, tiled=True)
    out_real, out_imag = fourier_last(mixed[:, 0], mixed[:, 1], 1.0, 1.0 / width_x)
    spatial_x = jnp.transpose(jnp.stack([out_real, out_imag], 1), (0, 3, 1, 2))
    lines = lax.all_to_all(spatial_x, "lat", split_axis=1, concat_axis=3, tiled=True)
    space_real, space_imag = fourier_last(lines[:, :, 0], lines[:, :, 1], 1.0, 1.0 / width_y)
    return jnp.stack([space_real, space_imag], 0) * contrast[None]


LANES = 128
SUBLANES = 8
MESH = pl.DeviceIdType.MESH


def split_pair(table):
    table = table.astype(np.float32)
    high = table.astype(jnp.bfloat16)
    return high, (table - high.astype(np.float32)).astype(jnp.bfloat16)


def split_tables(amount):
    half = amount // 2
    index = np.arange(half)
    angle = 2.0 * np.pi / half * (index[:, None] * index[None, :] % half)
    cos_part, sin_part = np.cos(angle), np.sin(angle)
    right = np.block([[cos_part, -sin_part], [sin_part, cos_part]])
    high, low = split_pair(right)
    turn = 2.0 * np.pi / amount * index
    twiddle = np.stack([np.cos(turn), np.sin(turn)]).astype(np.float32)
    return high, low, np.ascontiguousarray(high.T), np.ascontiguousarray(low.T), twiddle


def class_tables(amount, classes):
    length = amount // classes
    index = np.arange(length)
    every = []
    for which in range(classes):
        turns = (which + classes * index[:, None]) * index[None, :] % amount
        angle = 2.0 * np.pi / amount * turns
        cos_part, sin_part = np.cos(angle), np.sin(angle)
        forward = np.block([[cos_part, sin_part], [-sin_part, cos_part]])
        every.append(np.stack([*split_pair(forward), *split_pair(forward.T)]))
    return np.stack(every).reshape(2, classes // 2, 4, 2 * length, 2 * length)


def split(value):
    high = value.astype(jnp.bfloat16)
    return high, (value - high.astype(jnp.float32)).astype(jnp.bfloat16)


def product(left, right, contract):
    dot = functools.partial(
        lax.dot_general,
        dimension_numbers=(contract, ((), ())),
        preferred_element_type=jnp.float32,
    )
    return dot(left[0], right[0]) + (dot(left[1], right[0]) + dot(left[0], right[1]))


def swap_halves(first, second):
    low = lax.broadcasted_iota(jnp.int32, first.shape, first.ndim - 1) < LANES // 2
    one = jnp.where(low, first, pltpu.roll(second, LANES // 2, first.ndim - 1))
    two = jnp.where(low, pltpu.roll(first, LANES // 2, first.ndim - 1), second)
    return one, two


def butterfly_in(real_part, imag_part, twiddle):
    half = real_part.shape[-1] // 2
    cos_row, sin_row = twiddle[0:1, :], twiddle[1:2, :]
    even = (real_part[:, :half] + real_part[:, half:], imag_part[:, :half] + imag_part[:, half:])
    real_gap = real_part[:, :half] - real_part[:, half:]
    imag_gap = imag_part[:, :half] - imag_part[:, half:]
    odd = (
        real_gap * cos_row + imag_gap * sin_row,
        imag_gap * cos_row - real_gap * sin_row,
    )
    return even, odd


def butterfly_out(even, odd, twiddle):
    cos_row, sin_row = twiddle[0:1, :], twiddle[1:2, :]
    real_turn = odd[0] * cos_row - odd[1] * sin_row
    imag_turn = odd[0] * sin_row + odd[1] * cos_row
    real_part = jnp.concatenate([even[0] + real_turn, even[0] - real_turn], 1)
    imag_part = jnp.concatenate([even[1] + imag_turn, even[1] - imag_turn], 1)
    return real_part, imag_part


ROOT_HALF = math.sqrt(0.5)


def turn_eighths(pair, which, sign):
    if which == 0:
        return pair
    low = lax.broadcasted_iota(jnp.int32, pair.shape, pair.ndim - 1) < LANES // 2
    other = pltpu.roll(pair, LANES // 2, pair.ndim - 1)
    crossed = jnp.where(low, other, -other) if sign < 0 else jnp.where(low, -other, other)
    if which == 2:
        return crossed
    return ROOT_HALF * (crossed + pair) if which == 1 else ROOT_HALF * (crossed - pair)


def fold_classes(real_parts, imag_parts):
    def plus(first, second):
        return tuple(parts[first] + parts[second] for parts in (real_parts, imag_parts))

    def minus(first, second):
        return tuple(parts[first] - parts[second] for parts in (real_parts, imag_parts))

    sum_even, sum_odd, gap_even, gap_odd = plus(0, 2), plus(1, 3), minus(0, 2), minus(1, 3)
    fours = [
        (sum_even[0] + sum_odd[0], sum_even[1] + sum_odd[1]),
        (gap_even[0] + gap_odd[1], gap_even[1] - gap_odd[0]),
        (sum_even[0] - sum_odd[0], sum_even[1] - sum_odd[1]),
        (gap_even[0] - gap_odd[1], gap_even[1] + gap_odd[0]),
    ]
    sides = []
    for which, (real_part, imag_part) in enumerate(fours):
        near, far = swap_halves(real_part, imag_part)
        far = turn_eighths(far, which, -1)
        sides.append((near + far, near - far))
    return sides


def unfold_classes(sides):
    fours = []
    for which, (first, second) in enumerate(sides):
        near, far = first + second, turn_eighths(first - second, which, 1)
        fours.append(swap_halves(near, far))
    sum_even = [fours[0][i] + fours[2][i] for i in range(2)]
    gap_even = [fours[0][i] - fours[2][i] for i in range(2)]
    sum_odd = [fours[1][i] + fours[3][i] for i in range(2)]
    gap_odd = [fours[1][i] - fours[3][i] for i in range(2)]
    return [
        (sum_even[0] + sum_odd[0], sum_even[1] + sum_odd[1]),
        (gap_even[0] - gap_odd[1], gap_even[1] + gap_odd[0]),
        (sum_even[0] - sum_odd[0], sum_even[1] - sum_odd[1]),
        (gap_even[0] + gap_odd[1], gap_even[1] - gap_odd[0]),
    ]


ORDER = (3, 2, 1)


def couple_kernel(
    lat_count, lay_count, planes, rows,
    layer_any, rate_any, toeplitz_any, hankel_any,
    field_any, contrast_any, fh_any, fl_any, ih_any, il_any, tables_any, twiddle_any,
    out_any,
    send_fold, recv_fold, send_in, recv_in, send_out, recv_mid, send_fin, recv_fin,
    field_x, spectrum, mixed, powers,
    field_ref, fh_ref, fl_ref, ih_ref, il_ref, tables_ref, twiddle_ref,
    layer_ref, rate_ref, toeplitz_ref, hankel_ref, out_ref, contrast_ref,
    fold_send, fold_recv, in_send, in_recv, out_send, out_recv, fin_send, fin_recv, load_sem, store_sem, second_sem, third_sem,
):
    inner = 2
    outer = lat_count // inner
    peers = inner * lay_count
    my_lat, my_lay = lax.axis_index("lat"), lax.axis_index("lay")
    my_outer = my_lat // inner
    my_peer = my_lat % inner * lay_count + my_lay
    lines, width_y = field_ref.shape[1:]
    width_x = rows * lat_count
    half_x = width_x // 2
    classes = 2 * outer
    length = width_y // classes
    depth = length // peers
    plane_total = planes * lay_count
    layer_count = rate_ref.shape[0]
    pairs = planes // 2

    def column(way):
        low = (my_outer % 2 + way % 2) % 2
        high = (my_outer // 2 + way // 2) % 2
        return 2 * high + low

    def column_id(way):
        return column(way) * inner + my_lat % inner, my_lay

    def peer(step):
        return (my_peer + step) % peers

    def peer_id(step):
        to = peer(step)
        return my_outer * inner + to // lay_count, to % lay_count

    def over_peers(act):
        def one(step, carry):
            act(step)
            return carry

        lax.fori_loop(1, peers, one, 0)

    chunk = LANES // 2
    cuts = (0, chunk, lines // 2, lines)
    spans = list(zip(cuts[:-1], cuts[1:]))
    chunks = len(spans)
    loads = [
        pltpu.make_async_copy(
            field_any.at[:, pl.ds(start, stop - start)],
            field_ref.at[:, pl.ds(start, stop - start)],
            load_sem.at[i],
        )
        for i, (start, stop) in enumerate(spans)
    ] + [
        pltpu.make_async_copy(source, target, load_sem.at[chunks + i])
        for i, (source, target) in enumerate(
            [
                (tables_any.at[0, my_outer], tables_ref.at[0]),
                (tables_any.at[1, my_outer], tables_ref.at[1]),
                (rate_any, rate_ref), (layer_any, layer_ref),
                (toeplitz_any, toeplitz_ref), (hankel_any, hankel_ref),
                (fh_any, fh_ref), (fl_any, fl_ref), (ih_any, ih_ref), (il_any, il_ref),
                (twiddle_any, twiddle_ref), (contrast_any, contrast_ref),
            ]
        )
    ]
    for load in loads[:chunks]:
        load.start()

    middle = (my_outer + 1) // 2 % 2
    stages = [pltpu.get_barrier_semaphore(), second_sem, third_sem]

    def tell(sem):
        bit = 1
        while bit < peers:
            pl.semaphore_signal(
                sem,
                inc=1,
                device_id=peer_id(bit - 2 * bit * (my_peer // bit % 2) + peers),
                device_id_type=MESH,
            )
            bit = 2 * bit
        pl.semaphore_signal(sem, inc=1, device_id=column_id(1), device_id_type=MESH)

        @pl.when(middle == 1)
        def _():
            pl.semaphore_signal(sem, inc=1, device_id=column_id(3), device_id_type=MESH)

    def hear(sem):
        pl.semaphore_wait(sem, peers.bit_length() + middle)

    tell(stages[0])

    def remote(source, target, sems, device):
        return pltpu.make_async_remote_copy(
            src_ref=source,
            dst_ref=target,
            send_sem=sems[0],
            recv_sem=sems[1],
            device_id=device,
            device_id_type=MESH,
        )

    def wait_bytes(view, sem):
        pltpu.make_async_copy(view, view, sem).wait()

    others, ways = pl.ds(0, peers - 1), pl.ds(0, outer - 1)

    def fold_copy(side, way, start, stop):
        where = pl.ds(start, stop - start)
        return remote(
            send_fold.at[column(way), side, where], recv_fold.at[my_outer, side, where],
            (fold_send, fold_recv.at[side, way]), column_id(way),
        )

    def in_copy(origin, side, step):
        return remote(
            send_in.at[peer(step), origin, side], recv_in.at[origin, my_peer, side],
            (in_send, in_recv.at[origin, side]), peer_id(step),
        )

    def out_copy(side, pair, step):
        return remote(
            send_out.at[peer(step), side, pair], recv_mid.at[my_peer, side, pair],
            (out_send, out_recv.at[side, pair]), peer_id(step),
        )

    def fin_copy(side, pair, half, way):
        where = pl.ds(half * chunk, chunk)
        return remote(
            send_fin.at[column(way), side, pair, where],
            recv_fin.at[my_outer, side, pair, where],
            (fin_send, fin_recv.at[pair, half]), column_id(way),
        )

    def fold(start, stop):
        for first in range(start, stop, chunk):
            where = slice(first, first + chunk)
            parts = [
                [field_ref[comp, where, t * LANES:(t + 1) * LANES] for t in range(outer)]
                for comp in range(2)
            ]
            for which, both in enumerate(fold_classes(*parts)):
                for side in range(2):
                    send_fold[which, side, where] = both[side]

    def send_folded(side, ways, some):
        for start, stop in some:
            for way in ways:
                fold_copy(side, way, start, stop).start()

    halves = [(0, lines // 2), (lines // 2, lines)]

    def of_both(inside, outside):
        for flag, sends in ((1, inside), (0, outside)):
            if sends:

                @pl.when(middle == flag)
                def _():
                    for side, way, some in sends:
                        send_folded(side, [way], some)

    def fold_next(i):
        loads[i].wait()
        fold(*spans[i])

    fold_next(0)
    hear(stages[0])
    tell(stages[1])
    of_both([(0, 3, spans[:1])], [(0, 1, spans[:1])])
    for load in loads[chunks:]:
        load.start()
    fold_next(1)
    of_both([(0, 3, spans[1:2])], [])
    hear(stages[1])
    tell(stages[2])
    of_both([(0, 2, spans[:2])], [(0, 2, spans[:2])])
    fold_next(2)
    of_both(
        [(0, 3, spans[2:]), (0, 2, spans[2:]), (0, 1, spans)]
        + [(1, way, halves) for way in (3, 1, 2)],
        [(0, 2, spans[2:])],
    )
    hear(stages[2])
    of_both([], [(0, 3, spans), (0, 1, spans[1:])])

    loads[chunks].wait()
    loads[chunks + 1].wait()

    def transform_y(source, origin, side):
        for start in range(0, lines, 2 * LANES):
            where = slice(start, start + 2 * LANES)
            right = split(source[origin, side, where])
            result = product((tables_ref[side, 0], tables_ref[side, 1]), right, ((1,), (1,)))
            for comp in range(2):
                piece = result[comp * length:(comp + 1) * length]
                send_in[:, origin, side, comp, :, where] = piece.reshape(peers, depth, 2 * LANES)
        over_peers(lambda step: in_copy(origin, side, step).start())
        recv_in[origin, my_peer, side] = send_in[my_peer, origin, side]

    for side in range(2):
        transform_y(send_fold, my_outer, side)
    loads[chunks + 2].wait()

    def signed(index, amount):
        index = jnp.where(index >= amount // 2, index - amount, index)
        return index.astype(jnp.float32) / (amount / 2)

    tile = (depth, width_x)
    place_x = lax.broadcasted_iota(jnp.int32, tile, 1)
    freq_x = signed(2 * (place_x % half_x) + place_x // half_x, width_x)
    for side in range(2):
        place_y = my_peer * depth + lax.broadcasted_iota(jnp.int32, tile, 0)
        freq_y = signed(classes * place_y + my_outer + outer * side, width_y)
        steepness = jnp.sqrt(1.0 + freq_x * freq_x + freq_y * freq_y)

        def one_layer(layer, carry):
            base = jnp.exp(steepness * (-rate_ref[layer] / (2 * plane_total)))

            def one_power(m, value):
                powers[side, layer, m] = value
                return value * base

            lax.fori_loop(0, 2 * plane_total - 1, one_power, jnp.ones(tile, jnp.float32))
            return carry

        lax.fori_loop(0, layer_count, one_layer, 0)

    for load in loads[chunks + 3:]:
        load.wait()

    def gather(side, way):
        wait_bytes(recv_fold.at[column(way), side], fold_recv.at[side, way])
        transform_y(recv_fold, column(way), side)

    early, late = 3 - middle, 2 + middle
    gather(0, early)
    gather(0, 1)
    gather(0, late)

    @pl.when(middle == 0)
    def _():
        for way in (1, 3, 2):
            send_folded(1, [way], halves)

    def load_lines(side):
        def one_lay(lay, carry):
            for pair in range(pairs):
                lanes = slice(pair * LANES, (pair + 1) * LANES)
                for block in range(outer):
                    first = recv_in[block, lay, side, :, :, lanes]
                    second = recv_in[block, lay_count + lay, side, :, :, lanes]
                    even, odd = swap_halves(first, second)
                    place = slice(block * LANES, (block + 1) * LANES)
                    field_x[:, lay * planes + 2 * pair, :, place] = even
                    field_x[:, lay * planes + 2 * pair + 1, :, place] = odd
            return carry

        lax.fori_loop(0, lay_count, one_lay, 0)

    group = min(plane_total, LANES // SUBLANES)

    def transform_x(step, carry):
        some = pl.ds(step * group, group)
        flat = (group * depth, width_x)
        halves = butterfly_in(
            field_x[0, some].reshape(flat), field_x[1, some].reshape(flat), twiddle_ref
        )
        for half, pair in enumerate(halves):
            left = split(jnp.concatenate(pair, 1))
            result = product(left, (fh_ref[...], fl_ref[...]), ((1,), (0,)))
            for comp in range(2):
                piece = result[:, comp * half_x:(comp + 1) * half_x]
                spectrum[comp, some, :, half * half_x:(half + 1) * half_x] = piece.reshape(
                    group, depth, half_x
                )
        return carry

    some_planes = 2 * lay_count

    def invert_x():
        halves = []
        for half in range(2):
            place = slice(half * half_x, (half + 1) * half_x)
            flat = (some_planes * depth, half_x)
            left = split(
                jnp.concatenate(
                    [mixed[comp, :, :, place].reshape(flat) for comp in range(2)], 1
                )
            )
            result = product(left, (ih_ref[...], il_ref[...]), ((1,), (0,)))
            halves.append((result[:, :half_x], result[:, half_x:]))
        real_part, imag_part = butterfly_out(halves[0], halves[1], twiddle_ref)
        full = (some_planes, depth, width_x)
        factor = 1.0 / (width_x * width_y)
        mixed[0] = (real_part * factor).reshape(full)
        mixed[1] = (imag_part * factor).reshape(full)

    def store_lines(side, pair):
        for lay in range(lay_count):
            for block in range(outer):
                place = slice(block * LANES, (block + 1) * LANES)
                even, odd = mixed[:, 2 * lay, :, place], mixed[:, 2 * lay + 1, :, place]
                first, second = swap_halves(even, odd)
                send_out[lay, side, pair, :, :, place] = first
                send_out[lay_count + lay, side, pair, :, :, place] = second

    def couple(side, pair):
        def one_plane(place, carry):
            plane = place // 2 * planes + 2 * pair + place % 2
            layer = layer_ref[plane]
            real_sum = jnp.zeros(tile, jnp.float32)
            imag_sum = jnp.zeros(tile, jnp.float32)
            for source in range(plane_total):
                offset = plane - source
                direct = powers[side, layer, 2 * jnp.abs(offset)]
                mirror = powers[side, layer, plane + source]
                at = offset + plane_total - 1
                kern_real = (
                    toeplitz_ref[0, layer, at] * direct
                    + hankel_ref[0, layer, plane + source] * mirror
                )
                kern_imag = (
                    toeplitz_ref[1, layer, at] * direct
                    + hankel_ref[1, layer, plane + source] * mirror
                )
                real_src, imag_src = spectrum[0, source], spectrum[1, source]
                real_sum += kern_real * real_src - kern_imag * imag_src
                imag_sum += kern_real * imag_src + kern_imag * real_src
            mixed[0, place] = real_sum
            mixed[1, place] = imag_sum
            return carry

        lax.fori_loop(0, some_planes, one_plane, 0)

    def invert_y(side, pair):
        wait_bytes(recv_mid.at[others, side, pair], out_recv.at[side, pair])
        stack = jnp.concatenate(
            [recv_mid[:, side, pair, comp].reshape(length, outer * LANES) for comp in range(2)], 0
        )
        result = product((tables_ref[side, 2], tables_ref[side, 3]), split(stack), ((1,), (0,)))
        for block in range(outer):
            send_fin[block, side, pair] = result[:, block * LANES:(block + 1) * LANES].T
        recv_fin[my_outer, side, pair] = send_fin[my_outer, side, pair]

    def send_final(side, pair):
        for half in range(2):
            for way in (early, late, 1):
                fin_copy(side, pair, half, way).start()

    for side in range(2):
        for origin in range(outer):
            wait_bytes(recv_in.at[origin, others, side], in_recv.at[origin, side])
        load_lines(side)
        lax.fori_loop(0, plane_total // group, transform_x, 0)

        def one_pair(pair, carry):
            couple(side, pair)
            invert_x()
            store_lines(side, pair)
            if side == 0:

                @pl.when(pair == pairs - 1)
                def _():
                    gather(1, 2)

            over_peers(lambda step: out_copy(side, pair, step).start())
            recv_mid[my_peer, side, pair] = send_out[my_peer, side, pair]

            if side == 0:

                @pl.when(pair == 1)
                def _():
                    gather(1, 1)

                @pl.when(pair == 2 - middle)
                def _():
                    gather(1, 3)

                @pl.when(pair >= 2)
                def _():
                    invert_y(0, pair - 2)

                    @pl.when(middle == 1)
                    def _():
                        send_final(0, pair - 2)

            else:

                @pl.when(pair == 0)
                def _():
                    invert_y(0, pairs - 1)
                    send_final(0, pairs - 1)

                @pl.when(pair >= 1)
                def _():
                    invert_y(1, pair - 1)
                    send_final(1, pair - 1)

            return carry

        lax.fori_loop(0, pairs, one_pair, 0)
        if side == 0:
            invert_y(0, pairs - 2)

            @pl.when(middle == 0)
            def _():
                for pair in range(pairs - 2):
                    send_final(0, pair)

            send_final(0, pairs - 2)
        else:
            invert_y(1, pairs - 1)
            send_final(1, pairs - 1)

    wait_bytes(send_fold.at[ways], fold_send)
    wait_bytes(send_in.at[others], in_send)
    wait_bytes(send_out.at[others], out_send)

    def finish(step, carry):
        pair, half = step // 2, step % 2
        inside = pl.ds(half * chunk, chunk)
        wait_bytes(recv_fin.at[ways, :, pair, inside], fin_recv.at[pair, half])
        where = pl.ds(step * chunk, chunk)
        sides = [
            (recv_fin[which, 0, pair, inside], recv_fin[which, 1, pair, inside])
            for which in range(outer)
        ]
        for t, (real_part, imag_part) in enumerate(unfold_classes(sides)):
            place = slice(t * LANES, (t + 1) * LANES)
            scale = contrast_ref[where, place]
            out_ref[0, where, place] = real_part * scale
            out_ref[1, where, place] = imag_part * scale
        pltpu.make_async_copy(out_ref.at[:, where], out_any.at[:, where], store_sem).start()
        return carry

    lax.fori_loop(0, 2 * pairs, finish, 0)
    wait_bytes(send_fin.at[ways], fin_send)
    wait_bytes(out_ref, store_sem)


def fast_body(wave_field, contrast, layer_of_plane, toeplitz_table, hankel_table, layer_rates):
    _, planes, rows, width_y = wave_field.shape
    lat_count, lay_count = lax.axis_size("lat"), lax.axis_size("lay")
    outer, peers = lat_count // 2, 2 * lay_count
    width_x = rows * lat_count
    depth = width_y // (2 * outer * peers)
    plane_total = planes * lay_count
    layer_count = layer_rates.shape[0]
    lines = planes * rows
    pairs = planes // 2
    fh, fl, ih, il, twiddle = (jnp.asarray(t) for t in split_tables(width_x))
    tables = jnp.asarray(class_tables(width_y, 2 * outer))
    operands = [
        layer_of_plane, layer_rates, toeplitz_table, hankel_table,
        wave_field.reshape(2, lines, width_y), contrast.reshape(lines, width_y), fh, fl, ih, il, tables, twiddle,
    ]
    folded = (outer, 2, lines, LANES)
    final = (outer, 2, pairs, LANES, LANES)
    tile_all = (2, plane_total, depth, width_x)
    dma = pltpu.SemaphoreType.DMA
    space = pl.pallas_call(
        functools.partial(couple_kernel, lat_count, lay_count, planes, rows),
        out_shape=jax.ShapeDtypeStruct((2, lines, width_y), jnp.float32),
        in_specs=[pl.BlockSpec(memory_space=pltpu.HBM)] * len(operands),
        out_specs=pl.BlockSpec(memory_space=pl.ANY),
        scratch_shapes=[
            pltpu.VMEM(folded, jnp.float32),
            pltpu.VMEM(folded, jnp.float32),
            pltpu.VMEM((peers, outer, 2, 2, depth, lines), jnp.float32),
            pltpu.VMEM((outer, peers, 2, 2, depth, lines), jnp.float32),
            pltpu.VMEM((peers, 2, pairs, 2, depth, outer * LANES), jnp.float32),
            pltpu.VMEM((peers, 2, pairs, 2, depth, outer * LANES), jnp.float32),
            pltpu.VMEM(final, jnp.float32),
            pltpu.VMEM(final, jnp.float32),
            pltpu.VMEM(tile_all, jnp.float32),
            pltpu.VMEM(tile_all, jnp.float32),
            pltpu.VMEM((2, 2 * lay_count, depth, width_x), jnp.float32),
            pltpu.VMEM((2, layer_count, 2 * plane_total - 1, depth, width_x), jnp.float32),
            pltpu.VMEM((2, lines, width_y), jnp.float32),
            pltpu.VMEM(fh.shape, fh.dtype),
            pltpu.VMEM(fl.shape, fl.dtype),
            pltpu.VMEM(ih.shape, ih.dtype),
            pltpu.VMEM(il.shape, il.dtype),
            pltpu.VMEM((2,) + tables.shape[2:], tables.dtype),
            pltpu.VMEM(twiddle.shape, twiddle.dtype),
            pltpu.SMEM(layer_of_plane.shape, layer_of_plane.dtype),
            pltpu.SMEM(layer_rates.shape, layer_rates.dtype),
            pltpu.SMEM(toeplitz_table.shape, toeplitz_table.dtype),
            pltpu.SMEM(hankel_table.shape, hankel_table.dtype),
            pltpu.VMEM((2, lines, width_y), jnp.float32),
            pltpu.VMEM((lines, width_y), jnp.float32),
            dma(()), dma((2, outer)),
            dma(()), dma((outer, 2)),
            dma(()), dma((2, pairs)),
            dma(()), dma((pairs, 2)),
            dma((15,)),
            dma(()),
            pltpu.SemaphoreType.REGULAR,
            pltpu.SemaphoreType.REGULAR,
        ],
        compiler_params=pltpu.CompilerParams(
            collective_id=0, has_side_effects=True, vmem_limit_bytes=48 * 1024 * 1024
        ),
        name="couple",
    )(*(pltpu.with_memory_space_constraint(value, pltpu.HBM) for value in operands))
    return space.reshape(wave_field.shape)


def body(wave_field, *others):
    _, planes, rows, width_y = wave_field.shape
    lat_count, lay_count = lax.axis_size("lat"), lax.axis_size("lay")
    outer, peers = lat_count // 2, 2 * lay_count
    width_x = rows * lat_count
    fits = (
        lat_count % 2 == 0
        and outer == 4
        and 2 * rows == LANES
        and planes % 2 == 0
        and planes >= 4
        and width_x == width_y
        and width_y == outer * LANES
        and width_y == 2 * outer * peers * SUBLANES
        and (planes * lay_count) % (LANES // SUBLANES) == 0
        and (planes * rows) % (2 * LANES) == 0
    )
    return (fast_body if fits else general_body)(wave_field, *others)


def solution(mesh):
    return jax.shard_map(
        body,
        mesh=mesh,
        in_specs=(P(None, "lay", "lat", None), P("lay", "lat", None), P(), P(), P(), P()),
        out_specs=P(None, "lay", "lat", None),
        check_vma=False,
    )
```

```python
import math

import functools

import jax
import jax.numpy as jnp
import numpy as np
from jax import lax
from jax.experimental import pallas as pl
from jax.experimental.pallas import tpu as pltpu
from jax.sharding import PartitionSpec as P

HIGHEST = lax.Precision.HIGHEST


def signed_of(index, amount):
    return jnp.where(index >= amount // 2, index - amount, index).astype(jnp.float32) / (amount / 2)


def phase_tables(rows, cols, amount, sign):
    index_row = lax.broadcasted_iota(jnp.int32, (rows, cols), 0)
    index_col = lax.broadcasted_iota(jnp.int32, (rows, cols), 1)
    angle = 2.0 * math.pi / amount * (index_row * index_col % amount).astype(jnp.float32)
    return (jnp.cos(angle), sign * jnp.sin(angle))


def complex_apply(real_part, imag_part, cos_table, sin_table, form):
    out_real = jnp.einsum(form, real_part, cos_table, precision=HIGHEST) - jnp.einsum(
        form, imag_part, sin_table, precision=HIGHEST
    )
    out_imag = jnp.einsum(form, real_part, sin_table, precision=HIGHEST) + jnp.einsum(
        form, imag_part, cos_table, precision=HIGHEST
    )
    return (out_real, out_imag)


def fourier_last(real_part, imag_part, sign, factor):
    amount = real_part.shape[-1]
    leading = real_part.shape[:-1]
    first = 1
    for divisor in range(1, math.isqrt(amount) + 1):
        if amount % divisor == 0:
            first = divisor
    second = amount // first
    flat_real = real_part.reshape(-1, second, first)
    flat_imag = imag_part.reshape(-1, second, first)
    cos_second, sin_second = phase_tables(second, second, second, sign)
    section_real, section_imag = complex_apply(
        flat_real, flat_imag, cos_second, sin_second, "pmn,mk->pkn"
    )
    twist_cos, twist_sin = phase_tables(second, first, amount, sign)
    turned_real = section_real * twist_cos - section_imag * twist_sin
    turned_imag = section_real * twist_sin + section_imag * twist_cos
    cos_first, sin_first = phase_tables(first, first, first, sign)
    final_real, final_imag = complex_apply(
        turned_real, turned_imag, cos_first, sin_first, "pkn,nj->pjk"
    )
    final_real = final_real.reshape(leading + (amount,)) * factor
    final_imag = final_imag.reshape(leading + (amount,)) * factor
    return (final_real, final_imag)


def pick_amplitudes(rows, index, width):
    positions = jnp.arange(width, dtype=jnp.int32)
    onehot = (index[:, :, None] == positions[None, None, :]).astype(jnp.float32)
    return jnp.einsum("pan,ain->pai", rows, onehot, precision=HIGHEST)


def general_body(wave_field, contrast, layer_of_plane, toeplitz_table, hankel_table, layer_rates):
    row_count = wave_field.shape[2]
    width_y = wave_field.shape[3]
    lat_count = lax.axis_size("lat")
    lay_count = lax.axis_size("lay")
    width_x = row_count * lat_count
    ky_band = width_y // lat_count
    table_width = toeplitz_table.shape[-1]
    plane_total = (table_width + 1) // 2
    layer_count = layer_rates.shape[0]
    spec_real, spec_imag = fourier_last(wave_field[0], wave_field[1], -1.0, 1.0)
    along_y = jnp.stack([spec_real, spec_imag], 2)
    freq_x = signed_of(jnp.arange(width_x, dtype=jnp.int32), width_x)
    ky_first = lax.axis_index("lat") * ky_band
    layer_ids = jnp.arange(layer_count, dtype=jnp.int32)

    def couple(z_out, z_in, source, ky_rows):
        onehot = (layer_of_plane[z_out][:, None] == layer_ids[None, :]).astype(jnp.float32)
        rate_out = jnp.dot(onehot, layer_rates, precision=HIGHEST)
        rows_toeplitz = jnp.einsum("al,pln->pan", onehot, toeplitz_table, precision=HIGHEST)
        rows_hankel = jnp.einsum("al,pln->pan", onehot, hankel_table, precision=HIGHEST)
        offset = z_out[:, None] - z_in[None, :]
        plane_sum = z_out[:, None] + z_in[None, :]
        amp_toeplitz = pick_amplitudes(rows_toeplitz, offset + plane_total - 1, table_width)
        amp_hankel = pick_amplitudes(rows_hankel, plane_sum, table_width)
        freq_y = signed_of(ky_rows, width_y)
        steepness = jnp.sqrt(1.0 + freq_y[:, None] ** 2 + freq_x[None, :] ** 2)
        scaled = rate_out[:, None, None, None] * steepness[None, None] / plane_total
        decay_toeplitz = jnp.exp(-scaled * jnp.abs(offset).astype(jnp.float32)[:, :, None, None])
        decay_hankel = jnp.exp(-scaled * (0.5 * plane_sum.astype(jnp.float32))[:, :, None, None])
        kern_real = (
            amp_toeplitz[0][:, :, None, None] * decay_toeplitz
            + amp_hankel[0][:, :, None, None] * decay_hankel
        )
        kern_imag = (
            amp_toeplitz[1][:, :, None, None] * decay_toeplitz
            + amp_hankel[1][:, :, None, None] * decay_hankel
        )
        real_src = source[None, :, 0]
        imag_src = source[None, :, 1]
        out_real = jnp.sum(kern_real * real_src - kern_imag * imag_src, axis=1)
        out_imag = jnp.sum(kern_real * imag_src + kern_imag * real_src, axis=1)
        return jnp.stack([out_real, out_imag], 1)

    narrow = ky_band // lay_count
    narrow_rows = ky_first + lax.axis_index("lay") * narrow + jnp.arange(narrow, dtype=jnp.int32)
    lines_in = lax.all_to_all(along_y, "lat", split_axis=3, concat_axis=1, tiled=True)
    line_real = jnp.transpose(lines_in[:, :, 0], (0, 2, 1))
    line_imag = jnp.transpose(lines_in[:, :, 1], (0, 2, 1))
    out_real, out_imag = fourier_last(line_real, line_imag, -1.0, 1.0)
    spectrum = jnp.stack([out_real, out_imag], 1)
    gathered = lax.all_to_all(spectrum, "lay", split_axis=2, concat_axis=0, tiled=True)
    all_planes = gathered.shape[0]
    every_plane = jnp.arange(all_planes, dtype=jnp.int32)
    block_size = math.gcd(all_planes, 8)

    def one_block(which):
        z_out = which * block_size + jnp.arange(block_size, dtype=jnp.int32)
        return couple(z_out, every_plane, gathered, narrow_rows)

    stacked = lax.map(one_block, jnp.arange(all_planes // block_size, dtype=jnp.int32))
    coupled = stacked.reshape(all_planes, 2, narrow_rows.shape[0], width_x)
    mixed = lax.all_to_all(coupled, "lay", split_axis=0, concat_axis=2, tiled=True)
    out_real, out_imag = fourier_last(mixed[:, 0], mixed[:, 1], 1.0, 1.0 / width_x)
    spatial_x = jnp.transpose(jnp.stack([out_real, out_imag], 1), (0, 3, 1, 2))
    lines = lax.all_to_all(spatial_x, "lat", split_axis=1, concat_axis=3, tiled=True)
    space_real, space_imag = fourier_last(lines[:, :, 0], lines[:, :, 1], 1.0, 1.0 / width_y)
    return jnp.stack([space_real, space_imag], 0) * contrast[None]


LANES = 128
SUBLANES = 8
MESH = pl.DeviceIdType.MESH


def split_pair(table):
    table = table.astype(np.float32)
    high = table.astype(jnp.bfloat16)
    return high, (table - high.astype(np.float32)).astype(jnp.bfloat16)


def split_tables(amount):
    half = amount // 2
    index = np.arange(half)
    angle = 2.0 * np.pi / half * (index[:, None] * index[None, :] % half)
    cos_part, sin_part = np.cos(angle), np.sin(angle)
    right = np.block([[cos_part, -sin_part], [sin_part, cos_part]])
    high, low = split_pair(right)
    turn = 2.0 * np.pi / amount * index
    twiddle = np.stack([np.cos(turn), np.sin(turn)]).astype(np.float32)
    return np.stack([high, low, high.T, low.T]), twiddle


def class_tables(amount, classes):
    length = amount // classes
    index = np.arange(length)
    every = []
    for which in range(classes):
        turns = (which + classes * index[:, None]) * index[None, :] % amount
        angle = 2.0 * np.pi / amount * turns
        cos_part, sin_part = np.cos(angle), np.sin(angle)
        forward = np.block([[cos_part, sin_part], [-sin_part, cos_part]])
        every.append(np.stack([*split_pair(forward), *split_pair(forward.T)]))
    every = np.stack(every).reshape(2, classes // 2, 4, 2 * length, 2 * length)
    return np.ascontiguousarray(every.swapaxes(0, 1))


def split(value):
    high = value.astype(jnp.bfloat16)
    return high, (value - high.astype(jnp.float32)).astype(jnp.bfloat16)


def product(left, right, contract):
    dot = functools.partial(
        lax.dot_general,
        dimension_numbers=(contract, ((), ())),
        preferred_element_type=jnp.float32,
    )
    return dot(left[0], right[0]) + (dot(left[1], right[0]) + dot(left[0], right[1]))


def swap_halves(first, second):
    low = lax.broadcasted_iota(jnp.int32, first.shape, first.ndim - 1) < LANES // 2
    one = jnp.where(low, first, pltpu.roll(second, LANES // 2, first.ndim - 1))
    two = jnp.where(low, pltpu.roll(first, LANES // 2, first.ndim - 1), second)
    return one, two


def butterfly_in(real_part, imag_part, twiddle):
    half = real_part.shape[-1] // 2
    cos_row, sin_row = twiddle[0:1, :], twiddle[1:2, :]
    even = (real_part[:, :half] + real_part[:, half:], imag_part[:, :half] + imag_part[:, half:])
    real_gap = real_part[:, :half] - real_part[:, half:]
    imag_gap = imag_part[:, :half] - imag_part[:, half:]
    odd = (
        real_gap * cos_row + imag_gap * sin_row,
        imag_gap * cos_row - real_gap * sin_row,
    )
    return even, odd


def butterfly_out(even, odd, twiddle):
    cos_row, sin_row = twiddle[0:1, :], twiddle[1:2, :]
    real_turn = odd[0] * cos_row - odd[1] * sin_row
    imag_turn = odd[0] * sin_row + odd[1] * cos_row
    real_part = jnp.concatenate([even[0] + real_turn, even[0] - real_turn], 1)
    imag_part = jnp.concatenate([even[1] + imag_turn, even[1] - imag_turn], 1)
    return real_part, imag_part


ROOT_HALF = math.sqrt(0.5)


def turn_eighths(pair, which, sign):
    if which == 0:
        return pair
    low = lax.broadcasted_iota(jnp.int32, pair.shape, pair.ndim - 1) < LANES // 2
    other = pltpu.roll(pair, LANES // 2, pair.ndim - 1)
    crossed = jnp.where(low, other, -other) if sign < 0 else jnp.where(low, -other, other)
    if which == 2:
        return crossed
    return ROOT_HALF * (crossed + pair) if which == 1 else ROOT_HALF * (crossed - pair)


def fold_classes(real_parts, imag_parts):
    def plus(first, second):
        return tuple(parts[first] + parts[second] for parts in (real_parts, imag_parts))

    def minus(first, second):
        return tuple(parts[first] - parts[second] for parts in (real_parts, imag_parts))

    sum_even, sum_odd, gap_even, gap_odd = plus(0, 2), plus(1, 3), minus(0, 2), minus(1, 3)
    fours = [
        (sum_even[0] + sum_odd[0], sum_even[1] + sum_odd[1]),
        (gap_even[0] + gap_odd[1], gap_even[1] - gap_odd[0]),
        (sum_even[0] - sum_odd[0], sum_even[1] - sum_odd[1]),
        (gap_even[0] - gap_odd[1], gap_even[1] + gap_odd[0]),
    ]
    sides = []
    for which, (real_part, imag_part) in enumerate(fours):
        near, far = swap_halves(real_part, imag_part)
        far = turn_eighths(far, which, -1)
        sides.append((near + far, near - far))
    return sides


def unfold_classes(sides):
    fours = []
    for which, (first, second) in enumerate(sides):
        near, far = first + second, turn_eighths(first - second, which, 1)
        fours.append(swap_halves(near, far))
    sum_even = [fours[0][i] + fours[2][i] for i in range(2)]
    gap_even = [fours[0][i] - fours[2][i] for i in range(2)]
    sum_odd = [fours[1][i] + fours[3][i] for i in range(2)]
    gap_odd = [fours[1][i] - fours[3][i] for i in range(2)]
    return [
        (sum_even[0] + sum_odd[0], sum_even[1] + sum_odd[1]),
        (gap_even[0] - gap_odd[1], gap_even[1] + gap_odd[0]),
        (sum_even[0] - sum_odd[0], sum_even[1] - sum_odd[1]),
        (gap_even[0] + gap_odd[1], gap_even[1] - gap_odd[0]),
    ]


ORDER = (3, 2, 1)


def couple_kernel(
    lat_count, lay_count, planes, rows,
    layer_any, rate_any, toeplitz_any, hankel_any,
    field_any, contrast_any, lines_any, tables_any, twiddle_any,
    out_ref,
    send_fold, recv_fold, send_in, recv_in, send_out, recv_mid, send_fin, recv_fin,
    field_x, spectrum, mixed, powers,
    field_ref, lines_ref, tables_ref, twiddle_ref,
    layer_ref, rate_ref, toeplitz_ref, hankel_ref, contrast_ref,
    fold_send, fold_recv, in_send, in_recv, out_send, out_recv, fin_send, fin_recv, load_sem, second_sem, third_sem,
):
    inner = 2
    outer = lat_count // inner
    peers = inner * lay_count
    my_lat, my_lay = lax.axis_index("lat"), lax.axis_index("lay")
    my_outer = my_lat // inner
    my_peer = my_lat % inner * lay_count + my_lay
    lines, width_y = field_ref.shape[1:]
    width_x = rows * lat_count
    half_x = width_x // 2
    classes = 2 * outer
    length = width_y // classes
    depth = length // peers
    plane_total = planes * lay_count
    layer_count = rate_ref.shape[0]
    pairs = planes // 2

    def column(way):
        low = (my_outer % 2 + way % 2) % 2
        high = (my_outer // 2 + way // 2) % 2
        return 2 * high + low

    def column_id(way):
        return column(way) * inner + my_lat % inner, my_lay

    def peer(step):
        return (my_peer + step) % peers

    def peer_id(step):
        to = peer(step)
        return my_outer * inner + to // lay_count, to % lay_count

    def over_peers(act):
        def one(step, carry):
            act(step)
            return carry

        lax.fori_loop(1, peers, one, 0)

    chunk = LANES // 2
    cuts = (0, 2 * chunk, lines // 2, lines)
    spans = list(zip(cuts[:-1], cuts[1:]))
    chunks = len(spans)
    loads = [
        pltpu.make_async_copy(
            field_any.at[:, pl.ds(start, stop - start)],
            field_ref.at[:, pl.ds(start, stop - start)],
            load_sem.at[i],
        )
        for i, (start, stop) in enumerate(spans)
    ] + [
        pltpu.make_async_copy(source, target, load_sem.at[chunks + i])
        for i, (source, target) in enumerate(
            [
                (tables_any.at[my_outer], tables_ref),
                (rate_any, rate_ref), (layer_any, layer_ref),
                (toeplitz_any, toeplitz_ref), (hankel_any, hankel_ref),
                (lines_any, lines_ref), (twiddle_any, twiddle_ref), (contrast_any, contrast_ref),
            ]
        )
    ]
    middle = (my_outer + 1) // 2 % 2
    stages = [pltpu.get_barrier_semaphore(), second_sem, third_sem]

    def tell(sem):
        bit = 1
        while bit < peers:
            pl.semaphore_signal(
                sem,
                inc=1,
                device_id=peer_id(bit - 2 * bit * (my_peer // bit % 2) + peers),
                device_id_type=MESH,
            )
            bit = 2 * bit
        pl.semaphore_signal(sem, inc=1, device_id=column_id(1), device_id_type=MESH)

        @pl.when(middle == 1)
        def _():
            pl.semaphore_signal(sem, inc=1, device_id=column_id(3), device_id_type=MESH)

    def hear(sem):
        pl.semaphore_wait(sem, peers.bit_length() + middle)

    tell(stages[0])
    for load in loads[:chunks]:
        load.start()

    def remote(source, target, sems, device):
        return pltpu.make_async_remote_copy(
            src_ref=source,
            dst_ref=target,
            send_sem=sems[0],
            recv_sem=sems[1],
            device_id=device,
            device_id_type=MESH,
        )

    def wait_bytes(view, sem):
        pltpu.make_async_copy(view, view, sem).wait()

    others, ways = pl.ds(0, peers - 1), pl.ds(0, outer - 1)

    def fold_copy(side, way, start, stop):
        where = pl.ds(start, stop - start)
        return remote(
            send_fold.at[column(way), side, where], recv_fold.at[my_outer, side, where],
            (fold_send, fold_recv.at[side, way - 1]), column_id(way),
        )

    def in_copy(origin, side, step):
        return remote(
            send_in.at[peer(step), origin, side], recv_in.at[origin, my_peer, side],
            (in_send, in_recv.at[side]), peer_id(step),
        )

    def out_copy(side, pair, step):
        return remote(
            send_out.at[peer(step), side, pair], recv_mid.at[my_peer, side, pair],
            (out_send, out_recv.at[side, pair]), peer_id(step),
        )

    def fin_copy(side, pair, start, stop, sem, way):
        where = pl.ds(start, stop - start)
        return remote(
            send_fin.at[column(way), side, pair, where],
            recv_fin.at[my_outer, side, pair, where],
            (fin_send, sem), column_id(way),
        )

    def fold(start, stop):
        for first in range(start, stop, chunk):
            where = slice(first, first + chunk)
            parts = [
                [field_ref[comp, where, t * LANES:(t + 1) * LANES] for t in range(outer)]
                for comp in range(2)
            ]
            for which, both in enumerate(fold_classes(*parts)):
                for side in range(2):
                    send_fold[which, side, where] = both[side]

    def send_folded(side, ways, some):
        for start, stop in some:
            for way in ways:
                fold_copy(side, way, start, stop).start()

    whole = [(0, lines)]

    def of_both(inside, outside):
        for flag, sends in ((1, inside), (0, outside)):
            if sends:

                @pl.when(middle == flag)
                def _():
                    for side, way, some in sends:
                        send_folded(side, [way], some)

    def fold_next(i):
        loads[i].wait()
        fold(*spans[i])

    fold_next(0)
    hear(stages[0])
    tell(stages[1])
    of_both([(0, 3, spans[:1])], [(0, 1, spans[:1])])
    for load in loads[chunks:]:
        load.start()
    fold_next(1)
    of_both([(0, 3, spans[1:2])], [])
    hear(stages[1])
    tell(stages[2])
    of_both([(0, 2, spans[:2])], [(0, 2, spans[:2])])
    fold_next(2)
    of_both(
        [(0, 3, spans[2:]), (0, 2, spans[2:]), (0, 1, spans)]
        + [(1, way, whole) for way in (3, 1, 2)],
        [(0, 2, spans[2:])],
    )
    hear(stages[2])
    of_both([], [(0, 3, spans), (0, 1, spans[1:])])

    loads[chunks].wait()

    def transform_y(source, origin, side):
        for start in range(0, lines, 2 * LANES):
            where = slice(start, start + 2 * LANES)
            right = split(source[origin, side, where])
            result = product((tables_ref[side, 0], tables_ref[side, 1]), right, ((1,), (1,)))
            for comp in range(2):
                piece = result[comp * length:(comp + 1) * length]
                send_in[:, origin, side, comp, :, where] = piece.reshape(peers, depth, 2 * LANES)
        over_peers(lambda step: in_copy(origin, side, step).start())
        recv_in[origin, my_peer, side] = send_in[my_peer, origin, side]

    for side in range(2):
        transform_y(send_fold, my_outer, side)
    loads[chunks + 1].wait()

    def signed(index, amount):
        index = jnp.where(index >= amount // 2, index - amount, index)
        return index.astype(jnp.float32) / (amount / 2)

    tile = (depth, width_x)
    place_x = lax.broadcasted_iota(jnp.int32, tile, 1)
    freq_x = signed(2 * (place_x % half_x) + place_x // half_x, width_x)
    for side in range(2):
        place_y = my_peer * depth + lax.broadcasted_iota(jnp.int32, tile, 0)
        freq_y = signed(classes * place_y + my_outer + outer * side, width_y)
        steepness = jnp.sqrt(1.0 + freq_x * freq_x + freq_y * freq_y)

        def one_layer(layer, carry):
            base = jnp.exp(steepness * (-rate_ref[layer] / (2 * plane_total)))

            def one_power(m, value):
                powers[side, layer, m] = value
                return value * base

            lax.fori_loop(0, 2 * plane_total - 1, one_power, jnp.ones(tile, jnp.float32))
            return carry

        lax.fori_loop(0, layer_count, one_layer, 0)

    for load in loads[chunks + 2:]:
        load.wait()

    def gather(side, way):
        wait_bytes(recv_fold.at[column(way), side], fold_recv.at[side, way - 1])
        transform_y(recv_fold, column(way), side)

    early, late = 3 - middle, 2 + middle
    gather(0, early)
    gather(0, 1)
    gather(0, late)

    @pl.when(middle == 0)
    def _():
        for way in (1, 3, 2):
            send_folded(1, [way], whole)

    def load_lines(side):
        def one_lay(lay, carry):
            for pair in range(pairs):
                lanes = slice(pair * LANES, (pair + 1) * LANES)
                for block in range(outer):
                    first = recv_in[block, lay, side, :, :, lanes]
                    second = recv_in[block, lay_count + lay, side, :, :, lanes]
                    even, odd = swap_halves(first, second)
                    place = slice(block * LANES, (block + 1) * LANES)
                    field_x[:, lay * planes + 2 * pair, :, place] = even
                    field_x[:, lay * planes + 2 * pair + 1, :, place] = odd
            return carry

        lax.fori_loop(0, lay_count, one_lay, 0)

    group = min(plane_total, LANES // SUBLANES)

    def transform_x(step, carry):
        some = pl.ds(step * group, group)
        flat = (group * depth, width_x)
        halves = butterfly_in(
            field_x[0, some].reshape(flat), field_x[1, some].reshape(flat), twiddle_ref
        )
        for half, pair in enumerate(halves):
            left = split(jnp.concatenate(pair, 1))
            result = product(left, (lines_ref[0], lines_ref[1]), ((1,), (0,)))
            for comp in range(2):
                piece = result[:, comp * half_x:(comp + 1) * half_x]
                spectrum[comp, some, :, half * half_x:(half + 1) * half_x] = piece.reshape(
                    group, depth, half_x
                )
        return carry

    some_planes = 2 * lay_count

    def invert_x():
        halves = []
        for half in range(2):
            place = slice(half * half_x, (half + 1) * half_x)
            flat = (some_planes * depth, half_x)
            left = split(
                jnp.concatenate(
                    [mixed[comp, :, :, place].reshape(flat) for comp in range(2)], 1
                )
            )
            result = product(left, (lines_ref[2], lines_ref[3]), ((1,), (0,)))
            halves.append((result[:, :half_x], result[:, half_x:]))
        real_part, imag_part = butterfly_out(halves[0], halves[1], twiddle_ref)
        full = (some_planes, depth, width_x)
        factor = 1.0 / (width_x * width_y)
        mixed[0] = (real_part * factor).reshape(full)
        mixed[1] = (imag_part * factor).reshape(full)

    def store_lines(side, pair):
        for lay in range(lay_count):
            for block in range(outer):
                place = slice(block * LANES, (block + 1) * LANES)
                even, odd = mixed[:, 2 * lay, :, place], mixed[:, 2 * lay + 1, :, place]
                first, second = swap_halves(even, odd)
                send_out[lay, side, pair, :, :, place] = first
                send_out[lay_count + lay, side, pair, :, :, place] = second

    def couple(side, pair):
        def one_plane(place, carry):
            plane = place // 2 * planes + 2 * pair + place % 2
            layer = layer_ref[plane]
            real_sum = jnp.zeros(tile, jnp.float32)
            imag_sum = jnp.zeros(tile, jnp.float32)
            for source in range(plane_total):
                offset = plane - source
                direct = powers[side, layer, 2 * jnp.abs(offset)]
                mirror = powers[side, layer, plane + source]
                at = offset + plane_total - 1
                kern_real = (
                    toeplitz_ref[0, layer, at] * direct
                    + hankel_ref[0, layer, plane + source] * mirror
                )
                kern_imag = (
                    toeplitz_ref[1, layer, at] * direct
                    + hankel_ref[1, layer, plane + source] * mirror
                )
                real_src, imag_src = spectrum[0, source], spectrum[1, source]
                real_sum += kern_real * real_src - kern_imag * imag_src
                imag_sum += kern_real * imag_src + kern_imag * real_src
            mixed[0, place] = real_sum
            mixed[1, place] = imag_sum
            return carry

        lax.fori_loop(0, some_planes, one_plane, 0)

    def invert_y(side, pair):
        wait_bytes(recv_mid.at[others, side, pair], out_recv.at[side, pair])
        stack = jnp.concatenate(
            [recv_mid[:, side, pair, comp].reshape(length, outer * LANES) for comp in range(2)], 0
        )
        result = product((tables_ref[side, 2], tables_ref[side, 3]), split(stack), ((1,), (0,)))
        for block in range(outer):
            send_fin[block, side, pair] = result[:, block * LANES:(block + 1) * LANES].T
        recv_fin[my_outer, side, pair] = send_fin[my_outer, side, pair]

    def send_final(side, pair):
        for way in (early, late, 1):
            fin_copy(side, pair, 0, LANES, fin_recv.at[side, pair], way).start()

    ends = [(0, chunk, fin_recv.at[1, pairs - 1]), (chunk, LANES, fin_recv.at[2, 0])]

    for side in range(2):
        wait_bytes(recv_in.at[:, others, side], in_recv.at[side])
        load_lines(side)
        lax.fori_loop(0, plane_total // group, transform_x, 0)

        def one_pair(pair, carry):
            couple(side, pair)
            invert_x()
            store_lines(side, pair)
            if side == 0:

                @pl.when(pair == pairs - 1)
                def _():
                    gather(1, 2)

            over_peers(lambda step: out_copy(side, pair, step).start())
            recv_mid[my_peer, side, pair] = send_out[my_peer, side, pair]

            if side == 0:

                @pl.when(pair == 1)
                def _():
                    gather(1, 1)

                @pl.when(pair == 2 - middle)
                def _():
                    gather(1, 3)

                @pl.when(pair >= 2)
                def _():
                    invert_y(0, pair - 2)

                    @pl.when(middle == 1)
                    def _():
                        send_final(0, pair - 2)

            else:

                @pl.when(pair == 0)
                def _():
                    invert_y(0, pairs - 1)
                    send_final(0, pairs - 1)

                @pl.when(pair >= 1)
                def _():
                    invert_y(1, pair - 1)
                    send_final(1, pair - 1)

            return carry

        lax.fori_loop(0, pairs, one_pair, 0)
        if side == 0:
            invert_y(0, pairs - 2)

            @pl.when(middle == 0)
            def _():
                for pair in range(pairs - 2):
                    send_final(0, pair)

            send_final(0, pairs - 2)
        else:
            invert_y(1, pairs - 1)
            for start, stop, sem in ends:
                for way in (early, late, 1):
                    fin_copy(1, pairs - 1, start, stop, sem, way).start()

    wait_bytes(send_fold.at[ways], fold_send)
    wait_bytes(send_in.at[others], in_send)
    wait_bytes(send_out.at[others], out_send)

    def finish(pair, start, stop):
        inside = pl.ds(start, stop - start)
        where = pl.ds(pair * LANES + start, stop - start)
        sides = [
            (recv_fin[which, 0, pair, inside], recv_fin[which, 1, pair, inside])
            for which in range(outer)
        ]
        for t, (real_part, imag_part) in enumerate(unfold_classes(sides)):
            place = slice(t * LANES, (t + 1) * LANES)
            scale = contrast_ref[where, place]
            out_ref[0, where, place] = real_part * scale
            out_ref[1, where, place] = imag_part * scale

    def finish_pair(pair, carry):
        for side in range(2):
            wait_bytes(recv_fin.at[ways, side, pair], fin_recv.at[side, pair])
        for start in range(0, LANES, chunk):
            finish(pair, start, start + chunk)
        return carry

    lax.fori_loop(0, pairs - 1, finish_pair, 0)
    wait_bytes(recv_fin.at[ways, 0, pairs - 1], fin_recv.at[0, pairs - 1])
    for start, stop, sem in ends:
        wait_bytes(recv_fin.at[ways, 1, pairs - 1, pl.ds(start, stop - start)], sem)
        finish(pairs - 1, start, stop)
    wait_bytes(send_fin.at[ways], fin_send)


def fast_body(wave_field, contrast, layer_of_plane, toeplitz_table, hankel_table, layer_rates):
    _, planes, rows, width_y = wave_field.shape
    lat_count, lay_count = lax.axis_size("lat"), lax.axis_size("lay")
    outer, peers = lat_count // 2, 2 * lay_count
    width_x = rows * lat_count
    depth = width_y // (2 * outer * peers)
    plane_total = planes * lay_count
    layer_count = layer_rates.shape[0]
    lines = planes * rows
    pairs = planes // 2
    line_tables, twiddle = (jnp.asarray(t) for t in split_tables(width_x))
    tables = jnp.asarray(class_tables(width_y, 2 * outer))
    operands = [
        layer_of_plane, layer_rates, toeplitz_table, hankel_table,
        wave_field.reshape(2, lines, width_y), contrast.reshape(lines, width_y), line_tables, tables, twiddle,
    ]
    folded = (outer, 2, lines, LANES)
    final = (outer, 2, pairs, LANES, LANES)
    tile_all = (2, plane_total, depth, width_x)
    dma = pltpu.SemaphoreType.DMA
    space = pl.pallas_call(
        functools.partial(couple_kernel, lat_count, lay_count, planes, rows),
        out_shape=jax.ShapeDtypeStruct((2, lines, width_y), jnp.float32),
        in_specs=[pl.BlockSpec(memory_space=pltpu.HBM)] * len(operands),
        out_specs=pl.BlockSpec(memory_space=pltpu.VMEM),
        scratch_shapes=[
            pltpu.VMEM(folded, jnp.float32),
            pltpu.VMEM(folded, jnp.float32),
            pltpu.VMEM((peers, outer, 2, 2, depth, lines), jnp.float32),
            pltpu.VMEM((outer, peers, 2, 2, depth, lines), jnp.float32),
            pltpu.VMEM((peers, 2, pairs, 2, depth, outer * LANES), jnp.float32),
            pltpu.VMEM((peers, 2, pairs, 2, depth, outer * LANES), jnp.float32),
            pltpu.VMEM(final, jnp.float32),
            pltpu.VMEM(final, jnp.float32),
            pltpu.VMEM(tile_all, jnp.float32),
            pltpu.VMEM(tile_all, jnp.float32),
            pltpu.VMEM((2, 2 * lay_count, depth, width_x), jnp.float32),
            pltpu.VMEM((2, layer_count, 2 * plane_total - 1, depth, width_x), jnp.float32),
            pltpu.VMEM((2, lines, width_y), jnp.float32),
            pltpu.VMEM(line_tables.shape, line_tables.dtype),
            pltpu.VMEM(tables.shape[1:], tables.dtype),
            pltpu.VMEM(twiddle.shape, twiddle.dtype),
            pltpu.SMEM(layer_of_plane.shape, layer_of_plane.dtype),
            pltpu.SMEM(layer_rates.shape, layer_rates.dtype),
            pltpu.SMEM(toeplitz_table.shape, toeplitz_table.dtype),
            pltpu.SMEM(hankel_table.shape, hankel_table.dtype),
            pltpu.VMEM((lines, width_y), jnp.float32),
            dma(()), dma((2, outer - 1)),
            dma(()), dma((2,)),
            dma(()), dma((2, pairs)),
            dma(()), dma((3, pairs)),
            dma((11,)),
            pltpu.SemaphoreType.REGULAR,
            pltpu.SemaphoreType.REGULAR,
        ],
        compiler_params=pltpu.CompilerParams(
            collective_id=0, has_side_effects=True, vmem_limit_bytes=48 * 1024 * 1024
        ),
        name="couple",
    )(*(pltpu.with_memory_space_constraint(value, pltpu.HBM) for value in operands))
    return space.reshape(wave_field.shape)


def body(wave_field, *others):
    _, planes, rows, width_y = wave_field.shape
    lat_count, lay_count = lax.axis_size("lat"), lax.axis_size("lay")
    outer, peers = lat_count // 2, 2 * lay_count
    width_x = rows * lat_count
    fits = (
        lat_count % 2 == 0
        and outer == 4
        and 2 * rows == LANES
        and planes % 2 == 0
        and planes >= 4
        and width_x == width_y
        and width_y == outer * LANES
        and width_y == 2 * outer * peers * SUBLANES
        and (planes * lay_count) % (LANES // SUBLANES) == 0
        and (planes * rows) % (2 * LANES) == 0
    )
    return (fast_body if fits else general_body)(wave_field, *others)


def solution(mesh):
    return jax.shard_map(
        body,
        mesh=mesh,
        in_specs=(P(None, "lay", "lat", None), P("lay", "lat", None), P(), P(), P(), P()),
        out_specs=P(None, "lay", "lat", None),
        check_vma=False,
    )
```

```python
import math

import functools

import jax
import jax.numpy as jnp
import numpy as np
from jax import lax
from jax.experimental import pallas as pl
from jax.experimental.pallas import tpu as pltpu
from jax.sharding import PartitionSpec as P

HIGHEST = lax.Precision.HIGHEST


def signed_of(index, amount):
    return jnp.where(index >= amount // 2, index - amount, index).astype(jnp.float32) / (amount / 2)


def phase_tables(rows, cols, amount, sign):
    index_row = lax.broadcasted_iota(jnp.int32, (rows, cols), 0)
    index_col = lax.broadcasted_iota(jnp.int32, (rows, cols), 1)
    angle = 2.0 * math.pi / amount * (index_row * index_col % amount).astype(jnp.float32)
    return (jnp.cos(angle), sign * jnp.sin(angle))


def complex_apply(real_part, imag_part, cos_table, sin_table, form):
    out_real = jnp.einsum(form, real_part, cos_table, precision=HIGHEST) - jnp.einsum(
        form, imag_part, sin_table, precision=HIGHEST
    )
    out_imag = jnp.einsum(form, real_part, sin_table, precision=HIGHEST) + jnp.einsum(
        form, imag_part, cos_table, precision=HIGHEST
    )
    return (out_real, out_imag)


def fourier_last(real_part, imag_part, sign, factor):
    amount = real_part.shape[-1]
    leading = real_part.shape[:-1]
    first = 1
    for divisor in range(1, math.isqrt(amount) + 1):
        if amount % divisor == 0:
            first = divisor
    second = amount // first
    flat_real = real_part.reshape(-1, second, first)
    flat_imag = imag_part.reshape(-1, second, first)
    cos_second, sin_second = phase_tables(second, second, second, sign)
    section_real, section_imag = complex_apply(
        flat_real, flat_imag, cos_second, sin_second, "pmn,mk->pkn"
    )
    twist_cos, twist_sin = phase_tables(second, first, amount, sign)
    turned_real = section_real * twist_cos - section_imag * twist_sin
    turned_imag = section_real * twist_sin + section_imag * twist_cos
    cos_first, sin_first = phase_tables(first, first, first, sign)
    final_real, final_imag = complex_apply(
        turned_real, turned_imag, cos_first, sin_first, "pkn,nj->pjk"
    )
    final_real = final_real.reshape(leading + (amount,)) * factor
    final_imag = final_imag.reshape(leading + (amount,)) * factor
    return (final_real, final_imag)


def pick_amplitudes(rows, index, width):
    positions = jnp.arange(width, dtype=jnp.int32)
    onehot = (index[:, :, None] == positions[None, None, :]).astype(jnp.float32)
    return jnp.einsum("pan,ain->pai", rows, onehot, precision=HIGHEST)


def general_body(wave_field, contrast, layer_of_plane, toeplitz_table, hankel_table, layer_rates):
    row_count = wave_field.shape[2]
    width_y = wave_field.shape[3]
    lat_count = lax.axis_size("lat")
    lay_count = lax.axis_size("lay")
    width_x = row_count * lat_count
    ky_band = width_y // lat_count
    table_width = toeplitz_table.shape[-1]
    plane_total = (table_width + 1) // 2
    layer_count = layer_rates.shape[0]
    spec_real, spec_imag = fourier_last(wave_field[0], wave_field[1], -1.0, 1.0)
    along_y = jnp.stack([spec_real, spec_imag], 2)
    freq_x = signed_of(jnp.arange(width_x, dtype=jnp.int32), width_x)
    ky_first = lax.axis_index("lat") * ky_band
    layer_ids = jnp.arange(layer_count, dtype=jnp.int32)

    def couple(z_out, z_in, source, ky_rows):
        onehot = (layer_of_plane[z_out][:, None] == layer_ids[None, :]).astype(jnp.float32)
        rate_out = jnp.dot(onehot, layer_rates, precision=HIGHEST)
        rows_toeplitz = jnp.einsum("al,pln->pan", onehot, toeplitz_table, precision=HIGHEST)
        rows_hankel = jnp.einsum("al,pln->pan", onehot, hankel_table, precision=HIGHEST)
        offset = z_out[:, None] - z_in[None, :]
        plane_sum = z_out[:, None] + z_in[None, :]
        amp_toeplitz = pick_amplitudes(rows_toeplitz, offset + plane_total - 1, table_width)
        amp_hankel = pick_amplitudes(rows_hankel, plane_sum, table_width)
        freq_y = signed_of(ky_rows, width_y)
        steepness = jnp.sqrt(1.0 + freq_y[:, None] ** 2 + freq_x[None, :] ** 2)
        scaled = rate_out[:, None, None, None] * steepness[None, None] / plane_total
        decay_toeplitz = jnp.exp(-scaled * jnp.abs(offset).astype(jnp.float32)[:, :, None, None])
        decay_hankel = jnp.exp(-scaled * (0.5 * plane_sum.astype(jnp.float32))[:, :, None, None])
        kern_real = (
            amp_toeplitz[0][:, :, None, None] * decay_toeplitz
            + amp_hankel[0][:, :, None, None] * decay_hankel
        )
        kern_imag = (
            amp_toeplitz[1][:, :, None, None] * decay_toeplitz
            + amp_hankel[1][:, :, None, None] * decay_hankel
        )
        real_src = source[None, :, 0]
        imag_src = source[None, :, 1]
        out_real = jnp.sum(kern_real * real_src - kern_imag * imag_src, axis=1)
        out_imag = jnp.sum(kern_real * imag_src + kern_imag * real_src, axis=1)
        return jnp.stack([out_real, out_imag], 1)

    narrow = ky_band // lay_count
    narrow_rows = ky_first + lax.axis_index("lay") * narrow + jnp.arange(narrow, dtype=jnp.int32)
    lines_in = lax.all_to_all(along_y, "lat", split_axis=3, concat_axis=1, tiled=True)
    line_real = jnp.transpose(lines_in[:, :, 0], (0, 2, 1))
    line_imag = jnp.transpose(lines_in[:, :, 1], (0, 2, 1))
    out_real, out_imag = fourier_last(line_real, line_imag, -1.0, 1.0)
    spectrum = jnp.stack([out_real, out_imag], 1)
    gathered = lax.all_to_all(spectrum, "lay", split_axis=2, concat_axis=0, tiled=True)
    all_planes = gathered.shape[0]
    every_plane = jnp.arange(all_planes, dtype=jnp.int32)
    block_size = math.gcd(all_planes, 8)

    def one_block(which):
        z_out = which * block_size + jnp.arange(block_size, dtype=jnp.int32)
        return couple(z_out, every_plane, gathered, narrow_rows)

    stacked = lax.map(one_block, jnp.arange(all_planes // block_size, dtype=jnp.int32))
    coupled = stacked.reshape(all_planes, 2, narrow_rows.shape[0], width_x)
    mixed = lax.all_to_all(coupled, "lay", split_axis=0, concat_axis=2, tiled=True)
    out_real, out_imag = fourier_last(mixed[:, 0], mixed[:, 1], 1.0, 1.0 / width_x)
    spatial_x = jnp.transpose(jnp.stack([out_real, out_imag], 1), (0, 3, 1, 2))
    lines = lax.all_to_all(spatial_x, "lat", split_axis=1, concat_axis=3, tiled=True)
    space_real, space_imag = fourier_last(lines[:, :, 0], lines[:, :, 1], 1.0, 1.0 / width_y)
    return jnp.stack([space_real, space_imag], 0) * contrast[None]


LANES = 128
SUBLANES = 8
MESH = pl.DeviceIdType.MESH


def split_pair(table):
    table = table.astype(np.float32)
    high = table.astype(jnp.bfloat16)
    return high, (table - high.astype(np.float32)).astype(jnp.bfloat16)


def split_tables(amount):
    half = amount // 2
    index = np.arange(half)
    angle = 2.0 * np.pi / half * (index[:, None] * index[None, :] % half)
    cos_part, sin_part = np.cos(angle), np.sin(angle)
    right = np.block([[cos_part, -sin_part], [sin_part, cos_part]])
    high, low = split_pair(right)
    turn = 2.0 * np.pi / amount * index
    twiddle = np.stack([np.cos(turn), np.sin(turn)]).astype(np.float32)
    return np.stack([high, low, high.T, low.T]), twiddle


def class_tables(amount, classes):
    length = amount // classes
    index = np.arange(length)
    every = []
    for which in range(classes):
        turns = (which + classes * index[:, None]) * index[None, :] % amount
        angle = 2.0 * np.pi / amount * turns
        cos_part, sin_part = np.cos(angle), np.sin(angle)
        forward = np.block([[cos_part, sin_part], [-sin_part, cos_part]])
        every.append(np.stack([*split_pair(forward), *split_pair(forward.T)]))
    every = np.stack(every).reshape(2, classes // 2, 4, 2 * length, 2 * length)
    return np.ascontiguousarray(every.swapaxes(0, 1))


def split(value):
    high = value.astype(jnp.bfloat16)
    return high, (value - high.astype(jnp.float32)).astype(jnp.bfloat16)


def product(left, right, contract):
    dot = functools.partial(
        lax.dot_general,
        dimension_numbers=(contract, ((), ())),
        preferred_element_type=jnp.float32,
    )
    return dot(left[0], right[0]) + (dot(left[1], right[0]) + dot(left[0], right[1]))


def swap_halves(first, second):
    low = lax.broadcasted_iota(jnp.int32, first.shape, first.ndim - 1) < LANES // 2
    one = jnp.where(low, first, pltpu.roll(second, LANES // 2, first.ndim - 1))
    two = jnp.where(low, pltpu.roll(first, LANES // 2, first.ndim - 1), second)
    return one, two


def butterfly_in(real_part, imag_part, twiddle):
    half = real_part.shape[-1] // 2
    cos_row, sin_row = twiddle[0:1, :], twiddle[1:2, :]
    even = (real_part[:, :half] + real_part[:, half:], imag_part[:, :half] + imag_part[:, half:])
    real_gap = real_part[:, :half] - real_part[:, half:]
    imag_gap = imag_part[:, :half] - imag_part[:, half:]
    odd = (
        real_gap * cos_row + imag_gap * sin_row,
        imag_gap * cos_row - real_gap * sin_row,
    )
    return even, odd


def butterfly_out(even, odd, twiddle):
    cos_row, sin_row = twiddle[0:1, :], twiddle[1:2, :]
    real_turn = odd[0] * cos_row - odd[1] * sin_row
    imag_turn = odd[0] * sin_row + odd[1] * cos_row
    real_part = jnp.concatenate([even[0] + real_turn, even[0] - real_turn], 1)
    imag_part = jnp.concatenate([even[1] + imag_turn, even[1] - imag_turn], 1)
    return real_part, imag_part


ROOT_HALF = math.sqrt(0.5)


def turn_eighths(pair, which, sign):
    if which == 0:
        return pair
    low = lax.broadcasted_iota(jnp.int32, pair.shape, pair.ndim - 1) < LANES // 2
    other = pltpu.roll(pair, LANES // 2, pair.ndim - 1)
    crossed = jnp.where(low, other, -other) if sign < 0 else jnp.where(low, -other, other)
    if which == 2:
        return crossed
    return ROOT_HALF * (crossed + pair) if which == 1 else ROOT_HALF * (crossed - pair)


def fold_classes(real_parts, imag_parts):
    def plus(first, second):
        return tuple(parts[first] + parts[second] for parts in (real_parts, imag_parts))

    def minus(first, second):
        return tuple(parts[first] - parts[second] for parts in (real_parts, imag_parts))

    sum_even, sum_odd, gap_even, gap_odd = plus(0, 2), plus(1, 3), minus(0, 2), minus(1, 3)
    fours = [
        (sum_even[0] + sum_odd[0], sum_even[1] + sum_odd[1]),
        (gap_even[0] + gap_odd[1], gap_even[1] - gap_odd[0]),
        (sum_even[0] - sum_odd[0], sum_even[1] - sum_odd[1]),
        (gap_even[0] - gap_odd[1], gap_even[1] + gap_odd[0]),
    ]
    sides = []
    for which, (real_part, imag_part) in enumerate(fours):
        near, far = swap_halves(real_part, imag_part)
        far = turn_eighths(far, which, -1)
        sides.append((near + far, near - far))
    return sides


def unfold_classes(sides):
    fours = []
    for which, (first, second) in enumerate(sides):
        near, far = first + second, turn_eighths(first - second, which, 1)
        fours.append(swap_halves(near, far))
    sum_even = [fours[0][i] + fours[2][i] for i in range(2)]
    gap_even = [fours[0][i] - fours[2][i] for i in range(2)]
    sum_odd = [fours[1][i] + fours[3][i] for i in range(2)]
    gap_odd = [fours[1][i] - fours[3][i] for i in range(2)]
    return [
        (sum_even[0] + sum_odd[0], sum_even[1] + sum_odd[1]),
        (gap_even[0] - gap_odd[1], gap_even[1] + gap_odd[0]),
        (sum_even[0] - sum_odd[0], sum_even[1] - sum_odd[1]),
        (gap_even[0] + gap_odd[1], gap_even[1] - gap_odd[0]),
    ]


ORDER = (3, 2, 1)


def couple_kernel(
    lat_count, lay_count, planes, rows,
    layer_any, rate_any, toeplitz_any, hankel_any,
    field_any, contrast_any, lines_any, tables_any, twiddle_any,
    out_ref,
    send_fold, recv_fold, send_in, recv_in, send_out, recv_mid, send_fin, recv_fin,
    field_x, spectrum, mixed, powers,
    field_ref, lines_ref, tables_ref, twiddle_ref,
    layer_ref, rate_ref, toeplitz_ref, hankel_ref, contrast_ref,
    fold_send, fold_recv, in_send, in_recv, out_send, out_recv, fin_send, fin_recv, load_sem, second_sem, third_sem,
):
    inner = 2
    outer = lat_count // inner
    peers = inner * lay_count
    my_lat, my_lay = lax.axis_index("lat"), lax.axis_index("lay")
    my_outer = my_lat // inner
    my_peer = my_lat % inner * lay_count + my_lay
    lines, width_y = field_ref.shape[1:]
    width_x = rows * lat_count
    half_x = width_x // 2
    classes = 2 * outer
    length = width_y // classes
    depth = length // peers
    plane_total = planes * lay_count
    layer_count = rate_ref.shape[0]
    pairs = planes // 2

    def column(way):
        low = (my_outer % 2 + way % 2) % 2
        high = (my_outer // 2 + way // 2) % 2
        return 2 * high + low

    def column_id(way):
        return column(way) * inner + my_lat % inner, my_lay

    def peer(step):
        return (my_peer + step) % peers

    def peer_id(step):
        to = peer(step)
        return my_outer * inner + to // lay_count, to % lay_count

    def over_peers(act):
        def one(step, carry):
            act(step)
            return carry

        lax.fori_loop(1, peers, one, 0)

    chunk = LANES // 2
    cuts = (0, 2 * chunk, lines // 2, lines)
    spans = list(zip(cuts[:-1], cuts[1:]))
    chunks = len(spans)
    loads = [
        pltpu.make_async_copy(
            field_any.at[:, pl.ds(start, stop - start)],
            field_ref.at[:, pl.ds(start, stop - start)],
            load_sem.at[i],
        )
        for i, (start, stop) in enumerate(spans)
    ] + [
        pltpu.make_async_copy(source, target, load_sem.at[chunks + i])
        for i, (source, target) in enumerate(
            [
                (tables_any.at[my_outer], tables_ref),
                (rate_any, rate_ref), (layer_any, layer_ref),
                (toeplitz_any, toeplitz_ref), (hankel_any, hankel_ref),
                (lines_any, lines_ref), (twiddle_any, twiddle_ref), (contrast_any, contrast_ref),
            ]
        )
    ]
    middle = (my_outer + 1) // 2 % 2
    stages = [pltpu.get_barrier_semaphore(), second_sem, third_sem]

    def tell(sem):
        bit = 1
        while bit < peers:
            pl.semaphore_signal(
                sem,
                inc=1,
                device_id=peer_id(bit - 2 * bit * (my_peer // bit % 2) + peers),
                device_id_type=MESH,
            )
            bit = 2 * bit
        pl.semaphore_signal(sem, inc=1, device_id=column_id(1), device_id_type=MESH)

        @pl.when(middle == 1)
        def _():
            pl.semaphore_signal(sem, inc=1, device_id=column_id(3), device_id_type=MESH)

    def hear(sem):
        pl.semaphore_wait(sem, peers.bit_length() + middle)

    tell(stages[0])
    for load in loads[:chunks]:
        load.start()

    def remote(source, target, sems, device):
        return pltpu.make_async_remote_copy(
            src_ref=source,
            dst_ref=target,
            send_sem=sems[0],
            recv_sem=sems[1],
            device_id=device,
            device_id_type=MESH,
        )

    def wait_bytes(view, sem):
        pltpu.make_async_copy(view, view, sem).wait()

    others, ways = pl.ds(0, peers - 1), pl.ds(0, outer - 1)

    def fold_copy(side, way, start, stop):
        where = pl.ds(start, stop - start)
        return remote(
            send_fold.at[column(way), side, where], recv_fold.at[my_outer, side, where],
            (fold_send, fold_recv.at[side, way - 1]), column_id(way),
        )

    def in_copy(origin, side, step):
        return remote(
            send_in.at[peer(step), origin, side], recv_in.at[origin, my_peer, side],
            (in_send, in_recv.at[side]), peer_id(step),
        )

    def out_copy(side, pair, step):
        return remote(
            send_out.at[peer(step), side, pair], recv_mid.at[my_peer, side, pair],
            (out_send, out_recv.at[side, pair]), peer_id(step),
        )

    def fin_copy(side, pair, start, stop, sem, way):
        where = pl.ds(start, stop - start)
        return remote(
            send_fin.at[column(way), side, pair, where],
            recv_fin.at[my_outer, side, pair, where],
            (fin_send, sem), column_id(way),
        )

    def fold(start, stop):
        for first in range(start, stop, chunk):
            where = slice(first, first + chunk)
            parts = [
                [field_ref[comp, where, t * LANES:(t + 1) * LANES] for t in range(outer)]
                for comp in range(2)
            ]
            for which, both in enumerate(fold_classes(*parts)):
                for side in range(2):
                    send_fold[which, side, where] = both[side]

    def send_folded(side, ways, some):
        for start, stop in some:
            for way in ways:
                fold_copy(side, way, start, stop).start()

    whole = [(0, lines)]

    def of_both(inside, outside):
        for flag, sends in ((1, inside), (0, outside)):
            if sends:

                @pl.when(middle == flag)
                def _():
                    for side, way, some in sends:
                        send_folded(side, [way], some)

    def fold_next(i):
        loads[i].wait()
        fold(*spans[i])

    fold_next(0)
    hear(stages[0])
    tell(stages[1])
    of_both([(0, 3, spans[:1])], [(0, 1, spans[:1])])
    for load in loads[chunks:]:
        load.start()
    fold_next(1)
    of_both([(0, 3, spans[1:2])], [])
    hear(stages[1])
    tell(stages[2])
    of_both([(0, 2, spans[:2])], [(0, 2, spans[:2])])
    fold_next(2)
    of_both(
        [(0, 3, spans[2:]), (0, 2, spans[2:]), (0, 1, spans)]
        + [(1, way, whole) for way in (3, 1, 2)],
        [(0, 2, spans[2:])],
    )
    hear(stages[2])
    of_both([], [(0, 3, spans), (0, 1, spans[1:])])

    loads[chunks].wait()

    def transform_y(source, origin, side):
        for start in range(0, lines, 2 * LANES):
            where = slice(start, start + 2 * LANES)
            right = split(source[origin, side, where])
            result = product((tables_ref[side, 0], tables_ref[side, 1]), right, ((1,), (1,)))
            for comp in range(2):
                piece = result[comp * length:(comp + 1) * length]
                send_in[:, origin, side, comp, :, where] = piece.reshape(peers, depth, 2 * LANES)
        over_peers(lambda step: in_copy(origin, side, step).start())
        recv_in[origin, my_peer, side] = send_in[my_peer, origin, side]

    for side in range(2):
        transform_y(send_fold, my_outer, side)
    loads[chunks + 1].wait()

    def signed(index, amount):
        index = jnp.where(index >= amount // 2, index - amount, index)
        return index.astype(jnp.float32) / (amount / 2)

    tile = (depth, width_x)
    place_x = lax.broadcasted_iota(jnp.int32, tile, 1)
    freq_x = signed(2 * (place_x % half_x) + place_x // half_x, width_x)
    for side in range(2):
        place_y = my_peer * depth + lax.broadcasted_iota(jnp.int32, tile, 0)
        freq_y = signed(classes * place_y + my_outer + outer * side, width_y)
        steepness = jnp.sqrt(1.0 + freq_x * freq_x + freq_y * freq_y)

        def one_layer(layer, carry):
            base = jnp.exp(steepness * (-rate_ref[layer] / (2 * plane_total)))

            def one_power(m, value):
                powers[side, layer, m] = value
                return value * base

            lax.fori_loop(0, 2 * plane_total - 1, one_power, jnp.ones(tile, jnp.float32))
            return carry

        lax.fori_loop(0, layer_count, one_layer, 0)

    for load in loads[chunks + 2:]:
        load.wait()

    def gather(side, way):
        wait_bytes(recv_fold.at[column(way), side], fold_recv.at[side, way - 1])
        transform_y(recv_fold, column(way), side)

    early, late = 3 - middle, 2 + middle
    gather(0, early)
    gather(0, 1)
    gather(0, late)

    @pl.when(middle == 0)
    def _():
        for way in (1, 3, 2):
            send_folded(1, [way], whole)

    def load_lines(side):
        def one_lay(lay, carry):
            for pair in range(pairs):
                lanes = slice(pair * LANES, (pair + 1) * LANES)
                for block in range(outer):
                    first = recv_in[block, lay, side, :, :, lanes]
                    second = recv_in[block, lay_count + lay, side, :, :, lanes]
                    even, odd = swap_halves(first, second)
                    place = slice(block * LANES, (block + 1) * LANES)
                    field_x[:, lay * planes + 2 * pair, :, place] = even
                    field_x[:, lay * planes + 2 * pair + 1, :, place] = odd
            return carry

        lax.fori_loop(0, lay_count, one_lay, 0)

    group = min(plane_total, LANES // SUBLANES)

    def transform_x(step, carry):
        some = pl.ds(step * group, group)
        flat = (group * depth, width_x)
        halves = butterfly_in(
            field_x[0, some].reshape(flat), field_x[1, some].reshape(flat), twiddle_ref
        )
        for half, pair in enumerate(halves):
            left = split(jnp.concatenate(pair, 1))
            result = product(left, (lines_ref[0], lines_ref[1]), ((1,), (0,)))
            for comp in range(2):
                piece = result[:, comp * half_x:(comp + 1) * half_x]
                spectrum[comp, some, :, half * half_x:(half + 1) * half_x] = piece.reshape(
                    group, depth, half_x
                )
        return carry

    some_planes = 2 * lay_count

    def invert_x():
        halves = []
        for half in range(2):
            place = slice(half * half_x, (half + 1) * half_x)
            flat = (some_planes * depth, half_x)
            left = split(
                jnp.concatenate(
                    [mixed[comp, :, :, place].reshape(flat) for comp in range(2)], 1
                )
            )
            result = product(left, (lines_ref[2], lines_ref[3]), ((1,), (0,)))
            halves.append((result[:, :half_x], result[:, half_x:]))
        real_part, imag_part = butterfly_out(halves[0], halves[1], twiddle_ref)
        full = (some_planes, depth, width_x)
        factor = 1.0 / (width_x * width_y)
        mixed[0] = (real_part * factor).reshape(full)
        mixed[1] = (imag_part * factor).reshape(full)

    def store_lines(side, pair):
        for lay in range(lay_count):
            for block in range(outer):
                place = slice(block * LANES, (block + 1) * LANES)
                even, odd = mixed[:, 2 * lay, :, place], mixed[:, 2 * lay + 1, :, place]
                first, second = swap_halves(even, odd)
                send_out[lay, side, pair, :, :, place] = first
                send_out[lay_count + lay, side, pair, :, :, place] = second

    def couple(side, pair):
        def one_plane(place, carry):
            plane = place // 2 * planes + 2 * pair + place % 2
            layer = layer_ref[plane]
            real_sum = jnp.zeros(tile, jnp.float32)
            imag_sum = jnp.zeros(tile, jnp.float32)
            for source in range(plane_total):
                offset = plane - source
                direct = powers[side, layer, 2 * jnp.abs(offset)]
                mirror = powers[side, layer, plane + source]
                at = offset + plane_total - 1
                kern_real = (
                    toeplitz_ref[0, layer, at] * direct
                    + hankel_ref[0, layer, plane + source] * mirror
                )
                kern_imag = (
                    toeplitz_ref[1, layer, at] * direct
                    + hankel_ref[1, layer, plane + source] * mirror
                )
                real_src, imag_src = spectrum[0, source], spectrum[1, source]
                real_sum += kern_real * real_src - kern_imag * imag_src
                imag_sum += kern_real * imag_src + kern_imag * real_src
            mixed[0, place] = real_sum
            mixed[1, place] = imag_sum
            return carry

        lax.fori_loop(0, some_planes, one_plane, 0)

    def invert_y(side, pair):
        wait_bytes(recv_mid.at[others, side, pair], out_recv.at[side, pair])
        stack = jnp.concatenate(
            [recv_mid[:, side, pair, comp].reshape(length, outer * LANES) for comp in range(2)], 0
        )
        result = product((tables_ref[side, 2], tables_ref[side, 3]), split(stack), ((1,), (0,)))
        for block in range(outer):
            send_fin[block, side, pair] = result[:, block * LANES:(block + 1) * LANES].T
        recv_fin[my_outer, side, pair] = send_fin[my_outer, side, pair]

    first = 3 - (my_outer + 1) % 2
    second = 5 - first
    holds = my_outer == outer // 2

    def send_final(side, pair, some):
        for way in some:
            fin_copy(side, pair, 0, LANES, fin_recv.at[side, pair], way).start()

    ends = [(0, chunk, fin_recv.at[1, pairs - 1]), (chunk, LANES, fin_recv.at[2, 0])]

    for side in range(2):
        wait_bytes(recv_in.at[:, others, side], in_recv.at[side])
        load_lines(side)
        lax.fori_loop(0, plane_total // group, transform_x, 0)

        def one_pair(pair, carry):
            couple(side, pair)
            invert_x()
            store_lines(side, pair)
            if side == 0:

                @pl.when(pair == pairs - 1)
                def _():
                    gather(1, 2)

            over_peers(lambda step: out_copy(side, pair, step).start())
            recv_mid[my_peer, side, pair] = send_out[my_peer, side, pair]

            if side == 0:

                @pl.when(pair == 1)
                def _():
                    gather(1, 1)

                @pl.when(pair == 2 - middle)
                def _():
                    gather(1, 3)

                @pl.when(pair >= 2)
                def _():
                    invert_y(0, pair - 2)

                    @pl.when(middle == 1)
                    def _():
                        send_final(0, pair - 2, (first, second, 1))

            else:

                @pl.when(pair == 0)
                def _():
                    invert_y(0, pairs - 1)
                    send_final(0, pairs - 1, (first, second, 1))

                @pl.when(pair >= 1)
                def _():
                    invert_y(1, pair - 1)
                    send_final(1, pair - 1, (first, 1))

                    @pl.when(jnp.logical_not(jnp.logical_and(holds, pair >= 2)))
                    def _():
                        send_final(1, pair - 1, (second,))

            return carry

        lax.fori_loop(0, pairs, one_pair, 0)
        if side == 0:
            invert_y(0, pairs - 2)

            @pl.when(middle == 0)
            def _():
                for pair in range(pairs - 2):
                    send_final(0, pair, (first, second, 1))

            send_final(0, pairs - 2, (first, second, 1))
        else:
            invert_y(1, pairs - 1)

            def send_last(way):
                for start, stop, sem in ends:
                    fin_copy(1, pairs - 1, start, stop, sem, way).start()

            send_last(first)

            @pl.when(holds)
            def _():
                for pair in range(1, pairs - 1):
                    send_final(1, pair, (second,))

            send_last(second)
            send_last(1)

    wait_bytes(send_fold.at[ways], fold_send)
    wait_bytes(send_in.at[others], in_send)
    wait_bytes(send_out.at[others], out_send)

    def finish(pair, start, stop):
        inside = pl.ds(start, stop - start)
        where = pl.ds(pair * LANES + start, stop - start)
        sides = [
            (recv_fin[which, 0, pair, inside], recv_fin[which, 1, pair, inside])
            for which in range(outer)
        ]
        for t, (real_part, imag_part) in enumerate(unfold_classes(sides)):
            place = slice(t * LANES, (t + 1) * LANES)
            scale = contrast_ref[where, place]
            out_ref[0, where, place] = real_part * scale
            out_ref[1, where, place] = imag_part * scale

    def finish_pair(pair, carry):
        for side in range(2):
            wait_bytes(recv_fin.at[ways, side, pair], fin_recv.at[side, pair])
        for start in range(0, LANES, chunk):
            finish(pair, start, start + chunk)
        return carry

    lax.fori_loop(0, pairs - 1, finish_pair, 0)
    wait_bytes(recv_fin.at[ways, 0, pairs - 1], fin_recv.at[0, pairs - 1])
    for start, stop, sem in ends:
        wait_bytes(recv_fin.at[ways, 1, pairs - 1, pl.ds(start, stop - start)], sem)
        finish(pairs - 1, start, stop)
    wait_bytes(send_fin.at[ways], fin_send)


def fast_body(wave_field, contrast, layer_of_plane, toeplitz_table, hankel_table, layer_rates):
    _, planes, rows, width_y = wave_field.shape
    lat_count, lay_count = lax.axis_size("lat"), lax.axis_size("lay")
    outer, peers = lat_count // 2, 2 * lay_count
    width_x = rows * lat_count
    depth = width_y // (2 * outer * peers)
    plane_total = planes * lay_count
    layer_count = layer_rates.shape[0]
    lines = planes * rows
    pairs = planes // 2
    line_tables, twiddle = (jnp.asarray(t) for t in split_tables(width_x))
    tables = jnp.asarray(class_tables(width_y, 2 * outer))
    operands = [
        layer_of_plane, layer_rates, toeplitz_table, hankel_table,
        wave_field.reshape(2, lines, width_y), contrast.reshape(lines, width_y), line_tables, tables, twiddle,
    ]
    folded = (outer, 2, lines, LANES)
    final = (outer, 2, pairs, LANES, LANES)
    tile_all = (2, plane_total, depth, width_x)
    dma = pltpu.SemaphoreType.DMA
    space = pl.pallas_call(
        functools.partial(couple_kernel, lat_count, lay_count, planes, rows),
        out_shape=jax.ShapeDtypeStruct((2, lines, width_y), jnp.float32),
        in_specs=[pl.BlockSpec(memory_space=pltpu.HBM)] * len(operands),
        out_specs=pl.BlockSpec(memory_space=pltpu.VMEM),
        scratch_shapes=[
            pltpu.VMEM(folded, jnp.float32),
            pltpu.VMEM(folded, jnp.float32),
            pltpu.VMEM((peers, outer, 2, 2, depth, lines), jnp.float32),
            pltpu.VMEM((outer, peers, 2, 2, depth, lines), jnp.float32),
            pltpu.VMEM((peers, 2, pairs, 2, depth, outer * LANES), jnp.float32),
            pltpu.VMEM((peers, 2, pairs, 2, depth, outer * LANES), jnp.float32),
            pltpu.VMEM(final, jnp.float32),
            pltpu.VMEM(final, jnp.float32),
            pltpu.VMEM(tile_all, jnp.float32),
            pltpu.VMEM(tile_all, jnp.float32),
            pltpu.VMEM((2, 2 * lay_count, depth, width_x), jnp.float32),
            pltpu.VMEM((2, layer_count, 2 * plane_total - 1, depth, width_x), jnp.float32),
            pltpu.VMEM((2, lines, width_y), jnp.float32),
            pltpu.VMEM(line_tables.shape, line_tables.dtype),
            pltpu.VMEM(tables.shape[1:], tables.dtype),
            pltpu.VMEM(twiddle.shape, twiddle.dtype),
            pltpu.SMEM(layer_of_plane.shape, layer_of_plane.dtype),
            pltpu.SMEM(layer_rates.shape, layer_rates.dtype),
            pltpu.SMEM(toeplitz_table.shape, toeplitz_table.dtype),
            pltpu.SMEM(hankel_table.shape, hankel_table.dtype),
            pltpu.VMEM((lines, width_y), jnp.float32),
            dma(()), dma((2, outer - 1)),
            dma(()), dma((2,)),
            dma(()), dma((2, pairs)),
            dma(()), dma((3, pairs)),
            dma((11,)),
            pltpu.SemaphoreType.REGULAR,
            pltpu.SemaphoreType.REGULAR,
        ],
        compiler_params=pltpu.CompilerParams(
            collective_id=0, has_side_effects=True, vmem_limit_bytes=48 * 1024 * 1024
        ),
        name="couple",
    )(*(pltpu.with_memory_space_constraint(value, pltpu.HBM) for value in operands))
    return space.reshape(wave_field.shape)


def body(wave_field, *others):
    _, planes, rows, width_y = wave_field.shape
    lat_count, lay_count = lax.axis_size("lat"), lax.axis_size("lay")
    outer, peers = lat_count // 2, 2 * lay_count
    width_x = rows * lat_count
    fits = (
        lat_count % 2 == 0
        and outer == 4
        and 2 * rows == LANES
        and planes % 2 == 0
        and planes >= 4
        and width_x == width_y
        and width_y == outer * LANES
        and width_y == 2 * outer * peers * SUBLANES
        and (planes * lay_count) % (LANES // SUBLANES) == 0
        and (planes * rows) % (2 * LANES) == 0
    )
    return (fast_body if fits else general_body)(wave_field, *others)


def solution(mesh):
    return jax.shard_map(
        body,
        mesh=mesh,
        in_specs=(P(None, "lay", "lat", None), P("lay", "lat", None), P(), P(), P(), P()),
        out_specs=P(None, "lay", "lat", None),
        check_vma=False,
    )
```

```python
import math

import functools

import jax
import jax.numpy as jnp
import numpy as np
from jax import lax
from jax.experimental import pallas as pl
from jax.experimental.pallas import tpu as pltpu
from jax.sharding import PartitionSpec as P

HIGHEST = lax.Precision.HIGHEST


def signed_of(index, amount):
    return jnp.where(index >= amount // 2, index - amount, index).astype(jnp.float32) / (amount / 2)


def phase_tables(rows, cols, amount, sign):
    index_row = lax.broadcasted_iota(jnp.int32, (rows, cols), 0)
    index_col = lax.broadcasted_iota(jnp.int32, (rows, cols), 1)
    angle = 2.0 * math.pi / amount * (index_row * index_col % amount).astype(jnp.float32)
    return (jnp.cos(angle), sign * jnp.sin(angle))


def complex_apply(real_part, imag_part, cos_table, sin_table, form):
    out_real = jnp.einsum(form, real_part, cos_table, precision=HIGHEST) - jnp.einsum(
        form, imag_part, sin_table, precision=HIGHEST
    )
    out_imag = jnp.einsum(form, real_part, sin_table, precision=HIGHEST) + jnp.einsum(
        form, imag_part, cos_table, precision=HIGHEST
    )
    return (out_real, out_imag)


def fourier_last(real_part, imag_part, sign, factor):
    amount = real_part.shape[-1]
    leading = real_part.shape[:-1]
    first = 1
    for divisor in range(1, math.isqrt(amount) + 1):
        if amount % divisor == 0:
            first = divisor
    second = amount // first
    flat_real = real_part.reshape(-1, second, first)
    flat_imag = imag_part.reshape(-1, second, first)
    cos_second, sin_second = phase_tables(second, second, second, sign)
    section_real, section_imag = complex_apply(
        flat_real, flat_imag, cos_second, sin_second, "pmn,mk->pkn"
    )
    twist_cos, twist_sin = phase_tables(second, first, amount, sign)
    turned_real = section_real * twist_cos - section_imag * twist_sin
    turned_imag = section_real * twist_sin + section_imag * twist_cos
    cos_first, sin_first = phase_tables(first, first, first, sign)
    final_real, final_imag = complex_apply(
        turned_real, turned_imag, cos_first, sin_first, "pkn,nj->pjk"
    )
    final_real = final_real.reshape(leading + (amount,)) * factor
    final_imag = final_imag.reshape(leading + (amount,)) * factor
    return (final_real, final_imag)


def pick_amplitudes(rows, index, width):
    positions = jnp.arange(width, dtype=jnp.int32)
    onehot = (index[:, :, None] == positions[None, None, :]).astype(jnp.float32)
    return jnp.einsum("pan,ain->pai", rows, onehot, precision=HIGHEST)


def general_body(wave_field, contrast, layer_of_plane, toeplitz_table, hankel_table, layer_rates):
    row_count = wave_field.shape[2]
    width_y = wave_field.shape[3]
    lat_count = lax.axis_size("lat")
    lay_count = lax.axis_size("lay")
    width_x = row_count * lat_count
    ky_band = width_y // lat_count
    table_width = toeplitz_table.shape[-1]
    plane_total = (table_width + 1) // 2
    layer_count = layer_rates.shape[0]
    spec_real, spec_imag = fourier_last(wave_field[0], wave_field[1], -1.0, 1.0)
    along_y = jnp.stack([spec_real, spec_imag], 2)
    freq_x = signed_of(jnp.arange(width_x, dtype=jnp.int32), width_x)
    ky_first = lax.axis_index("lat") * ky_band
    layer_ids = jnp.arange(layer_count, dtype=jnp.int32)

    def couple(z_out, z_in, source, ky_rows):
        onehot = (layer_of_plane[z_out][:, None] == layer_ids[None, :]).astype(jnp.float32)
        rate_out = jnp.dot(onehot, layer_rates, precision=HIGHEST)
        rows_toeplitz = jnp.einsum("al,pln->pan", onehot, toeplitz_table, precision=HIGHEST)
        rows_hankel = jnp.einsum("al,pln->pan", onehot, hankel_table, precision=HIGHEST)
        offset = z_out[:, None] - z_in[None, :]
        plane_sum = z_out[:, None] + z_in[None, :]
        amp_toeplitz = pick_amplitudes(rows_toeplitz, offset + plane_total - 1, table_width)
        amp_hankel = pick_amplitudes(rows_hankel, plane_sum, table_width)
        freq_y = signed_of(ky_rows, width_y)
        steepness = jnp.sqrt(1.0 + freq_y[:, None] ** 2 + freq_x[None, :] ** 2)
        scaled = rate_out[:, None, None, None] * steepness[None, None] / plane_total
        decay_toeplitz = jnp.exp(-scaled * jnp.abs(offset).astype(jnp.float32)[:, :, None, None])
        decay_hankel = jnp.exp(-scaled * (0.5 * plane_sum.astype(jnp.float32))[:, :, None, None])
        kern_real = (
            amp_toeplitz[0][:, :, None, None] * decay_toeplitz
            + amp_hankel[0][:, :, None, None] * decay_hankel
        )
        kern_imag = (
            amp_toeplitz[1][:, :, None, None] * decay_toeplitz
            + amp_hankel[1][:, :, None, None] * decay_hankel
        )
        real_src = source[None, :, 0]
        imag_src = source[None, :, 1]
        out_real = jnp.sum(kern_real * real_src - kern_imag * imag_src, axis=1)
        out_imag = jnp.sum(kern_real * imag_src + kern_imag * real_src, axis=1)
        return jnp.stack([out_real, out_imag], 1)

    narrow = ky_band // lay_count
    narrow_rows = ky_first + lax.axis_index("lay") * narrow + jnp.arange(narrow, dtype=jnp.int32)
    lines_in = lax.all_to_all(along_y, "lat", split_axis=3, concat_axis=1, tiled=True)
    line_real = jnp.transpose(lines_in[:, :, 0], (0, 2, 1))
    line_imag = jnp.transpose(lines_in[:, :, 1], (0, 2, 1))
    out_real, out_imag = fourier_last(line_real, line_imag, -1.0, 1.0)
    spectrum = jnp.stack([out_real, out_imag], 1)
    gathered = lax.all_to_all(spectrum, "lay", split_axis=2, concat_axis=0, tiled=True)
    all_planes = gathered.shape[0]
    every_plane = jnp.arange(all_planes, dtype=jnp.int32)
    block_size = math.gcd(all_planes, 8)

    def one_block(which):
        z_out = which * block_size + jnp.arange(block_size, dtype=jnp.int32)
        return couple(z_out, every_plane, gathered, narrow_rows)

    stacked = lax.map(one_block, jnp.arange(all_planes // block_size, dtype=jnp.int32))
    coupled = stacked.reshape(all_planes, 2, narrow_rows.shape[0], width_x)
    mixed = lax.all_to_all(coupled, "lay", split_axis=0, concat_axis=2, tiled=True)
    out_real, out_imag = fourier_last(mixed[:, 0], mixed[:, 1], 1.0, 1.0 / width_x)
    spatial_x = jnp.transpose(jnp.stack([out_real, out_imag], 1), (0, 3, 1, 2))
    lines = lax.all_to_all(spatial_x, "lat", split_axis=1, concat_axis=3, tiled=True)
    space_real, space_imag = fourier_last(lines[:, :, 0], lines[:, :, 1], 1.0, 1.0 / width_y)
    return jnp.stack([space_real, space_imag], 0) * contrast[None]


LANES = 128
SUBLANES = 8
MESH = pl.DeviceIdType.MESH


def split_pair(table):
    table = table.astype(np.float32)
    high = table.astype(jnp.bfloat16)
    return high, (table - high.astype(np.float32)).astype(jnp.bfloat16)


def split_tables(amount):
    half = amount // 2
    index = np.arange(half)
    angle = 2.0 * np.pi / half * (index[:, None] * index[None, :] % half)
    cos_part, sin_part = np.cos(angle), np.sin(angle)
    right = np.block([[cos_part, -sin_part], [sin_part, cos_part]])
    high, low = split_pair(right)
    turn = 2.0 * np.pi / amount * index
    twiddle = np.stack([np.cos(turn), np.sin(turn)]).astype(np.float32)
    return np.stack([high, low, high.T, low.T]), twiddle


def class_tables(amount, classes):
    length = amount // classes
    index = np.arange(length)
    every = []
    for which in range(classes):
        turns = (which + classes * index[:, None]) * index[None, :] % amount
        angle = 2.0 * np.pi / amount * turns
        cos_part, sin_part = np.cos(angle), np.sin(angle)
        forward = np.block([[cos_part, sin_part], [-sin_part, cos_part]])
        every.append(np.stack([*split_pair(forward), *split_pair(forward.T)]))
    every = np.stack(every).reshape(2, classes // 2, 4, 2 * length, 2 * length)
    return np.ascontiguousarray(every.swapaxes(0, 1))


def split(value):
    high = value.astype(jnp.bfloat16)
    return high, (value - high.astype(jnp.float32)).astype(jnp.bfloat16)


def product(left, right, contract):
    dot = functools.partial(
        lax.dot_general,
        dimension_numbers=(contract, ((), ())),
        preferred_element_type=jnp.float32,
    )
    return dot(left[0], right[0]) + (dot(left[1], right[0]) + dot(left[0], right[1]))


def swap_halves(first, second):
    low = lax.broadcasted_iota(jnp.int32, first.shape, first.ndim - 1) < LANES // 2
    one = jnp.where(low, first, pltpu.roll(second, LANES // 2, first.ndim - 1))
    two = jnp.where(low, pltpu.roll(first, LANES // 2, first.ndim - 1), second)
    return one, two


def butterfly_in(real_part, imag_part, twiddle):
    half = real_part.shape[-1] // 2
    cos_row, sin_row = twiddle[0:1, :], twiddle[1:2, :]
    even = (real_part[:, :half] + real_part[:, half:], imag_part[:, :half] + imag_part[:, half:])
    real_gap = real_part[:, :half] - real_part[:, half:]
    imag_gap = imag_part[:, :half] - imag_part[:, half:]
    odd = (
        real_gap * cos_row + imag_gap * sin_row,
        imag_gap * cos_row - real_gap * sin_row,
    )
    return even, odd


def butterfly_out(even, odd, twiddle):
    cos_row, sin_row = twiddle[0:1, :], twiddle[1:2, :]
    real_turn = odd[0] * cos_row - odd[1] * sin_row
    imag_turn = odd[0] * sin_row + odd[1] * cos_row
    real_part = jnp.concatenate([even[0] + real_turn, even[0] - real_turn], 1)
    imag_part = jnp.concatenate([even[1] + imag_turn, even[1] - imag_turn], 1)
    return real_part, imag_part


ROOT_HALF = math.sqrt(0.5)


def turn_eighths(pair, which, sign):
    if which == 0:
        return pair
    low = lax.broadcasted_iota(jnp.int32, pair.shape, pair.ndim - 1) < LANES // 2
    other = pltpu.roll(pair, LANES // 2, pair.ndim - 1)
    crossed = jnp.where(low, other, -other) if sign < 0 else jnp.where(low, -other, other)
    if which == 2:
        return crossed
    return ROOT_HALF * (crossed + pair) if which == 1 else ROOT_HALF * (crossed - pair)


def fold_classes(real_parts, imag_parts):
    def plus(first, second):
        return tuple(parts[first] + parts[second] for parts in (real_parts, imag_parts))

    def minus(first, second):
        return tuple(parts[first] - parts[second] for parts in (real_parts, imag_parts))

    sum_even, sum_odd, gap_even, gap_odd = plus(0, 2), plus(1, 3), minus(0, 2), minus(1, 3)
    fours = [
        (sum_even[0] + sum_odd[0], sum_even[1] + sum_odd[1]),
        (gap_even[0] + gap_odd[1], gap_even[1] - gap_odd[0]),
        (sum_even[0] - sum_odd[0], sum_even[1] - sum_odd[1]),
        (gap_even[0] - gap_odd[1], gap_even[1] + gap_odd[0]),
    ]
    sides = []
    for which, (real_part, imag_part) in enumerate(fours):
        near, far = swap_halves(real_part, imag_part)
        far = turn_eighths(far, which, -1)
        sides.append((near + far, near - far))
    return sides


def unfold_classes(sides):
    fours = []
    for which, (first, second) in enumerate(sides):
        near, far = first + second, turn_eighths(first - second, which, 1)
        fours.append(swap_halves(near, far))
    sum_even = [fours[0][i] + fours[2][i] for i in range(2)]
    gap_even = [fours[0][i] - fours[2][i] for i in range(2)]
    sum_odd = [fours[1][i] + fours[3][i] for i in range(2)]
    gap_odd = [fours[1][i] - fours[3][i] for i in range(2)]
    return [
        (sum_even[0] + sum_odd[0], sum_even[1] + sum_odd[1]),
        (gap_even[0] - gap_odd[1], gap_even[1] + gap_odd[0]),
        (sum_even[0] - sum_odd[0], sum_even[1] - sum_odd[1]),
        (gap_even[0] + gap_odd[1], gap_even[1] - gap_odd[0]),
    ]


ORDER = (3, 2, 1)


def couple_kernel(
    lat_count, lay_count, planes, rows,
    layer_any, rate_any, toeplitz_any, hankel_any,
    field_any, contrast_any, lines_any, tables_any, twiddle_any,
    out_ref,
    send_fold, recv_fold, send_in, recv_in, send_out, recv_mid, send_fin, recv_fin,
    field_x, spectrum, mixed, powers,
    field_ref, lines_ref, tables_ref, twiddle_ref,
    layer_ref, rate_ref, toeplitz_ref, hankel_ref, contrast_ref,
    fold_send, fold_recv, in_send, in_recv, out_send, out_recv, fin_send, fin_recv, load_sem, second_sem, third_sem,
):
    inner = 2
    outer = lat_count // inner
    peers = inner * lay_count
    my_lat, my_lay = lax.axis_index("lat"), lax.axis_index("lay")
    my_outer = my_lat // inner
    my_peer = my_lat % inner * lay_count + my_lay
    lines, width_y = field_ref.shape[1:]
    width_x = rows * lat_count
    half_x = width_x // 2
    classes = 2 * outer
    length = width_y // classes
    depth = length // peers
    plane_total = planes * lay_count
    layer_count = rate_ref.shape[0]
    pairs = planes // 2

    def column(way):
        low = (my_outer % 2 + way % 2) % 2
        high = (my_outer // 2 + way // 2) % 2
        return 2 * high + low

    def column_id(way):
        return column(way) * inner + my_lat % inner, my_lay

    def peer(step):
        return (my_peer + step) % peers

    def peer_id(step):
        to = peer(step)
        return my_outer * inner + to // lay_count, to % lay_count

    def over_peers(act):
        def one(step, carry):
            act(step)
            return carry

        lax.fori_loop(1, peers, one, 0)

    chunk = LANES // 2
    cuts = (0, 2 * chunk, lines // 2, lines)
    spans = list(zip(cuts[:-1], cuts[1:]))
    chunks = len(spans)
    loads = [
        pltpu.make_async_copy(
            field_any.at[:, pl.ds(start, stop - start)],
            field_ref.at[:, pl.ds(start, stop - start)],
            load_sem.at[i],
        )
        for i, (start, stop) in enumerate(spans)
    ] + [
        pltpu.make_async_copy(source, target, load_sem.at[chunks + i])
        for i, (source, target) in enumerate(
            [
                (tables_any.at[my_outer], tables_ref),
                (rate_any, rate_ref), (layer_any, layer_ref),
                (toeplitz_any, toeplitz_ref), (hankel_any, hankel_ref),
                (lines_any, lines_ref), (twiddle_any, twiddle_ref), (contrast_any, contrast_ref),
            ]
        )
    ]
    middle = (my_outer + 1) // 2 % 2
    stages = [pltpu.get_barrier_semaphore(), second_sem, third_sem]

    def tell(sem):
        bit = 1
        while bit < peers:
            pl.semaphore_signal(
                sem,
                inc=1,
                device_id=peer_id(bit - 2 * bit * (my_peer // bit % 2) + peers),
                device_id_type=MESH,
            )
            bit = 2 * bit
        pl.semaphore_signal(sem, inc=1, device_id=column_id(1), device_id_type=MESH)

        @pl.when(middle == 1)
        def _():
            pl.semaphore_signal(sem, inc=1, device_id=column_id(3), device_id_type=MESH)

    def hear(sem):
        pl.semaphore_wait(sem, peers.bit_length() + middle)

    tell(stages[0])
    for load in loads[:chunks]:
        load.start()

    def remote(source, target, sems, device):
        return pltpu.make_async_remote_copy(
            src_ref=source,
            dst_ref=target,
            send_sem=sems[0],
            recv_sem=sems[1],
            device_id=device,
            device_id_type=MESH,
        )

    def wait_bytes(view, sem):
        pltpu.make_async_copy(view, view, sem).wait()

    others, ways = pl.ds(0, peers - 1), pl.ds(0, outer - 1)

    def fold_copy(side, way, start, stop):
        where = pl.ds(start, stop - start)
        return remote(
            send_fold.at[column(way), side, where], recv_fold.at[my_outer, side, where],
            (fold_send, fold_recv.at[side, way - 1]), column_id(way),
        )

    def in_copy(origin, side, step):
        return remote(
            send_in.at[peer(step), origin, side], recv_in.at[origin, my_peer, side],
            (in_send, in_recv.at[side]), peer_id(step),
        )

    def out_copy(side, pair, step):
        return remote(
            send_out.at[peer(step), side, pair], recv_mid.at[my_peer, side, pair],
            (out_send, out_recv.at[side, pair]), peer_id(step),
        )

    def fin_copy(side, pair, start, stop, sem, way):
        where = pl.ds(start, stop - start)
        return remote(
            send_fin.at[column(way), side, pair, where],
            recv_fin.at[my_outer, side, pair, where],
            (fin_send, sem), column_id(way),
        )

    def fold(start, stop):
        for first in range(start, stop, chunk):
            where = slice(first, first + chunk)
            parts = [
                [field_ref[comp, where, t * LANES:(t + 1) * LANES] for t in range(outer)]
                for comp in range(2)
            ]
            for which, both in enumerate(fold_classes(*parts)):
                for side in range(2):
                    send_fold[which, side, where] = both[side]

    def send_folded(side, ways, some):
        for start, stop in some:
            for way in ways:
                fold_copy(side, way, start, stop).start()

    whole = [(0, lines)]

    def of_both(inside, outside):
        for flag, sends in ((1, inside), (0, outside)):
            if sends:

                @pl.when(middle == flag)
                def _():
                    for side, way, some in sends:
                        send_folded(side, [way], some)

    def fold_next(i):
        loads[i].wait()
        fold(*spans[i])

    fold_next(0)
    hear(stages[0])
    tell(stages[1])
    of_both([(0, 3, spans[:1])], [(0, 1, spans[:1])])
    for load in loads[chunks:]:
        load.start()
    fold_next(1)
    of_both([(0, 3, spans[1:2])], [])
    hear(stages[1])
    tell(stages[2])
    of_both([(0, 2, spans[:2])], [(0, 2, spans[:2])])
    fold_next(2)
    of_both(
        [(0, 3, spans[2:]), (0, 2, spans[2:]), (0, 1, spans)]
        + [(1, way, whole) for way in (3, 1, 2)],
        [(0, 2, spans[2:])],
    )
    hear(stages[2])
    of_both([], [(0, 3, spans), (0, 1, spans[1:])])

    loads[chunks].wait()

    def transform_y(source, origin, side):
        for start in range(0, lines, 2 * LANES):
            where = slice(start, start + 2 * LANES)
            right = split(source[origin, side, where])
            result = product((tables_ref[side, 0], tables_ref[side, 1]), right, ((1,), (1,)))
            for comp in range(2):
                piece = result[comp * length:(comp + 1) * length]
                send_in[:, origin, side, comp, :, where] = piece.reshape(peers, depth, 2 * LANES)
        over_peers(lambda step: in_copy(origin, side, step).start())
        recv_in[origin, my_peer, side] = send_in[my_peer, origin, side]

    for side in range(2):
        transform_y(send_fold, my_outer, side)
    loads[chunks + 1].wait()

    def signed(index, amount):
        index = jnp.where(index >= amount // 2, index - amount, index)
        return index.astype(jnp.float32) / (amount / 2)

    tile = (depth, width_x)
    place_x = lax.broadcasted_iota(jnp.int32, tile, 1)
    freq_x = signed(2 * (place_x % half_x) + place_x // half_x, width_x)
    for side in range(2):
        place_y = my_peer * depth + lax.broadcasted_iota(jnp.int32, tile, 0)
        freq_y = signed(classes * place_y + my_outer + outer * side, width_y)
        steepness = jnp.sqrt(1.0 + freq_x * freq_x + freq_y * freq_y)

        def one_layer(layer, carry):
            base = jnp.exp(steepness * (-rate_ref[layer] / (2 * plane_total)))

            def one_power(m, value):
                powers[side, layer, m] = value
                return value * base

            lax.fori_loop(0, 2 * plane_total - 1, one_power, jnp.ones(tile, jnp.float32))
            return carry

        lax.fori_loop(0, layer_count, one_layer, 0)

    for load in loads[chunks + 2:]:
        load.wait()

    def gather(side, way):
        wait_bytes(recv_fold.at[column(way), side], fold_recv.at[side, way - 1])
        transform_y(recv_fold, column(way), side)

    early, late = 3 - middle, 2 + middle
    gather(0, early)
    gather(0, 1)
    gather(0, late)

    @pl.when(middle == 0)
    def _():
        for way in (1, 3, 2):
            send_folded(1, [way], whole)

    def load_lines(side):
        def one_lay(lay, carry):
            for pair in range(pairs):
                lanes = slice(pair * LANES, (pair + 1) * LANES)
                for block in range(outer):
                    first = recv_in[block, lay, side, :, :, lanes]
                    second = recv_in[block, lay_count + lay, side, :, :, lanes]
                    even, odd = swap_halves(first, second)
                    place = slice(block * LANES, (block + 1) * LANES)
                    field_x[:, lay * planes + 2 * pair, :, place] = even
                    field_x[:, lay * planes + 2 * pair + 1, :, place] = odd
            return carry

        lax.fori_loop(0, lay_count, one_lay, 0)

    group = min(plane_total, LANES // SUBLANES)

    def transform_x(step, carry):
        some = pl.ds(step * group, group)
        flat = (group * depth, width_x)
        halves = butterfly_in(
            field_x[0, some].reshape(flat), field_x[1, some].reshape(flat), twiddle_ref
        )
        for half, pair in enumerate(halves):
            left = split(jnp.concatenate(pair, 1))
            result = product(left, (lines_ref[0], lines_ref[1]), ((1,), (0,)))
            for comp in range(2):
                piece = result[:, comp * half_x:(comp + 1) * half_x]
                spectrum[comp, some, :, half * half_x:(half + 1) * half_x] = piece.reshape(
                    group, depth, half_x
                )
        return carry

    some_planes = 2 * lay_count

    def invert_x():
        halves = []
        for half in range(2):
            place = slice(half * half_x, (half + 1) * half_x)
            flat = (some_planes * depth, half_x)
            left = split(
                jnp.concatenate(
                    [mixed[comp, :, :, place].reshape(flat) for comp in range(2)], 1
                )
            )
            result = product(left, (lines_ref[2], lines_ref[3]), ((1,), (0,)))
            halves.append((result[:, :half_x], result[:, half_x:]))
        real_part, imag_part = butterfly_out(halves[0], halves[1], twiddle_ref)
        full = (some_planes, depth, width_x)
        factor = 1.0 / (width_x * width_y)
        mixed[0] = (real_part * factor).reshape(full)
        mixed[1] = (imag_part * factor).reshape(full)

    def store_lines(side, pair):
        for lay in range(lay_count):
            for block in range(outer):
                place = slice(block * LANES, (block + 1) * LANES)
                even, odd = mixed[:, 2 * lay, :, place], mixed[:, 2 * lay + 1, :, place]
                first, second = swap_halves(even, odd)
                send_out[lay, side, pair, :, :, place] = first
                send_out[lay_count + lay, side, pair, :, :, place] = second

    def couple(side, pair):
        def one_plane(place, carry):
            plane = place // 2 * planes + 2 * pair + place % 2
            layer = layer_ref[plane]
            real_sum = jnp.zeros(tile, jnp.float32)
            imag_sum = jnp.zeros(tile, jnp.float32)
            for source in range(plane_total):
                offset = plane - source
                direct = powers[side, layer, 2 * jnp.abs(offset)]
                mirror = powers[side, layer, plane + source]
                at = offset + plane_total - 1
                kern_real = (
                    toeplitz_ref[0, layer, at] * direct
                    + hankel_ref[0, layer, plane + source] * mirror
                )
                kern_imag = (
                    toeplitz_ref[1, layer, at] * direct
                    + hankel_ref[1, layer, plane + source] * mirror
                )
                real_src, imag_src = spectrum[0, source], spectrum[1, source]
                real_sum += kern_real * real_src - kern_imag * imag_src
                imag_sum += kern_real * imag_src + kern_imag * real_src
            mixed[0, place] = real_sum
            mixed[1, place] = imag_sum
            return carry

        lax.fori_loop(0, some_planes, one_plane, 0)

    def invert_y(side, pair):
        wait_bytes(recv_mid.at[others, side, pair], out_recv.at[side, pair])
        stack = jnp.concatenate(
            [recv_mid[:, side, pair, comp].reshape(length, outer * LANES) for comp in range(2)], 0
        )
        result = product((tables_ref[side, 2], tables_ref[side, 3]), split(stack), ((1,), (0,)))
        for block in range(outer):
            send_fin[block, side, pair] = result[:, block * LANES:(block + 1) * LANES].T
        recv_fin[my_outer, side, pair] = send_fin[my_outer, side, pair]

    first = 3 - (my_outer + 1) % 2
    second = 5 - first
    holds = my_outer == outer // 2

    def send_final(side, pair, some):
        for way in some:
            fin_copy(side, pair, 0, LANES, fin_recv.at[side, pair], way).start()

    ends = [(0, chunk, fin_recv.at[1, pairs - 1]), (chunk, LANES, fin_recv.at[2, 0])]

    for side in range(2):
        wait_bytes(recv_in.at[:, others, side], in_recv.at[side])
        load_lines(side)
        lax.fori_loop(0, plane_total // group, transform_x, 0)

        def one_pair(pair, carry):
            couple(side, pair)
            invert_x()
            store_lines(side, pair)
            if side == 0:

                @pl.when(pair == pairs - 1)
                def _():
                    gather(1, 2)

                    @pl.when(middle == 0)
                    def _():
                        send_final(0, 0, (first, second, 1))

            over_peers(lambda step: out_copy(side, pair, step).start())
            recv_mid[my_peer, side, pair] = send_out[my_peer, side, pair]

            if side == 0:

                @pl.when(pair == 1)
                def _():
                    gather(1, 1)

                @pl.when(pair == 2 - middle)
                def _():
                    gather(1, 3)

                @pl.when(pair >= 2)
                def _():
                    invert_y(0, pair - 2)

                    @pl.when(jnp.logical_or(middle == 1, pair == pairs - 1))
                    def _():
                        send_final(0, pair - 2, (first, second, 1))

            else:

                @pl.when(pair == 0)
                def _():
                    invert_y(0, pairs - 1)
                    send_final(0, pairs - 1, (first, second, 1))

                @pl.when(pair >= 1)
                def _():
                    invert_y(1, pair - 1)
                    send_final(1, pair - 1, (first, 1))

                    @pl.when(jnp.logical_not(jnp.logical_and(holds, pair >= 2)))
                    def _():
                        send_final(1, pair - 1, (second,))

            return carry

        lax.fori_loop(0, pairs, one_pair, 0)
        if side == 0:
            invert_y(0, pairs - 2)

            send_final(0, pairs - 2, (first, second, 1))
        else:
            invert_y(1, pairs - 1)

            def send_last(way):
                for start, stop, sem in ends:
                    fin_copy(1, pairs - 1, start, stop, sem, way).start()

            send_last(first)

            @pl.when(holds)
            def _():
                for pair in range(1, pairs - 1):
                    send_final(1, pair, (second,))

            send_last(second)
            send_last(1)

    wait_bytes(send_fold.at[ways], fold_send)
    wait_bytes(send_in.at[others], in_send)
    wait_bytes(send_out.at[others], out_send)

    def finish(pair, start, stop):
        inside = pl.ds(start, stop - start)
        where = pl.ds(pair * LANES + start, stop - start)
        sides = [
            (recv_fin[which, 0, pair, inside], recv_fin[which, 1, pair, inside])
            for which in range(outer)
        ]
        for t, (real_part, imag_part) in enumerate(unfold_classes(sides)):
            place = slice(t * LANES, (t + 1) * LANES)
            scale = contrast_ref[where, place]
            out_ref[0, where, place] = real_part * scale
            out_ref[1, where, place] = imag_part * scale

    def finish_pair(pair, carry):
        for side in range(2):
            wait_bytes(recv_fin.at[ways, side, pair], fin_recv.at[side, pair])
        for start in range(0, LANES, chunk):
            finish(pair, start, start + chunk)
        return carry

    lax.fori_loop(0, pairs - 1, finish_pair, 0)
    wait_bytes(recv_fin.at[ways, 0, pairs - 1], fin_recv.at[0, pairs - 1])
    for start, stop, sem in ends:
        wait_bytes(recv_fin.at[ways, 1, pairs - 1, pl.ds(start, stop - start)], sem)
        finish(pairs - 1, start, stop)
    wait_bytes(send_fin.at[ways], fin_send)


def fast_body(wave_field, contrast, layer_of_plane, toeplitz_table, hankel_table, layer_rates):
    _, planes, rows, width_y = wave_field.shape
    lat_count, lay_count = lax.axis_size("lat"), lax.axis_size("lay")
    outer, peers = lat_count // 2, 2 * lay_count
    width_x = rows * lat_count
    depth = width_y // (2 * outer * peers)
    plane_total = planes * lay_count
    layer_count = layer_rates.shape[0]
    lines = planes * rows
    pairs = planes // 2
    line_tables, twiddle = (jnp.asarray(t) for t in split_tables(width_x))
    tables = jnp.asarray(class_tables(width_y, 2 * outer))
    operands = [
        layer_of_plane, layer_rates, toeplitz_table, hankel_table,
        wave_field.reshape(2, lines, width_y), contrast.reshape(lines, width_y), line_tables, tables, twiddle,
    ]
    folded = (outer, 2, lines, LANES)
    final = (outer, 2, pairs, LANES, LANES)
    tile_all = (2, plane_total, depth, width_x)
    dma = pltpu.SemaphoreType.DMA
    space = pl.pallas_call(
        functools.partial(couple_kernel, lat_count, lay_count, planes, rows),
        out_shape=jax.ShapeDtypeStruct((2, lines, width_y), jnp.float32),
        in_specs=[pl.BlockSpec(memory_space=pltpu.HBM)] * len(operands),
        out_specs=pl.BlockSpec(memory_space=pltpu.VMEM),
        scratch_shapes=[
            pltpu.VMEM(folded, jnp.float32),
            pltpu.VMEM(folded, jnp.float32),
            pltpu.VMEM((peers, outer, 2, 2, depth, lines), jnp.float32),
            pltpu.VMEM((outer, peers, 2, 2, depth, lines), jnp.float32),
            pltpu.VMEM((peers, 2, pairs, 2, depth, outer * LANES), jnp.float32),
            pltpu.VMEM((peers, 2, pairs, 2, depth, outer * LANES), jnp.float32),
            pltpu.VMEM(final, jnp.float32),
            pltpu.VMEM(final, jnp.float32),
            pltpu.VMEM(tile_all, jnp.float32),
            pltpu.VMEM(tile_all, jnp.float32),
            pltpu.VMEM((2, 2 * lay_count, depth, width_x), jnp.float32),
            pltpu.VMEM((2, layer_count, 2 * plane_total - 1, depth, width_x), jnp.float32),
            pltpu.VMEM((2, lines, width_y), jnp.float32),
            pltpu.VMEM(line_tables.shape, line_tables.dtype),
            pltpu.VMEM(tables.shape[1:], tables.dtype),
            pltpu.VMEM(twiddle.shape, twiddle.dtype),
            pltpu.SMEM(layer_of_plane.shape, layer_of_plane.dtype),
            pltpu.SMEM(layer_rates.shape, layer_rates.dtype),
            pltpu.SMEM(toeplitz_table.shape, toeplitz_table.dtype),
            pltpu.SMEM(hankel_table.shape, hankel_table.dtype),
            pltpu.VMEM((lines, width_y), jnp.float32),
            dma(()), dma((2, outer - 1)),
            dma(()), dma((2,)),
            dma(()), dma((2, pairs)),
            dma(()), dma((3, pairs)),
            dma((11,)),
            pltpu.SemaphoreType.REGULAR,
            pltpu.SemaphoreType.REGULAR,
        ],
        compiler_params=pltpu.CompilerParams(
            collective_id=0, has_side_effects=True, vmem_limit_bytes=48 * 1024 * 1024
        ),
        name="couple",
    )(*(pltpu.with_memory_space_constraint(value, pltpu.HBM) for value in operands))
    return space.reshape(wave_field.shape)


def body(wave_field, *others):
    _, planes, rows, width_y = wave_field.shape
    lat_count, lay_count = lax.axis_size("lat"), lax.axis_size("lay")
    outer, peers = lat_count // 2, 2 * lay_count
    width_x = rows * lat_count
    fits = (
        lat_count % 2 == 0
        and outer == 4
        and 2 * rows == LANES
        and planes == 2 * outer
        and width_x == width_y
        and width_y == outer * LANES
        and width_y == 2 * outer * peers * SUBLANES
        and (planes * lay_count) % (LANES // SUBLANES) == 0
        and (planes * rows) % (2 * LANES) == 0
    )
    return (fast_body if fits else general_body)(wave_field, *others)


def solution(mesh):
    return jax.shard_map(
        body,
        mesh=mesh,
        in_specs=(P(None, "lay", "lat", None), P("lay", "lat", None), P(), P(), P(), P()),
        out_specs=P(None, "lay", "lat", None),
        check_vma=False,
    )
```
